32 devices in a mesh: groups: 2 (over y), strip: 4 (over z), panel: 2 (over x), sub: 2 (over core).
Axes of the slice: x: 2, y: 2, z: 4, core: 2. Of those that a mesh axis runs over, the one named last changes fastest.
Arguments:
- start_block: float32 [64, 128, 256], P('groups', ('strip', 'sub'), 'panel'), parts along dimension 0, may hold values from -120 to 120, as said below
- edge_weights: float32 [16, 128, 256], P('groups', ('strip', 'sub'), 'panel'), parts along dimension 0, may hold values from 0 to 1, as said below
- mass: float32 [256, 256], P(('groups', 'strip', 'sub'), 'panel'), parts along dimension 0, may hold values from 0.5 to 2
- locked: bfloat16 [2048, 128, 256], P(('groups', 'panel'), ('strip', 'sub')), parts along dimension 0, may hold values from -4 to 4
Outputs:
- ortho: float32 [64, 128, 256], P('groups', ('strip', 'sub'), 'panel'), parts along dimension 0
- coupling: float32 [2048, 32], P(('groups', 'panel')), parts along dimension 0
- r_factor: float32 [64, 32], P('groups'), parts along dimension 0
The draws below stay inside these ranges and needn't reach their ends.
There are 2 independent parts, one for each index of `groups`. The reference program is written for one: setup_inputs(seed, part) draws one part's arguments, and reference() takes and returns one part's arrays. A program takes and returns all parts, laid end to end along the dimension named above; each array names one. Nothing has to cross between parts.
Inputs may be any that keep to these rules, and one draw needn't show every extreme that they name: `start_block`: the sum of an entry's square over the block's vertices is positive for every vector. edge_weights[k + 4] at vertex (i, j) equals edge_weights[k] at vertex (i, j) - o_k for k = 0..3, and is zero where that vertex lies outside the grid; edge_weights[0..3] are positive everywhere.
All inputs are finite; a program needn't handle non-finite values.
Results may differ from the reference program's by a relative error of at most 0.003.
Values may be sent and summed in bfloat16 or wider, within the bound.
No kernel may reach another device: no remote copies, remote signals or barrier semaphores. Data moves between devices by JAX's collectives and lax.ppermute only.
A program may use at most 64 MiB of HBM per device.

```python
import math
import jax
import jax.numpy as jnp
from jax import lax

BLOCK = 32
BASIS = 1024
DEGREE = 6
CUT_LOW = 2
CUT_HIGH = 32
NX = 128
NY = 256


OFFSETS_DRAW = ((0, 1), (1, 0), (1, 1), (1, -1))


def draw_start_block(key, part):
    key_values, key_vertex, key_vector = jax.random.split(key, 3)
    grid_rows = jnp.arange(NX, dtype=jnp.float32)
    row_ramp = 1.0 + 2.0 * grid_rows / max(NX - 1, 1)
    vertex_scale = jnp.exp(jax.random.uniform(key_vertex, (NX, NY), dtype=jnp.float32) * math.log(10.0))
    vector_scale = jnp.exp(jax.random.uniform(key_vector, (BLOCK, 1, 1), dtype=jnp.float32) * math.log(10.0))
    values = jax.random.truncated_normal(key_values, -4.0, 4.0, (BLOCK, NX, NY), dtype=jnp.float32)
    return 0.1 * values * vector_scale * vertex_scale * row_ramp[None, :, None]


def draw_edge_weights(key, part):
    base_weights = jax.random.uniform(key, (4, NX, NY), dtype=jnp.float32, minval=0.25, maxval=1.0)
    padded = jnp.pad(base_weights, ((0, 0), (1, 1), (1, 1)))
    shifted = []
    for direction in range(4):
        step_row, step_col = OFFSETS_DRAW[direction]
        shifted.append(padded[direction, 1 - step_row:1 - step_row + NX, 1 - step_col:1 - step_col + NY])
    return jnp.concatenate([base_weights, jnp.stack(shifted)], axis=0)


def level_of(stream_key, dims, pieces, low, top_value):
    loudness = 1.0
    for axis_at, shards_of in pieces:
        heights = jax.random.uniform(jax.random.fold_in(jax.random.fold_in(stream_key, 6), axis_at), (shards_of,), jnp.float32, low / len(pieces), top_value / len(pieces))
        loudness = loudness * jnp.repeat(jnp.exp(heights), dims[axis_at] // shards_of).reshape((-1,) + (1,) * (len(dims) - 1 - axis_at))
    return loudness


def centred(stream_key, dims, width, limit, shards=(), kind=jnp.bfloat16):
    level = level_of(stream_key, dims, shards, -0.22, 0.18) if shards else 1.0
    result = jax.random.normal(stream_key, dims, jnp.float32) * width * level
    return jnp.minimum(jnp.maximum(result, -limit), limit).astype(kind)


def setup_inputs(seed: int = 0, part: int = 0) -> dict:
    arg_keys = jax.random.split(jax.random.key(seed), 5)
    own_keys = jax.random.split(jax.random.fold_in(arg_keys[4], part), 5)
    start_block = draw_start_block(jax.random.fold_in(jax.random.fold_in(arg_keys[4], part), 71), part)
    edge_weights = draw_edge_weights(jax.random.fold_in(jax.random.fold_in(arg_keys[4], part), 71), part)
    mass = jnp.clip(jnp.exp(math.log(2.0) - 1.3862944 * jax.random.uniform(own_keys[2], (NX, NY), jnp.float32) ** level_of(own_keys[2], (NX, NY), ((0, 8), (1, 2)), -0.2, 0.2)), 0.5, 2.0)
    locked = centred(own_keys[3], (BASIS, NX, NY), 1.0, 4.0, ((0, 2), (1, 8)))
    return {"start_block": start_block, "edge_weights": edge_weights, "mass": mass, "locked": locked}


OFFSETS = ((0, 1), (1, 0), (1, 1), (1, -1), (0, -1), (-1, 0), (-1, -1), (-1, 1))

def apply_operator(vectors, edge_weights, scaling):
    scaled = scaling * vectors
    padded = jnp.pad(scaled, ((0, 0), (1, 1), (1, 1)))
    height = scaled.shape[1]
    across = scaled.shape[2]
    summed = jnp.zeros_like(scaled)
    for direction in range(8):
        step_row, step_col = OFFSETS[direction]
        beside = padded[:, 1 + step_row:1 + step_row + height, 1 + step_col:1 + step_col + across]
        summed = summed + edge_weights[direction] * (scaled - beside)
    return scaling * summed

def chebyshev(start_block, edge_weights, scaling):
    centre = 0.5 * (CUT_HIGH + CUT_LOW)
    spread = 0.5 * (CUT_HIGH - CUT_LOW)
    previous = start_block
    current = (apply_operator(start_block, edge_weights, scaling) - centre * start_block) / spread
    for order_now in range(1, DEGREE):
        following = 2.0 * (apply_operator(current, edge_weights, scaling) - centre * current) / spread - previous
        previous, current = (current, following)
    return current

def reference(start_block, edge_weights, mass, locked):
    scaling = 1.0 / jnp.sqrt(mass)
    filtered = chebyshev(start_block, edge_weights, scaling)
    block_count = filtered.shape[0]
    flat_block = filtered.reshape(block_count, -1)
    vertices = flat_block.shape[1]
    identity_matrix = jnp.eye(block_count, dtype=jnp.float32)
    gram_matrix = jnp.dot(flat_block.astype(jnp.float32), flat_block.T.astype(jnp.float32), precision=lax.Precision.HIGHEST, preferred_element_type=jnp.float32) / vertices + 1e-06 * identity_matrix
    lower_factor = jnp.linalg.cholesky(gram_matrix)
    ortho_flat = lax.linalg.triangular_solve(lower_factor, flat_block, left_side=True, lower=True)
    ortho = ortho_flat.reshape(filtered.shape)
    ortho_half = ortho_flat.astype(jnp.bfloat16)
    locked_flat = locked.reshape(locked.shape[0], -1)
    coupling = jnp.dot(locked_flat.astype(jnp.float32), ortho_half.T.astype(jnp.float32), preferred_element_type=jnp.float32) / jnp.sqrt(jnp.float32(vertices))
    return (ortho, coupling, jnp.transpose(lower_factor))
```

```python
import math

import jax
import jax.numpy as jnp
from jax import lax
from jax.experimental import pallas as pl
from jax.experimental.pallas import tpu as pltpu
from jax.sharding import PartitionSpec as P

DEGREE = 6
CUT_LOW = 2
CUT_HIGH = 32
CENTRE = 0.5 * (CUT_HIGH + CUT_LOW)
SPREAD = 0.5 * (CUT_HIGH - CUT_LOW)
HALO = DEGREE
GRID_ROWS = ("strip", "sub")


def pack_kernel(block_ref, weights_ref, mass_ref, out_ref):
    count, height, _ = block_ref.shape
    out_ref[:, 0:count, :] = pltpu.einshape("brc->rbc", block_ref[...])
    side = jnp.concatenate([weights_ref[0:4], mass_ref[...][None], mass_ref[...][None],
                            mass_ref[...][None], mass_ref[...][None]], axis=0)
    out_ref[:, count : count + 8, :] = pltpu.einshape("brc->rbc", side)


def pack(start_block, edge_weights, mass):
    count, height, width = start_block.shape
    return pl.pallas_call(
        pack_kernel,
        out_shape=jax.ShapeDtypeStruct((height, count + 8, width), jnp.float32),
        name="pack",
    )(start_block, edge_weights, mass)


def filter_kernel(panel_ref, *refs, panels, height, count, width):
    bodies = refs[0:panels]
    above = refs[panels : 2 * panels]
    below = refs[2 * panels : 3 * panels]
    locked_ref, payload_ref, own_ref, y_even, y_odd, coef, split = refs[3 * panels :]
    total = panels * width
    rows = height + 2 * HALO
    panel = panel_ref[0]

    def source(row):
        if row < HALO:
            return [a[row] for a in above]
        if row < HALO + height:
            return [b[row - HALO] for b in bodies]
        return [b[row - HALO - height] for b in below]

    lane = lax.broadcasted_iota(jnp.int32, (1, total), 1)
    column = lax.rem(lane + panel * width, total)
    not_last = (column != total - 1).astype(jnp.float32)
    not_first = (column != 0).astype(jnp.float32)

    factor = 2.0 / SPREAD

    def left(x):
        return pltpu.roll(x, total - 1, 1)

    def right(x):
        return pltpu.roll(x, 1, 1)

    weights = []
    scale = []
    for row in range(rows):
        parts = source(row)
        full = jnp.concatenate(parts, axis=1)
        y_even[row] = full[0:count]
        side = full[count : count + 8]
        mass = side[4:5]
        inside = mass > 0.0
        scale.append(jnp.where(inside, 1.0 / jnp.sqrt(jnp.where(inside, mass, 1.0)), 0.0))
        weights.append([side[d : d + 1] for d in range(4)])
    edges = []
    for row in range(rows - 1):
        s0 = scale[row]
        s1 = scale[row + 1]
        w = weights[row]
        e0 = -factor * (w[0] * (s0 * left(s0))) * not_last
        e1 = -factor * (w[1] * (s0 * s1))
        e2 = -factor * (w[2] * (s0 * left(s1))) * not_last
        e3 = -factor * (w[3] * (s0 * right(s1))) * not_first
        edges.append((e0, e1, e2, e3))
    for row in range(1, rows - 1):
        w = weights[row]
        v = weights[row - 1]
        total_weight = (
            ((w[0] + w[1]) + (w[2] + w[3]))
            + (right(w[0] * not_last) + v[1])
            + (right(v[2] * not_last) + left(v[3] * not_first))
        )
        diagonal = factor * (scale[row] * scale[row] * total_weight - CENTRE)
        e0, e1, e2, e3 = edges[row]
        u0, u1, u2, u3 = edges[row - 1]
        planes = (diagonal, e1, u1, right(e0), right(e2), u3, e0, left(e3), u2)
        for index, plane in enumerate(planes):
            coef[row, index] = jnp.broadcast_to(plane, (8, total))

    def step(order, source_ref, target_ref):
        first = order
        last = rows - order

        def body(row, carry):
            c = [jnp.concatenate([coef[row, i]] * (count // 8), axis=0) for i in range(9)]
            ym = source_ref[row - 1]
            y0 = source_ref[row]
            yp = source_ref[row + 1]
            out = c[0] * y0 + (c[1] * yp + c[2] * ym)
            to_left = c[3] * y0 + (c[4] * yp + c[5] * ym)
            to_right = c[6] * y0 + (c[7] * yp + c[8] * ym)
            out = out + (left(to_left) + right(to_right))
            if order == 1:
                out = 0.5 * out
            else:
                out = out - target_ref[row]
            target_ref[row] = out
            return carry

        lax.fori_loop(first, last, body, 0, unroll=2)

    buffers = (y_even, y_odd)
    for order in range(1, DEGREE + 1):
        step(order, buffers[(order - 1) % 2], buffers[order % 2])
    result = buffers[DEGREE % 2]

    for row in range(height):
        full = result[row + HALO]
        own_ref[row] = full[:, 0:width]
        high = full.astype(jnp.bfloat16)
        rest = full - high.astype(jnp.float32)
        middle = rest.astype(jnp.bfloat16)
        low = (rest - middle.astype(jnp.float32)).astype(jnp.bfloat16)
        stacked = jnp.concatenate([high, middle, low], axis=0)
        for t in range(panels):
            at = row * total + lax.rem(panel + t, panels) * width
            split[:, pl.ds(pl.multiple_of(at, width), width)] = stacked[:, t * width : (t + 1) * width]

    dims = (((1,), (1,)), ((), ()))
    pieces = split[...]
    products = lax.dot_general(pieces, locked_ref[...], dims, preferred_element_type=jnp.float32)
    basis = locked_ref.shape[0]
    payload_ref[:, 0:basis] = (
        products[0:count] + products[count : 2 * count] + products[2 * count : 3 * count]
    )
    gram = lax.dot_general(pieces, pieces, dims, preferred_element_type=jnp.float32)
    gram = gram[0:count] + gram[count : 2 * count] + gram[2 * count : 3 * count]
    gram = gram[:, 0:count] + gram[:, count : 2 * count] + gram[:, 2 * count : 3 * count]
    payload_ref[:, basis : basis + 128] = jnp.concatenate(
        [gram, jnp.zeros((count, 128 - count), jnp.float32)], axis=1
    )


def filter_call(panel, bodies, above, below, locked_flat):
    panels = len(bodies)
    height, planes, width = bodies[0].shape
    count = planes - 8
    basis = locked_flat.shape[0]
    total = panels * width
    rows = height + 2 * HALO
    vmem = pl.BlockSpec(memory_space=pltpu.VMEM)
    return pl.pallas_call(
        lambda *refs: filter_kernel(*refs, panels=panels, height=height, count=count, width=width),
        in_specs=[pl.BlockSpec(memory_space=pltpu.SMEM)] + [vmem] * (3 * panels + 1),
        out_specs=[vmem, vmem],
        out_shape=[
            jax.ShapeDtypeStruct((count, basis + 128), jnp.float32),
            jax.ShapeDtypeStruct((height, count, width), jnp.float32),
        ],
        scratch_shapes=[
            pltpu.VMEM((rows, count, total), jnp.float32),
            pltpu.VMEM((rows, count, total), jnp.float32),
            pltpu.VMEM((rows, 9, 8, total), jnp.float32),
            pltpu.VMEM((3 * count, height * total), jnp.bfloat16),
        ],
        compiler_params=pltpu.CompilerParams(vmem_limit_bytes=48 << 20),
        name="filter",
    )(panel, *bodies, *above, *below, locked_flat)


def finish_kernel(mine_ref, other_ref, own_ref, ortho_ref, coupling_ref, factor_ref, *, vertices):
    height, count, width = own_ref.shape
    basis = coupling_ref.shape[0]
    cut = slice(basis, basis + 128)
    gram = mine_ref[:, cut] + other_ref[:, cut]
    row = lax.broadcasted_iota(jnp.int32, (count, 128), 0)
    col = lax.broadcasted_iota(jnp.int32, (count, 128), 1)
    gram = gram * (1.0 / vertices) + jnp.where(row == col, 1e-06, 0.0)
    work = gram + jnp.where(row + count == col, 1.0, 0.0)
    for j in range(count - 1):
        pivot_row = work[j : j + 1, :]
        multiplier = work[:, j : j + 1] / work[j : j + 1, j : j + 1]
        work = work - jnp.where(row > j, multiplier * pivot_row, 0.0)
    pivots = jnp.sum(jnp.where(row == col, work, 0.0), axis=1, keepdims=True)
    work = work * (1.0 / jnp.sqrt(pivots))
    upper = jnp.where(row <= col, work, 0.0)
    factor_ref[...] = upper[:, 0:count]
    inverse = work[:, count : 2 * count]
    highest = lax.Precision.HIGHEST
    coefficients = mine_ref[:, 0:basis] + other_ref[:, 0:basis]
    coupling = lax.dot_general(
        coefficients, inverse * (1.0 / math.sqrt(vertices)), (((0,), (1,)), ((), ())),
        precision=highest, preferred_element_type=jnp.float32,
    )
    coupling_ref[...] = coupling
    flat = jnp.concatenate([own_ref[r] for r in range(height)], axis=1)
    ortho = jnp.dot(inverse, flat, precision=highest, preferred_element_type=jnp.float32)
    stacked = jnp.stack([ortho[:, r * width : (r + 1) * width] for r in range(height)], axis=0)
    ortho_ref[...] = pltpu.einshape("rbc->brc", stacked)


def finish(mine, other, own, basis, vertices):
    height, count, width = own.shape
    return pl.pallas_call(
        lambda *refs: finish_kernel(*refs, vertices=float(vertices)),
        out_shape=[
            jax.ShapeDtypeStruct((count, height, width), jnp.float32),
            jax.ShapeDtypeStruct((basis, count), jnp.float32),
            jax.ShapeDtypeStruct((count, count), jnp.float32),
        ],
        name="finish",
    )(mine, other, own)


def swap(array, axis, distance):
    size = lax.axis_size(axis)
    return lax.ppermute(array, axis, [(i, i ^ distance) for i in range(size)])


def on_device(start_block, edge_weights, mass, locked):
    panels = lax.axis_size("panel")
    lines = lax.axis_size(GRID_ROWS)
    strips = lax.axis_size("strip")
    subs = lax.axis_size("sub")
    count, height, width = start_block.shape
    vertices = height * width * lines * panels
    locked_flat = locked.reshape(locked.shape[0], -1)

    down_moves = [(i, i + 1) for i in range(lines - 1)]
    up_moves = [(i + 1, i) for i in range(lines - 1)]
    body = pack(start_block, edge_weights, mass)
    bodies = [body]
    for shift in range(1, panels):
        bodies.append(
            lax.ppermute(body, "panel", [((i + shift) % panels, i) for i in range(panels)])
        )
    above = [lax.ppermute(b[height - HALO :], GRID_ROWS, down_moves) for b in bodies]
    below = [lax.ppermute(b[:HALO], GRID_ROWS, up_moves) for b in bodies]
    panel = lax.axis_index("panel").astype(jnp.int32).reshape(1)
    payload, own = filter_call(panel, bodies, above, below, locked_flat)

    rounds = [("sub", 1 << k) for k in range(subs.bit_length() - 1)]
    rounds += [("strip", 1 << k) for k in range(strips.bit_length() - 1)]
    other = jnp.zeros_like(payload)
    for index, (axis, distance) in enumerate(rounds):
        if index > 0:
            payload = payload + other
        other = swap(payload, axis, distance)
    ortho, coupling, factor = finish(payload, other, own, locked.shape[0], vertices)
    return (ortho, coupling, factor)


def solution(mesh):
    return jax.shard_map(
        on_device,
        mesh=mesh,
        in_specs=(
            P("groups", ("strip", "sub"), "panel"),
            P("groups", ("strip", "sub"), "panel"),
            P(("groups", "strip", "sub"), "panel"),
            P(("groups", "panel"), ("strip", "sub"), None),
        ),
        out_specs=(
            P("groups", ("strip", "sub"), "panel"),
            P(("groups", "panel"), None),
            P("groups", None),
        ),
        check_vma=False,
    )
```

```python
import math

import jax
import jax.numpy as jnp
from jax import lax
from jax.experimental import pallas as pl
from jax.experimental.pallas import tpu as pltpu
from jax.sharding import PartitionSpec as P

DEGREE = 6
CUT_LOW = 2
CUT_HIGH = 32
CENTRE = 0.5 * (CUT_HIGH + CUT_LOW)
SPREAD = 0.5 * (CUT_HIGH - CUT_LOW)
HALO = DEGREE
GRID_ROWS = ("strip", "sub")
SIDE = 8

VMEM = pl.BlockSpec(memory_space=pltpu.VMEM)
SMEM = pl.BlockSpec(memory_space=pltpu.SMEM)
HBM = pl.BlockSpec(memory_space=pltpu.HBM)


def pack_kernel(
    sub_ref, block_hbm, weights_hbm, mass_hbm, body_ref, near_ref, far_ref,
    block_ref, weights_ref, mass_ref, sems,
):
    copies = [
        pltpu.make_async_copy(block_hbm, block_ref, sems.at[0]),
        pltpu.make_async_copy(weights_hbm.at[0:4], weights_ref, sems.at[1]),
        pltpu.make_async_copy(mass_hbm, mass_ref, sems.at[2]),
    ]
    for copy in copies:
        copy.start()
    for copy in copies:
        copy.wait()
    count, height, width = block_ref.shape
    body_ref[:, 0:count, :] = pltpu.einshape("brc->rbc", block_ref[...])
    mass = mass_ref[...][None]
    side = jnp.concatenate([weights_ref[...], mass, mass, mass, mass], axis=0)
    body_ref[:, count : count + SIDE, :] = pltpu.einshape("brc->rbc", side)
    sub = sub_ref[0]
    near_ref[...] = body_ref[pl.ds((1 - sub) * (height - HALO), HALO)]
    far_ref[...] = body_ref[pl.ds(sub * (height - HALO), HALO)]


def pack(sub, start_block, edge_weights, mass):
    count, height, width = start_block.shape
    halo = jax.ShapeDtypeStruct((HALO, count + SIDE, width), jnp.float32)
    return pl.pallas_call(
        pack_kernel,
        in_specs=[SMEM, HBM, HBM, HBM],
        out_specs=[VMEM, VMEM, VMEM],
        out_shape=[jax.ShapeDtypeStruct((height, count + SIDE, width), jnp.float32), halo, halo],
        scratch_shapes=[
            pltpu.VMEM((count, height, width), jnp.float32),
            pltpu.VMEM((4, height, width), jnp.float32),
            pltpu.VMEM((height, width), jnp.float32),
            pltpu.SemaphoreType.DMA((3,)),
        ],
        compiler_params=pltpu.CompilerParams(vmem_limit_bytes=8 << 20),
        name="pack",
    )(sub, start_block, edge_weights, mass)


def filter_kernel(panel_ref, sub_ref, *refs, panels, height, count, width):
    bodies = refs[0:panels]
    nears = refs[panels : 2 * panels]
    fars = refs[2 * panels : 3 * panels]
    locked_hbm, keep_ref, send_ref, own_ref, y_even, y_odd, split, locked_ref, sem = refs[3 * panels :]
    locked_copy = pltpu.make_async_copy(locked_hbm, locked_ref, sem)
    locked_copy.start()
    total = panels * width
    rows = height + 2 * HALO
    panel = panel_ref[0]
    first_sub = sub_ref[0] == 0

    def source(row):
        if HALO <= row < HALO + height:
            parts = [b[row - HALO] for b in bodies]
        elif row < HALO:
            parts = [jnp.where(first_sub, f[row], n[row]) for n, f in zip(nears, fars)]
        else:
            at = row - HALO - height
            parts = [jnp.where(first_sub, n[at], f[at]) for n, f in zip(nears, fars)]
        return jnp.concatenate(parts, axis=1)

    lane = lax.broadcasted_iota(jnp.int32, (1, total), 1)
    column = lax.rem(lane + panel * width, total)
    not_last = (column != total - 1).astype(jnp.float32)
    not_first = (column != 0).astype(jnp.float32)

    factor = 2.0 / SPREAD

    def left(x):
        return pltpu.roll(x, total - 1, 1)

    def right(x):
        return pltpu.roll(x, 1, 1)

    weights = []
    scale = []
    for row in range(rows):
        full = source(row)
        y_even[row] = full[0:count]
        side = full[count : count + SIDE]
        mass = side[4:5]
        inside = mass > 0.0
        scale.append(jnp.where(inside, 1.0 / jnp.sqrt(jnp.where(inside, mass, 1.0)), 0.0))
        weights.append([side[d : d + 1] for d in range(4)])
    edges = []
    for row in range(rows - 1):
        s0 = scale[row]
        s1 = scale[row + 1]
        w = weights[row]
        e0 = -factor * (w[0] * (s0 * left(s0))) * not_last
        e1 = -factor * (w[1] * (s0 * s1))
        e2 = -factor * (w[2] * (s0 * left(s1))) * not_last
        e3 = -factor * (w[3] * (s0 * right(s1))) * not_first
        edges.append((e0, e1, e2, e3))
    coefficients = [None]
    for row in range(1, rows - 1):
        w = weights[row]
        v = weights[row - 1]
        total_weight = (
            ((w[0] + w[1]) + (w[2] + w[3]))
            + (right(w[0] * not_last) + v[1])
            + (right(v[2] * not_last) + left(v[3] * not_first))
        )
        diagonal = factor * (scale[row] * scale[row] * total_weight - CENTRE)
        e0, e1, e2, e3 = edges[row]
        u0, u1, u2, u3 = edges[row - 1]
        coefficients.append((diagonal, e1, u1, right(e0), right(e2), u3, e0, left(e3), u2))

    buffers = (y_even, y_odd)
    for order in range(1, DEGREE + 1):
        source_ref = buffers[(order - 1) % 2]
        target_ref = buffers[order % 2]
        for row in range(order, rows - order):
            c = coefficients[row]
            ym = source_ref[row - 1]
            y0 = source_ref[row]
            yp = source_ref[row + 1]
            out = c[0] * y0 + (c[1] * yp + c[2] * ym)
            to_left = c[3] * y0 + (c[4] * yp + c[5] * ym)
            to_right = c[6] * y0 + (c[7] * yp + c[8] * ym)
            out = out + (left(to_left) + right(to_right))
            if order == 1:
                out = 0.5 * out
            else:
                out = out - target_ref[row]
            target_ref[row] = out
    result = buffers[DEGREE % 2]

    for row in range(height):
        full = result[row + HALO]
        own_ref[row] = full[:, 0:width]
        high = full.astype(jnp.bfloat16)
        rest = full - high.astype(jnp.float32)
        middle = rest.astype(jnp.bfloat16)
        low = (rest - middle.astype(jnp.float32)).astype(jnp.bfloat16)
        stacked = jnp.concatenate([high, middle, low], axis=0)
        for t in range(panels):
            at = row * total + lax.rem(panel + t, panels) * width
            split[:, pl.ds(pl.multiple_of(at, width), width)] = stacked[:, t * width : (t + 1) * width]

    dims = (((1,), (1,)), ((), ()))
    pieces = split[...]
    gram = lax.dot_general(pieces, pieces, dims, preferred_element_type=jnp.float32)
    gram = gram[0:count] + gram[count : 2 * count] + gram[2 * count : 3 * count]
    gram = gram[:, 0:count] + gram[:, count : 2 * count] + gram[:, 2 * count : 3 * count]
    locked_copy.wait()
    products = lax.dot_general(pieces, locked_ref[...], dims, preferred_element_type=jnp.float32)
    products = products[0:count] + products[count : 2 * count] + products[2 * count : 3 * count]
    half = products.shape[1] // 2
    lower = products[:, 0:half]
    upper = products[:, half:]
    keep_ref[0:count] = jnp.where(first_sub, lower, upper)
    send_ref[0:count] = jnp.where(first_sub, upper, lower)
    dense = fold(gram, half)
    keep_ref[count : count + 8] = dense
    send_ref[count : count + 8] = dense


def fold(gram, width):
    count = gram.shape[0]
    parts = [gram[r : r + 8] for r in range(0, count, 8)]
    spare = width - count * len(parts)
    if spare > 0:
        parts.append(jnp.zeros((8, spare), jnp.float32))
    return jnp.concatenate(parts, axis=1)


def filter_call(panel, sub, bodies, nears, fars, locked_flat):
    panels = len(bodies)
    height, planes, width = bodies[0].shape
    count = planes - SIDE
    basis = locked_flat.shape[0]
    total = panels * width
    rows = height + 2 * HALO
    payload = jax.ShapeDtypeStruct((count + 8, basis // 2), jnp.float32)
    return pl.pallas_call(
        lambda *refs: filter_kernel(*refs, panels=panels, height=height, count=count, width=width),
        in_specs=[SMEM, SMEM] + [VMEM] * (3 * panels) + [HBM],
        out_specs=[VMEM] * 3,
        out_shape=[payload, payload, jax.ShapeDtypeStruct((height, count, width), jnp.float32)],
        scratch_shapes=[
            pltpu.VMEM((rows, count, total), jnp.float32),
            pltpu.VMEM((rows, count, total), jnp.float32),
            pltpu.VMEM((3 * count, height * total), jnp.bfloat16),
            pltpu.VMEM(locked_flat.shape, jnp.bfloat16),
            pltpu.SemaphoreType.DMA(()),
        ],
        compiler_params=pltpu.CompilerParams(vmem_limit_bytes=20 << 20),
        name="filter",
    )(panel, sub, *bodies, *nears, *fars, locked_flat)


def factor_kernel(gram_ref, own_ref, ortho_ref, factor_ref, inverse_ref, *, vertices):
    height, count, width = own_ref.shape
    dense = gram_ref[...]
    groups = [dense[:, g * count : (g + 1) * count] for g in range(count // 8)]
    gram = jnp.concatenate(groups, axis=0)
    gram = jnp.concatenate([gram, jnp.zeros((count, 128 - count), jnp.float32)], axis=1)
    row = lax.broadcasted_iota(jnp.int32, (count, 128), 0)
    col = lax.broadcasted_iota(jnp.int32, (count, 128), 1)
    gram = gram * (1.0 / vertices) + jnp.where(row == col, 1e-06, 0.0)
    work = gram + jnp.where(row + count == col, 1.0, 0.0)
    for j in range(count - 1):
        pivot_row = work[j : j + 1, :]
        multiplier = work[:, j : j + 1] / work[j : j + 1, j : j + 1]
        work = work - jnp.where(row > j, multiplier * pivot_row, 0.0)
    pivots = jnp.sum(jnp.where(row == col, work, 0.0), axis=1, keepdims=True)
    work = work * (1.0 / jnp.sqrt(pivots))
    factor_ref[...] = jnp.where(row <= col, work, 0.0)[:, 0:count]
    inverse = work[:, count : 2 * count]
    inverse_ref[...] = inverse
    flat = jnp.concatenate([own_ref[r] for r in range(height)], axis=1)
    ortho = jnp.dot(
        inverse, flat, precision=lax.Precision.HIGHEST, preferred_element_type=jnp.float32
    )
    stacked = jnp.stack([ortho[:, r * width : (r + 1) * width] for r in range(height)], axis=0)
    ortho_ref[...] = pltpu.einshape("rbc->brc", stacked)


def factorize(gram, own, vertices):
    height, count, width = own.shape
    square = jax.ShapeDtypeStruct((count, count), jnp.float32)
    return pl.pallas_call(
        lambda *refs: factor_kernel(*refs, vertices=float(vertices)),
        in_specs=[VMEM, VMEM],
        out_specs=[VMEM, VMEM, VMEM],
        out_shape=[jax.ShapeDtypeStruct((count, height, width), jnp.float32), square, square],
        compiler_params=pltpu.CompilerParams(vmem_limit_bytes=8 << 20),
        name="factor",
    )(gram, own)


def coupling_kernel(sub_ref, inverse_ref, mine_ref, other_ref, out_ref, *, vertices):
    first_sub = sub_ref[0] == 0
    half = mine_ref.shape[1]
    mine = mine_ref[...]
    other = other_ref[...]
    inverse = inverse_ref[...] * (1.0 / math.sqrt(vertices))
    for index, part in enumerate(
        (jnp.where(first_sub, mine, other), jnp.where(first_sub, other, mine))
    ):
        out_ref[:, index * half : (index + 1) * half] = jnp.dot(
            inverse, part, precision=lax.Precision.HIGHEST, preferred_element_type=jnp.float32
        )


def couple(sub, inverse, mine, other, vertices):
    count, half = mine.shape
    return pl.pallas_call(
        lambda *refs: coupling_kernel(*refs, vertices=float(vertices)),
        in_specs=[SMEM, VMEM, VMEM, VMEM],
        out_specs=VMEM,
        out_shape=jax.ShapeDtypeStruct((count, 2 * half), jnp.float32),
        compiler_params=pltpu.CompilerParams(vmem_limit_bytes=8 << 20),
        name="couple",
    )(sub, inverse, mine, other)


def swap(array, axis, distance):
    size = lax.axis_size(axis)
    return lax.ppermute(array, axis, [(i, i ^ distance) for i in range(size)])


def strip_sum(part):
    strips = lax.axis_size("strip")
    distance = 1
    while distance * 4 < strips or distance * 2 == strips:
        part = part + swap(part, "strip", distance)
        distance *= 2
    if distance * 4 == strips:
        one = swap(part, "strip", distance)
        two = swap(part, "strip", 2 * distance)
        three = swap(part, "strip", 3 * distance)
        part = (part + one) + (two + three)
    return part


def on_device(start_block, edge_weights, mass, locked):
    panels = lax.axis_size("panel")
    lines = lax.axis_size(GRID_ROWS)
    count, height, width = start_block.shape
    vertices = height * width * lines * panels
    panel = lax.axis_index("panel").astype(jnp.int32).reshape(1)
    sub = lax.axis_index("sub").astype(jnp.int32).reshape(1)

    body, near, far = pack(sub, start_block, edge_weights, mass)
    bodies = [body]
    for shift in range(1, panels):
        bodies.append(
            lax.ppermute(body, "panel", [((i + shift) % panels, i) for i in range(panels)])
        )
    locked_flat = locked.reshape(locked.shape[0], -1)
    across = []
    for line in range(1, lines - 1, 2):
        across += [(line, line + 1), (line + 1, line)]

    def exchange(near, far):
        return swap(near, "sub", 1), lax.ppermute(far, GRID_ROWS, across)

    halos = [exchange(near, far)]
    rest, locked_flat = lax.optimization_barrier((bodies[1:], locked_flat))
    for other in rest:
        edge = height - HALO
        halos.append(
            exchange(
                lax.dynamic_slice_in_dim(other, (1 - sub[0]) * edge, HALO, 0),
                lax.dynamic_slice_in_dim(other, sub[0] * edge, HALO, 0),
            )
        )
    keep, send, own = filter_call(
        panel, sub, [body] + list(rest), [h[0] for h in halos], [h[1] for h in halos], locked_flat
    )
    part = strip_sum(keep + swap(send, "sub", 1))
    mine = part[:count]
    other = swap(mine, "sub", 1)
    ortho, factor, inverse = factorize(part[count:, : count * count // 8], own, vertices)
    coupling = couple(sub, inverse, mine, other, vertices)
    return (ortho, jnp.transpose(coupling), factor)


def solution(mesh):
    return jax.shard_map(
        on_device,
        mesh=mesh,
        in_specs=(
            P("groups", ("strip", "sub"), "panel"),
            P("groups", ("strip", "sub"), "panel"),
            P(("groups", "strip", "sub"), "panel"),
            P(("groups", "panel"), ("strip", "sub"), None),
        ),
        out_specs=(
            P("groups", ("strip", "sub"), "panel"),
            P(("groups", "panel"), None),
            P("groups", None),
        ),
        check_vma=False,
    )
```

```python
import math

import jax
import jax.numpy as jnp
from jax import lax
from jax.experimental import pallas as pl
from jax.experimental.pallas import tpu as pltpu
from jax.sharding import PartitionSpec as P

DEGREE = 6
CUT_LOW = 2
CUT_HIGH = 32
CENTRE = 0.5 * (CUT_HIGH + CUT_LOW)
SPREAD = 0.5 * (CUT_HIGH - CUT_LOW)
HALO = DEGREE
GRID_ROWS = ("strip", "sub")
SIDE = 8

VMEM = pl.BlockSpec(memory_space=pltpu.VMEM)
SMEM = pl.BlockSpec(memory_space=pltpu.SMEM)
HBM = pl.BlockSpec(memory_space=pltpu.HBM)


def pack_kernel(
    sub_ref, block_hbm, weights_hbm, mass_hbm, body_ref, near_ref, far_ref,
    block_ref, weights_ref, mass_ref, sems,
):
    copies = [
        pltpu.make_async_copy(block_hbm, block_ref, sems.at[0]),
        pltpu.make_async_copy(weights_hbm.at[0:4], weights_ref, sems.at[1]),
        pltpu.make_async_copy(mass_hbm, mass_ref, sems.at[2]),
    ]
    for copy in copies:
        copy.start()
    for copy in copies:
        copy.wait()
    count, height, width = block_ref.shape
    body_ref[:, 0:count, :] = pltpu.einshape("brc->rbc", block_ref[...])
    mass = mass_ref[...][None]
    side = jnp.concatenate([weights_ref[...], mass, mass, mass, mass], axis=0)
    body_ref[:, count : count + SIDE, :] = pltpu.einshape("brc->rbc", side)
    sub = sub_ref[0]
    near_ref[...] = body_ref[pl.ds((1 - sub) * (height - HALO), HALO)]
    far_ref[...] = body_ref[pl.ds(sub * (height - HALO), HALO)]


def pack(sub, start_block, edge_weights, mass):
    count, height, width = start_block.shape
    halo = jax.ShapeDtypeStruct((HALO, count + SIDE, width), jnp.float32)
    return pl.pallas_call(
        pack_kernel,
        in_specs=[SMEM, HBM, HBM, HBM],
        out_specs=[VMEM, VMEM, VMEM],
        out_shape=[jax.ShapeDtypeStruct((height, count + SIDE, width), jnp.float32), halo, halo],
        scratch_shapes=[
            pltpu.VMEM((count, height, width), jnp.float32),
            pltpu.VMEM((4, height, width), jnp.float32),
            pltpu.VMEM((height, width), jnp.float32),
            pltpu.SemaphoreType.DMA((3,)),
        ],
        compiler_params=pltpu.CompilerParams(vmem_limit_bytes=8 << 20),
        name="pack",
    )(sub, *[in_hbm(x) for x in (start_block, edge_weights, mass)])


def in_hbm(array):
    return pltpu.with_memory_space_constraint(array, pltpu.HBM)


def relayout_kernel(locked_hbm, out_hbm, token_ref, chunks_ref, flat_ref, read_sems, write_sems):
    chunks, size, height, width = chunks_ref.shape
    reads = [
        pltpu.make_async_copy(locked_hbm.at[pl.ds(i * size, size)], chunks_ref.at[i], read_sems.at[i])
        for i in range(chunks)
    ]
    writes = [
        pltpu.make_async_copy(flat_ref.at[i], out_hbm.at[pl.ds(i * size, size)], write_sems.at[i])
        for i in range(chunks)
    ]
    for read in reads:
        read.start()
    token_ref[...] = jnp.zeros_like(token_ref)
    for i in range(chunks):
        reads[i].wait()
        rows = pltpu.einshape("krc->rkc", chunks_ref[i])
        for r in range(height):
            flat_ref[i, :, r * width : (r + 1) * width] = rows[r]
        writes[i].start()
    for write in writes:
        write.wait()


def relayout(locked):
    basis, height, width = locked.shape
    chunks = max(1, basis // 64)
    return pl.pallas_call(
        relayout_kernel,
        in_specs=[HBM],
        out_specs=[HBM, VMEM],
        out_shape=[
            pltpu.HBM((basis, height * width), locked.dtype),
            jax.ShapeDtypeStruct((8, 128), jnp.float32),
        ],
        scratch_shapes=[
            pltpu.VMEM((chunks, basis // chunks, height, width), locked.dtype),
            pltpu.VMEM((chunks, basis // chunks, height * width), locked.dtype),
            pltpu.SemaphoreType.DMA((chunks,)),
            pltpu.SemaphoreType.DMA((chunks,)),
        ],
        compiler_params=pltpu.CompilerParams(vmem_limit_bytes=16 << 20),
        name="relayout",
    )(in_hbm(locked))


def filter_kernel(panel_ref, sub_ref, *refs, panels, height, count, width):
    bodies = refs[0:panels]
    nears = refs[panels : 2 * panels]
    fars = refs[2 * panels : 3 * panels]
    locked_hbm, keep_ref, send_ref, own_ref, y_even, y_odd, split, locked_ref, sem = refs[3 * panels :]
    locked_copy = pltpu.make_async_copy(locked_hbm, locked_ref, sem)
    locked_copy.start()
    total = panels * width
    rows = height + 2 * HALO
    panel = panel_ref[0]
    first_sub = sub_ref[0] == 0

    def source(row):
        if HALO <= row < HALO + height:
            parts = [b[row - HALO] for b in bodies]
        elif row < HALO:
            parts = [jnp.where(first_sub, f[row], n[row]) for n, f in zip(nears, fars)]
        else:
            at = row - HALO - height
            parts = [jnp.where(first_sub, n[at], f[at]) for n, f in zip(nears, fars)]
        return jnp.concatenate(parts, axis=1)

    lane = lax.broadcasted_iota(jnp.int32, (1, total), 1)
    column = lax.rem(lane + panel * width, total)
    not_last = (column != total - 1).astype(jnp.float32)
    not_first = (column != 0).astype(jnp.float32)

    factor = 2.0 / SPREAD

    def left(x):
        return pltpu.roll(x, total - 1, 1)

    def right(x):
        return pltpu.roll(x, 1, 1)

    weights = []
    scale = []
    for row in range(rows):
        full = source(row)
        y_even[row] = full[0:count]
        side = full[count : count + SIDE]
        mass = side[4:5]
        inside = mass > 0.0
        scale.append(jnp.where(inside, 1.0 / jnp.sqrt(jnp.where(inside, mass, 1.0)), 0.0))
        weights.append([side[d : d + 1] for d in range(4)])
    edges = []
    for row in range(rows - 1):
        s0 = scale[row]
        s1 = scale[row + 1]
        w = weights[row]
        e0 = -factor * (w[0] * (s0 * left(s0))) * not_last
        e1 = -factor * (w[1] * (s0 * s1))
        e2 = -factor * (w[2] * (s0 * left(s1))) * not_last
        e3 = -factor * (w[3] * (s0 * right(s1))) * not_first
        edges.append((e0, e1, e2, e3))
    coefficients = [None]
    for row in range(1, rows - 1):
        w = weights[row]
        v = weights[row - 1]
        total_weight = (
            ((w[0] + w[1]) + (w[2] + w[3]))
            + (right(w[0] * not_last) + v[1])
            + (right(v[2] * not_last) + left(v[3] * not_first))
        )
        diagonal = factor * (scale[row] * scale[row] * total_weight - CENTRE)
        e0, e1, e2, e3 = edges[row]
        u0, u1, u2, u3 = edges[row - 1]
        coefficients.append((diagonal, e1, u1, right(e0), right(e2), u3, e0, left(e3), u2))

    buffers = (y_even, y_odd)
    for order in range(1, DEGREE + 1):
        source_ref = buffers[(order - 1) % 2]
        target_ref = buffers[order % 2]
        for row in range(order, rows - order):
            c = coefficients[row]
            ym = source_ref[row - 1]
            y0 = source_ref[row]
            yp = source_ref[row + 1]
            out = c[0] * y0 + (c[1] * yp + c[2] * ym)
            to_left = c[3] * y0 + (c[4] * yp + c[5] * ym)
            to_right = c[6] * y0 + (c[7] * yp + c[8] * ym)
            out = out + (left(to_left) + right(to_right))
            if order == 1:
                out = 0.5 * out
            else:
                out = out - target_ref[row]
            target_ref[row] = out
    result = buffers[DEGREE % 2]

    for row in range(height):
        full = result[row + HALO]
        own_ref[row] = full[:, 0:width]
        high = full.astype(jnp.bfloat16)
        rest = full - high.astype(jnp.float32)
        middle = rest.astype(jnp.bfloat16)
        low = (rest - middle.astype(jnp.float32)).astype(jnp.bfloat16)
        stacked = jnp.concatenate([high, middle, low], axis=0)
        for t in range(panels):
            at = row * total + lax.rem(panel + t, panels) * width
            split[:, pl.ds(pl.multiple_of(at, width), width)] = stacked[:, t * width : (t + 1) * width]

    dims = (((1,), (1,)), ((), ()))
    pieces = split[...]
    gram = lax.dot_general(pieces, pieces, dims, preferred_element_type=jnp.float32)
    gram = gram[0:count] + gram[count : 2 * count] + gram[2 * count : 3 * count]
    gram = gram[:, 0:count] + gram[:, count : 2 * count] + gram[:, 2 * count : 3 * count]
    locked_copy.wait()
    products = lax.dot_general(pieces, locked_ref[...], dims, preferred_element_type=jnp.float32)
    products = products[0:count] + products[count : 2 * count] + products[2 * count : 3 * count]
    half = products.shape[1] // 2
    lower = products[:, 0:half]
    upper = products[:, half:]
    keep_ref[0:count] = jnp.where(first_sub, lower, upper)
    send_ref[0:count] = jnp.where(first_sub, upper, lower)
    dense = fold(gram, half)
    keep_ref[count : count + 8] = dense
    send_ref[count : count + 8] = dense


def fold(gram, width):
    count = gram.shape[0]
    parts = [gram[r : r + 8] for r in range(0, count, 8)]
    spare = width - count * len(parts)
    if spare > 0:
        parts.append(jnp.zeros((8, spare), jnp.float32))
    return jnp.concatenate(parts, axis=1)


def filter_call(panel, sub, bodies, nears, fars, locked_flat):
    panels = len(bodies)
    height, planes, width = bodies[0].shape
    count = planes - SIDE
    basis = locked_flat.shape[0]
    total = panels * width
    rows = height + 2 * HALO
    payload = jax.ShapeDtypeStruct((count + 8, basis // 2), jnp.float32)
    return pl.pallas_call(
        lambda *refs: filter_kernel(*refs, panels=panels, height=height, count=count, width=width),
        in_specs=[SMEM, SMEM] + [VMEM] * (3 * panels) + [HBM],
        out_specs=[VMEM] * 3,
        out_shape=[payload, payload, jax.ShapeDtypeStruct((height, count, width), jnp.float32)],
        scratch_shapes=[
            pltpu.VMEM((rows, count, total), jnp.float32),
            pltpu.VMEM((rows, count, total), jnp.float32),
            pltpu.VMEM((3 * count, height * total), jnp.bfloat16),
            pltpu.VMEM(locked_flat.shape, jnp.bfloat16),
            pltpu.SemaphoreType.DMA(()),
        ],
        compiler_params=pltpu.CompilerParams(vmem_limit_bytes=20 << 20),
        name="filter",
    )(panel, sub, *bodies, *nears, *fars, in_hbm(locked_flat))


def factor_kernel(gram_ref, factor_ref, inverse_ref, *, vertices):
    count = factor_ref.shape[0]
    tiles = count // 8
    dense = gram_ref[...]
    row = lax.broadcasted_iota(jnp.int32, (8, 128), 0)
    col = lax.broadcasted_iota(jnp.int32, (8, 128), 1)
    blank = jnp.zeros((8, 128 - count), jnp.float32)

    def fill(x):
        return jnp.broadcast_to(x, (8, 128))

    work = []
    for t in range(tiles):
        gram = jnp.concatenate([dense[:, t * count : (t + 1) * count], blank], axis=1)
        at = row + 8 * t
        gram = gram * (1.0 / vertices) + jnp.where(at == col, 1e-06, 0.0)
        work.append(gram + jnp.where(at + count == col, 1.0, 0.0))
    for b in range(tiles):
        columns = {
            (t, k): fill(work[t][:, 8 * b + k : 8 * b + k + 1])
            for t in range(b, tiles)
            for k in range(8)
        }
        pivots = jnp.ones((8, 128), jnp.float32)
        for j in range(8):
            pivot = fill(columns[b, j][j : j + 1])
            pivots = jnp.where(row == j, pivot, pivots)
            inverse = 1.0 / pivot
            pivot_row = fill(work[b][j : j + 1])
            entries = {k: fill(columns[b, k][j : j + 1]) for k in range(j + 1, 8)}
            for t in range(b, tiles):
                multiplier = columns[t, j] * inverse
                if t == b:
                    multiplier = jnp.where(row > j, multiplier, 0.0)
                for k in range(j + 1, 8):
                    columns[t, k] = columns[t, k] - multiplier * entries[k]
                work[t] = work[t] - multiplier * pivot_row
        work[b] = work[b] * (1.0 / jnp.sqrt(pivots))
    for t in range(tiles):
        upper = jnp.where(row + 8 * t <= col, work[t], 0.0)
        factor_ref[8 * t : 8 * t + 8, :] = upper[:, 0:count]
        inverse_ref[8 * t : 8 * t + 8, :] = work[t][:, count : 2 * count]


def factorize(dense, count, vertices):
    square = jax.ShapeDtypeStruct((count, count), jnp.float32)
    return pl.pallas_call(
        lambda *refs: factor_kernel(*refs, vertices=float(vertices)),
        in_specs=[VMEM],
        out_specs=[VMEM, VMEM],
        out_shape=[square, square],
        compiler_params=pltpu.CompilerParams(vmem_limit_bytes=8 << 20),
        name="factor",
    )(dense)


def finish_kernel(
    sub_ref, inverse_ref, own_ref, mine_ref, other_ref, ortho_hbm, coupling_hbm,
    ortho_ref, coupling_ref, sems, *, vertices,
):
    height, count, width = own_ref.shape
    first_sub = sub_ref[0] == 0
    half = mine_ref.shape[1]
    mine = mine_ref[0:count]
    other = other_ref[...]
    inverse = inverse_ref[...]

    def times(left, right):
        return jnp.dot(
            left, right, precision=lax.Precision.HIGHEST, preferred_element_type=jnp.float32
        )

    flat = jnp.concatenate([own_ref[r] for r in range(height)], axis=1)
    ortho = times(inverse, flat)
    stacked = jnp.stack([ortho[:, r * width : (r + 1) * width] for r in range(height)], axis=0)
    ortho_ref[...] = pltpu.einshape("rbc->brc", stacked)
    ortho_copy = pltpu.make_async_copy(ortho_ref, ortho_hbm, sems.at[0])
    ortho_copy.start()
    inverse = inverse * (1.0 / math.sqrt(vertices))
    coupling_ref[:, 0:half] = times(inverse, jnp.where(first_sub, mine, other))
    coupling_ref[:, half:] = times(inverse, jnp.where(first_sub, other, mine))
    coupling_copy = pltpu.make_async_copy(coupling_ref, coupling_hbm, sems.at[1])
    coupling_copy.start()
    ortho_copy.wait()
    coupling_copy.wait()


def finish(sub, inverse, own, mine, other, vertices):
    height, count, width = own.shape
    ortho = (count, height, width)
    coupling = (count, 2 * mine.shape[1])
    return pl.pallas_call(
        lambda *refs: finish_kernel(*refs, vertices=float(vertices)),
        in_specs=[SMEM, VMEM, VMEM, VMEM, VMEM],
        out_specs=[HBM, HBM],
        out_shape=[jax.ShapeDtypeStruct(s, jnp.float32) for s in (ortho, coupling)],
        scratch_shapes=[
            pltpu.VMEM(ortho, jnp.float32),
            pltpu.VMEM(coupling, jnp.float32),
            pltpu.SemaphoreType.DMA((2,)),
        ],
        compiler_params=pltpu.CompilerParams(vmem_limit_bytes=8 << 20),
        name="finish",
    )(sub, inverse, own, mine, other)


def swap(array, axis, distance):
    size = lax.axis_size(axis)
    return lax.ppermute(array, axis, [(i, i ^ distance) for i in range(size)])


def strip_sum(part):
    strips = lax.axis_size("strip")
    distance = 1
    while distance * 4 < strips or distance * 2 == strips:
        part = part + swap(part, "strip", distance)
        distance *= 2
    if distance * 4 == strips:
        one = swap(part, "strip", distance)
        two = swap(part, "strip", 2 * distance)
        three = swap(part, "strip", 3 * distance)
        part = (part + one) + (two + three)
    return part


def on_device(start_block, edge_weights, mass, locked):
    panels = lax.axis_size("panel")
    lines = lax.axis_size(GRID_ROWS)
    count, height, width = start_block.shape
    vertices = height * width * lines * panels
    panel = lax.axis_index("panel").astype(jnp.int32).reshape(1)
    sub = lax.axis_index("sub").astype(jnp.int32).reshape(1)

    body, near, far = pack(sub, start_block, edge_weights, mass)
    bodies = [body]
    for shift in range(1, panels):
        bodies.append(
            lax.ppermute(body, "panel", [((i + shift) % panels, i) for i in range(panels)])
        )
    locked_flat, token = relayout(locked)
    across = []
    for line in range(1, lines - 1, 2):
        across += [(line, line + 1), (line + 1, line)]

    def exchange(near, far):
        return swap(near, "sub", 1), lax.ppermute(far, GRID_ROWS, across)

    halos = [exchange(near, far)]
    zero = token[0, 0]
    for other in bodies[1:]:
        edge = height - HALO
        halos.append(
            exchange(
                lax.dynamic_slice_in_dim(other, (1 - sub[0]) * edge, HALO, 0) + zero,
                lax.dynamic_slice_in_dim(other, sub[0] * edge, HALO, 0) + zero,
            )
        )
    keep, send, own = filter_call(
        panel, sub, bodies, [h[0] for h in halos], [h[1] for h in halos], locked_flat
    )
    part = strip_sum(keep + swap(send, "sub", 1))
    other = swap(part[:count], "sub", 1)
    factor, inverse = factorize(part[count:, : count * count // 8], count, vertices)
    ortho, coupling = finish(sub, inverse, own, part, other, vertices)
    return (ortho, jnp.transpose(coupling), factor)


def solution(mesh):
    return jax.shard_map(
        on_device,
        mesh=mesh,
        in_specs=(
            P("groups", ("strip", "sub"), "panel"),
            P("groups", ("strip", "sub"), "panel"),
            P(("groups", "strip", "sub"), "panel"),
            P(("groups", "panel"), ("strip", "sub"), None),
        ),
        out_specs=(
            P("groups", ("strip", "sub"), "panel"),
            P(("groups", "panel"), None),
            P("groups", None),
        ),
        check_vma=False,
    )
```

```python
import math

import jax
import jax.numpy as jnp
from jax import lax
from jax.experimental import pallas as pl
from jax.experimental.pallas import tpu as pltpu
from jax.sharding import PartitionSpec as P

DEGREE = 6
CUT_LOW = 2
CUT_HIGH = 32
CENTRE = 0.5 * (CUT_HIGH + CUT_LOW)
SPREAD = 0.5 * (CUT_HIGH - CUT_LOW)
HALO = DEGREE
GRID_ROWS = ("strip", "sub")
SIDE = 8

VMEM = pl.BlockSpec(memory_space=pltpu.VMEM)
SMEM = pl.BlockSpec(memory_space=pltpu.SMEM)
HBM = pl.BlockSpec(memory_space=pltpu.HBM)


def pack_kernel(
    sub_ref, block_hbm, weights_hbm, mass_hbm, body_ref, near_ref, far_ref,
    block_ref, weights_ref, mass_ref, sems,
):
    copies = [
        pltpu.make_async_copy(block_hbm, block_ref, sems.at[0]),
        pltpu.make_async_copy(weights_hbm.at[0:4], weights_ref, sems.at[1]),
        pltpu.make_async_copy(mass_hbm, mass_ref, sems.at[2]),
    ]
    for copy in copies:
        copy.start()
    for copy in copies:
        copy.wait()
    count, height, width = block_ref.shape
    body_ref[:, 0:count, :] = pltpu.einshape("brc->rbc", block_ref[...])
    mass = mass_ref[...][None]
    side = jnp.concatenate([weights_ref[...], mass, mass, mass, mass], axis=0)
    body_ref[:, count : count + SIDE, :] = pltpu.einshape("brc->rbc", side)
    sub = sub_ref[0]
    near_ref[...] = body_ref[pl.ds((1 - sub) * (height - HALO), HALO)]
    far_ref[...] = body_ref[pl.ds(sub * (height - HALO), HALO)]


def pack(sub, start_block, edge_weights, mass):
    count, height, width = start_block.shape
    halo = jax.ShapeDtypeStruct((HALO, count + SIDE, width), jnp.float32)
    return pl.pallas_call(
        pack_kernel,
        in_specs=[SMEM, HBM, HBM, HBM],
        out_specs=[VMEM, VMEM, VMEM],
        out_shape=[jax.ShapeDtypeStruct((height, count + SIDE, width), jnp.float32), halo, halo],
        scratch_shapes=[
            pltpu.VMEM((count, height, width), jnp.float32),
            pltpu.VMEM((4, height, width), jnp.float32),
            pltpu.VMEM((height, width), jnp.float32),
            pltpu.SemaphoreType.DMA((3,)),
        ],
        compiler_params=pltpu.CompilerParams(vmem_limit_bytes=8 << 20),
        name="pack",
    )(sub, *[in_hbm(x) for x in (start_block, edge_weights, mass)])


def in_hbm(array):
    return pltpu.with_memory_space_constraint(array, pltpu.HBM)


def in_vmem(array):
    return pltpu.with_memory_space_constraint(array, pltpu.VMEM)


def relayout_kernel(locked_hbm, flat_ref, chunks_ref, sems):
    chunks, size, height, width = chunks_ref.shape
    copies = [
        pltpu.make_async_copy(locked_hbm.at[pl.ds(i * size, size)], chunks_ref.at[i], sems.at[i])
        for i in range(chunks)
    ]
    for copy in copies:
        copy.start()
    for i in range(chunks):
        copies[i].wait()
        rows = pltpu.einshape("krc->rkc", chunks_ref[i])
        for r in range(height):
            flat_ref[pl.ds(i * size, size), r * width : (r + 1) * width] = rows[r]


def relayout(locked):
    basis, height, width = locked.shape
    chunks = max(1, basis // 64)
    return pl.pallas_call(
        relayout_kernel,
        in_specs=[HBM],
        out_specs=VMEM,
        out_shape=pltpu.VMEM((basis, height * width), locked.dtype),
        scratch_shapes=[
            pltpu.VMEM((chunks, basis // chunks, height, width), locked.dtype),
            pltpu.SemaphoreType.DMA((chunks,)),
        ],
        compiler_params=pltpu.CompilerParams(vmem_limit_bytes=12 << 20),
        name="relayout",
    )(in_hbm(locked))


def filter_kernel(panel_ref, sub_ref, *refs, panels, height, count, width):
    bodies = refs[0:panels]
    nears = refs[panels : 2 * panels]
    fars = refs[2 * panels : 3 * panels]
    locked_ref, keep_ref, send_ref, own_ref, y_even, y_odd, split = refs[3 * panels :]
    total = panels * width
    rows = height + 2 * HALO
    panel = panel_ref[0]
    first_sub = sub_ref[0] == 0

    def source(row):
        if HALO <= row < HALO + height:
            parts = [b[row - HALO] for b in bodies]
        elif row < HALO:
            parts = [jnp.where(first_sub, f[row], n[row]) for n, f in zip(nears, fars)]
        else:
            at = row - HALO - height
            parts = [jnp.where(first_sub, n[at], f[at]) for n, f in zip(nears, fars)]
        return jnp.concatenate(parts, axis=1)

    lane = lax.broadcasted_iota(jnp.int32, (1, total), 1)
    column = lax.rem(lane + panel * width, total)
    not_last = (column != total - 1).astype(jnp.float32)
    not_first = (column != 0).astype(jnp.float32)

    factor = 2.0 / SPREAD

    def left(x):
        return pltpu.roll(x, total - 1, 1)

    def right(x):
        return pltpu.roll(x, 1, 1)

    weights = []
    scale = []
    for row in range(rows):
        full = source(row)
        y_even[row] = full[0:count]
        side = full[count : count + SIDE]
        mass = side[4:5]
        inside = mass > 0.0
        scale.append(jnp.where(inside, 1.0 / jnp.sqrt(jnp.where(inside, mass, 1.0)), 0.0))
        weights.append([side[d : d + 1] for d in range(4)])
    edges = []
    for row in range(rows - 1):
        s0 = scale[row]
        s1 = scale[row + 1]
        w = weights[row]
        e0 = -factor * (w[0] * (s0 * left(s0))) * not_last
        e1 = -factor * (w[1] * (s0 * s1))
        e2 = -factor * (w[2] * (s0 * left(s1))) * not_last
        e3 = -factor * (w[3] * (s0 * right(s1))) * not_first
        edges.append((e0, e1, e2, e3))
    coefficients = [None]
    for row in range(1, rows - 1):
        w = weights[row]
        v = weights[row - 1]
        total_weight = (
            ((w[0] + w[1]) + (w[2] + w[3]))
            + (right(w[0] * not_last) + v[1])
            + (right(v[2] * not_last) + left(v[3] * not_first))
        )
        diagonal = factor * (scale[row] * scale[row] * total_weight - CENTRE)
        e0, e1, e2, e3 = edges[row]
        u0, u1, u2, u3 = edges[row - 1]
        coefficients.append((diagonal, e1, u1, right(e0), right(e2), u3, e0, left(e3), u2))

    buffers = (y_even, y_odd)
    for order in range(1, DEGREE + 1):
        source_ref = buffers[(order - 1) % 2]
        target_ref = buffers[order % 2]
        for row in range(order, rows - order):
            c = coefficients[row]
            ym = source_ref[row - 1]
            y0 = source_ref[row]
            yp = source_ref[row + 1]
            out = c[0] * y0 + (c[1] * yp + c[2] * ym)
            to_left = c[3] * y0 + (c[4] * yp + c[5] * ym)
            to_right = c[6] * y0 + (c[7] * yp + c[8] * ym)
            out = out + (left(to_left) + right(to_right))
            if order == 1:
                out = 0.5 * out
            else:
                out = out - target_ref[row]
            target_ref[row] = out
    result = buffers[DEGREE % 2]

    for row in range(height):
        full = result[row + HALO]
        own_ref[row] = full[:, 0:width]
        high = full.astype(jnp.bfloat16)
        rest = full - high.astype(jnp.float32)
        middle = rest.astype(jnp.bfloat16)
        low = (rest - middle.astype(jnp.float32)).astype(jnp.bfloat16)
        stacked = jnp.concatenate([high, middle, low], axis=0)
        for t in range(panels):
            at = row * total + lax.rem(panel + t, panels) * width
            split[:, pl.ds(pl.multiple_of(at, width), width)] = stacked[:, t * width : (t + 1) * width]

    dims = (((1,), (1,)), ((), ()))
    pieces = split[...]
    gram = lax.dot_general(pieces, pieces, dims, preferred_element_type=jnp.float32)
    gram = gram[0:count] + gram[count : 2 * count] + gram[2 * count : 3 * count]
    gram = gram[:, 0:count] + gram[:, count : 2 * count] + gram[:, 2 * count : 3 * count]
    products = lax.dot_general(pieces, locked_ref[...], dims, preferred_element_type=jnp.float32)
    products = products[0:count] + products[count : 2 * count] + products[2 * count : 3 * count]
    half = products.shape[1] // 2
    lower = products[:, 0:half]
    upper = products[:, half:]
    keep_ref[0:count] = jnp.where(first_sub, lower, upper)
    send_ref[0:count] = jnp.where(first_sub, upper, lower)
    dense = fold(gram, half)
    keep_ref[count : count + 8] = dense
    send_ref[count : count + 8] = dense


def fold(gram, width):
    count = gram.shape[0]
    parts = [gram[r : r + 8] for r in range(0, count, 8)]
    spare = width - count * len(parts)
    if spare > 0:
        parts.append(jnp.zeros((8, spare), jnp.float32))
    return jnp.concatenate(parts, axis=1)


def filter_call(panel, sub, bodies, nears, fars, locked_flat):
    panels = len(bodies)
    height, planes, width = bodies[0].shape
    count = planes - SIDE
    basis = locked_flat.shape[0]
    total = panels * width
    rows = height + 2 * HALO
    payload = jax.ShapeDtypeStruct((count + 8, basis // 2), jnp.float32)
    return pl.pallas_call(
        lambda *refs: filter_kernel(*refs, panels=panels, height=height, count=count, width=width),
        in_specs=[SMEM, SMEM] + [VMEM] * (3 * panels + 1),
        out_specs=[VMEM] * 3,
        out_shape=[payload, payload, jax.ShapeDtypeStruct((height, count, width), jnp.float32)],
        scratch_shapes=[
            pltpu.VMEM((rows, count, total), jnp.float32),
            pltpu.VMEM((rows, count, total), jnp.float32),
            pltpu.VMEM((3 * count, height * total), jnp.bfloat16),
        ],
        compiler_params=pltpu.CompilerParams(vmem_limit_bytes=20 << 20),
        name="filter",
    )(panel, sub, *bodies, *nears, *fars, in_vmem(locked_flat))


def factor_kernel(gram_ref, factor_ref, inverse_ref, *, vertices):
    count = factor_ref.shape[0]
    tiles = count // 8
    dense = gram_ref[...]
    row = lax.broadcasted_iota(jnp.int32, (8, 128), 0)
    col = lax.broadcasted_iota(jnp.int32, (8, 128), 1)
    blank = jnp.zeros((8, 128 - count), jnp.float32)

    def fill(x):
        return jnp.broadcast_to(x, (8, 128))

    work = []
    for t in range(tiles):
        gram = jnp.concatenate([dense[:, t * count : (t + 1) * count], blank], axis=1)
        at = row + 8 * t
        gram = gram * (1.0 / vertices) + jnp.where(at == col, 1e-06, 0.0)
        work.append(gram + jnp.where(at + count == col, 1.0, 0.0))
    for b in range(tiles):
        columns = {
            (t, k): fill(work[t][:, 8 * b + k : 8 * b + k + 1])
            for t in range(b, tiles)
            for k in range(8)
        }
        pivots = jnp.ones((8, 128), jnp.float32)
        for j in range(8):
            pivot = fill(columns[b, j][j : j + 1])
            pivots = jnp.where(row == j, pivot, pivots)
            inverse = 1.0 / pivot
            pivot_row = fill(work[b][j : j + 1])
            entries = {k: fill(columns[b, k][j : j + 1]) for k in range(j + 1, 8)}
            for t in range(b, tiles):
                multiplier = columns[t, j] * inverse
                if t == b:
                    multiplier = jnp.where(row > j, multiplier, 0.0)
                for k in range(j + 1, 8):
                    columns[t, k] = columns[t, k] - multiplier * entries[k]
                work[t] = work[t] - multiplier * pivot_row
        work[b] = work[b] * (1.0 / jnp.sqrt(pivots))
    for t in range(tiles):
        upper = jnp.where(row + 8 * t <= col, work[t], 0.0)
        factor_ref[8 * t : 8 * t + 8, :] = upper[:, 0:count]
        inverse_ref[8 * t : 8 * t + 8, :] = work[t][:, count : 2 * count]


def factorize(dense, count, vertices):
    square = jax.ShapeDtypeStruct((count, count), jnp.float32)
    return pl.pallas_call(
        lambda *refs: factor_kernel(*refs, vertices=float(vertices)),
        in_specs=[VMEM],
        out_specs=[VMEM, VMEM],
        out_shape=[square, square],
        compiler_params=pltpu.CompilerParams(vmem_limit_bytes=8 << 20),
        name="factor",
    )(dense)


def finish_kernel(
    sub_ref, inverse_ref, own_ref, mine_ref, other_ref, ortho_hbm, coupling_hbm,
    ortho_ref, coupling_ref, sems, *, vertices,
):
    height, count, width = own_ref.shape
    first_sub = sub_ref[0] == 0
    half = mine_ref.shape[1]
    mine = mine_ref[0:count]
    other = other_ref[...]
    inverse = inverse_ref[...]

    def times(left, right):
        return jnp.dot(
            left, right, precision=lax.Precision.HIGHEST, preferred_element_type=jnp.float32
        )

    flat = jnp.concatenate([own_ref[r] for r in range(height)], axis=1)
    ortho = times(inverse, flat)
    stacked = jnp.stack([ortho[:, r * width : (r + 1) * width] for r in range(height)], axis=0)
    ortho_ref[...] = pltpu.einshape("rbc->brc", stacked)
    ortho_copy = pltpu.make_async_copy(ortho_ref, ortho_hbm, sems.at[0])
    ortho_copy.start()
    inverse = inverse * (1.0 / math.sqrt(vertices))
    coupling_ref[:, 0:half] = times(inverse, jnp.where(first_sub, mine, other))
    coupling_ref[:, half:] = times(inverse, jnp.where(first_sub, other, mine))
    coupling_copy = pltpu.make_async_copy(coupling_ref, coupling_hbm, sems.at[1])
    coupling_copy.start()
    ortho_copy.wait()
    coupling_copy.wait()


def finish(sub, inverse, own, mine, other, vertices):
    height, count, width = own.shape
    ortho = (count, height, width)
    coupling = (count, 2 * mine.shape[1])
    return pl.pallas_call(
        lambda *refs: finish_kernel(*refs, vertices=float(vertices)),
        in_specs=[SMEM, VMEM, VMEM, VMEM, VMEM],
        out_specs=[HBM, HBM],
        out_shape=[jax.ShapeDtypeStruct(s, jnp.float32) for s in (ortho, coupling)],
        scratch_shapes=[
            pltpu.VMEM(ortho, jnp.float32),
            pltpu.VMEM(coupling, jnp.float32),
            pltpu.SemaphoreType.DMA((2,)),
        ],
        compiler_params=pltpu.CompilerParams(vmem_limit_bytes=8 << 20),
        name="finish",
    )(sub, inverse, own, mine, other)


def swap(array, axis, distance):
    size = lax.axis_size(axis)
    return lax.ppermute(array, axis, [(i, i ^ distance) for i in range(size)])


def strip_sum(part):
    strips = lax.axis_size("strip")
    distance = 1
    while distance * 4 < strips or distance * 2 == strips:
        part = part + swap(part, "strip", distance)
        distance *= 2
    if distance * 4 == strips:
        one = swap(part, "strip", distance)
        two = swap(part, "strip", 2 * distance)
        three = swap(part, "strip", 3 * distance)
        part = (part + one) + (two + three)
    return part


def on_device(start_block, edge_weights, mass, locked):
    panels = lax.axis_size("panel")
    lines = lax.axis_size(GRID_ROWS)
    count, height, width = start_block.shape
    vertices = height * width * lines * panels
    panel = lax.axis_index("panel").astype(jnp.int32).reshape(1)
    sub = lax.axis_index("sub").astype(jnp.int32).reshape(1)

    body, near, far = pack(sub, start_block, edge_weights, mass)
    bodies = [body]
    for shift in range(1, panels):
        bodies.append(
            lax.ppermute(body, "panel", [((i + shift) % panels, i) for i in range(panels)])
        )
    locked_flat = relayout(locked)
    across = []
    for line in range(1, lines - 1, 2):
        across += [(line, line + 1), (line + 1, line)]

    def exchange(near, far):
        return swap(near, "sub", 1), lax.ppermute(far, GRID_ROWS, across)

    halos = [exchange(near, far)]
    for other in bodies[1:]:
        edge = height - HALO
        halos.append(
            exchange(
                lax.dynamic_slice_in_dim(other, (1 - sub[0]) * edge, HALO, 0),
                lax.dynamic_slice_in_dim(other, sub[0] * edge, HALO, 0),
            )
        )
    keep, send, own = filter_call(
        panel, sub, bodies, [h[0] for h in halos], [h[1] for h in halos], locked_flat
    )
    part = strip_sum(keep + swap(send, "sub", 1))
    other = swap(part[:count], "sub", 1)
    factor, inverse = factorize(part[count:, : count * count // 8], count, vertices)
    ortho, coupling = finish(sub, inverse, own, part, other, vertices)
    return (ortho, jnp.transpose(coupling), factor)


def solution(mesh):
    return jax.shard_map(
        on_device,
        mesh=mesh,
        in_specs=(
            P("groups", ("strip", "sub"), "panel"),
            P("groups", ("strip", "sub"), "panel"),
            P(("groups", "strip", "sub"), "panel"),
            P(("groups", "panel"), ("strip", "sub"), None),
        ),
        out_specs=(
            P("groups", ("strip", "sub"), "panel"),
            P(("groups", "panel"), None),
            P("groups", None),
        ),
        check_vma=False,
    )
```

```python
import math

import jax
import jax.numpy as jnp
from jax import lax
from jax.experimental import pallas as pl
from jax.experimental.pallas import tpu as pltpu
from jax.sharding import PartitionSpec as P

DEGREE = 6
CUT_LOW = 2
CUT_HIGH = 32
CENTRE = 0.5 * (CUT_HIGH + CUT_LOW)
SPREAD = 0.5 * (CUT_HIGH - CUT_LOW)
HALO = DEGREE
GRID_ROWS = ("strip", "sub")
SIDE = 8
SLOT = 16
LOW_SHARE = 3

VMEM = pl.BlockSpec(memory_space=pltpu.VMEM)
SMEM = pl.BlockSpec(memory_space=pltpu.SMEM)
HBM = pl.BlockSpec(memory_space=pltpu.HBM)


def pack_kernel(
    sub_ref, block_hbm, weights_hbm, mass_hbm, body_ref, near_ref, far_ref, packet_ref,
    block_ref, weights_ref, mass_ref, sems,
):
    copies = [
        pltpu.make_async_copy(block_hbm, block_ref, sems.at[0]),
        pltpu.make_async_copy(weights_hbm.at[0:4], weights_ref, sems.at[1]),
        pltpu.make_async_copy(mass_hbm, mass_ref, sems.at[2]),
    ]
    for copy in copies:
        copy.start()
    for copy in copies:
        copy.wait()
    count, height, width = block_ref.shape
    body_ref[:, 0:count, :] = pltpu.einshape("brc->rbc", block_ref[...])
    mass = mass_ref[...][None]
    side = jnp.concatenate([weights_ref[...], mass, mass, mass, mass], axis=0)
    body_ref[:, count : count + SIDE, :] = pltpu.einshape("brc->rbc", side)
    sub = sub_ref[0]
    near_ref[...] = body_ref[pl.ds((1 - sub) * (height - HALO), HALO)]
    far_ref[...] = body_ref[pl.ds(sub * (height - HALO), HALO)]
    lane = lax.broadcasted_iota(jnp.int32, (count + SIDE, width), 1)
    for tile in range(height // 8):
        packet = pltpu.roll(body_ref[8 * tile], HALO, 1)
        for i in range(1, 8):
            moved = pltpu.roll(body_ref[8 * tile + i], HALO + SLOT * i, 1)
            packet = jnp.where(lane >= SLOT * i, moved, packet)
        packet_ref[tile] = packet


def pack(sub, start_block, edge_weights, mass):
    count, height, width = start_block.shape
    halo = jax.ShapeDtypeStruct((HALO, count + SIDE, width), jnp.float32)
    return pl.pallas_call(
        pack_kernel,
        in_specs=[SMEM, HBM, HBM, HBM],
        out_specs=[VMEM] * 4,
        out_shape=[
            jax.ShapeDtypeStruct((height, count + SIDE, width), jnp.float32),
            halo,
            halo,
            jax.ShapeDtypeStruct((height // 8, count + SIDE, width), jnp.float32),
        ],
        scratch_shapes=[
            pltpu.VMEM((count, height, width), jnp.float32),
            pltpu.VMEM((4, height, width), jnp.float32),
            pltpu.VMEM((height, width), jnp.float32),
            pltpu.SemaphoreType.DMA((3,)),
        ],
        compiler_params=pltpu.CompilerParams(vmem_limit_bytes=8 << 20),
        name="pack",
    )(sub, *[in_hbm(x) for x in (start_block, edge_weights, mass)])


def in_hbm(array):
    return pltpu.with_memory_space_constraint(array, pltpu.HBM)


def in_vmem(array):
    return pltpu.with_memory_space_constraint(array, pltpu.VMEM)


def relayout_kernel(locked_hbm, flat_ref, chunks_ref, sems, *, panels):
    chunks, size, height, total = chunks_ref.shape
    width = total // panels
    copies = [
        pltpu.make_async_copy(locked_hbm.at[pl.ds(i * size, size)], chunks_ref.at[i], sems.at[i])
        for i in range(chunks)
    ]
    for copy in copies:
        copy.start()
    for i in range(chunks):
        copies[i].wait()
        rows = pltpu.einshape("krc->rkc", chunks_ref[i])
        for r in range(height):
            for t in range(panels):
                at = (t * height + r) * width
                flat_ref[pl.ds(i * size, size), at : at + width] = rows[
                    r, :, t * width : (t + 1) * width
                ]


def relayout(locked, panels):
    basis, height, width = locked.shape
    chunks = max(1, basis // 64)
    return pl.pallas_call(
        lambda *refs: relayout_kernel(*refs, panels=panels),
        in_specs=[HBM],
        out_specs=VMEM,
        out_shape=pltpu.VMEM((basis, height * width), locked.dtype),
        scratch_shapes=[
            pltpu.VMEM((chunks, basis // chunks, height, width), locked.dtype),
            pltpu.SemaphoreType.DMA((chunks,)),
        ],
        compiler_params=pltpu.CompilerParams(vmem_limit_bytes=12 << 20),
        name="relayout",
    )(in_hbm(locked))


def filter_kernel(panel_ref, sub_ref, *refs, packets, first, panels):
    body_ref, near_ref, far_ref = refs[0:3]
    packet_refs = refs[3 : 3 + packets]
    if first:
        own_ref, coef_ref, y_even, y_odd = refs[4 + packets :]
    else:
        coef_ref, own_ref, y_even, y_odd = refs[3 + packets :]
    height, planes, width = body_ref.shape
    count = own_ref.shape[1]
    total = 2 * width
    rows = height + 2 * HALO
    start = 0 if first else planes - SIDE - count
    first_sub = sub_ref[0] == 0

    def unpack(tiles, i, lane):
        moved = [pltpu.roll(t, width - HALO - SLOT * i, 1) for t in tiles]
        after = jnp.where(lane < HALO, moved[0], 0.0)
        return jnp.where(lane >= width - HALO, moved[-1], after)

    def source(row, at, size):
        cut = slice(at, at + size)
        lane = lax.broadcasted_iota(jnp.int32, (size, width), 1)
        if HALO <= row < HALO + height:
            line = row - HALO
            own = body_ref[line, cut]
            tiles = [p[line // 8, cut] for p in packet_refs]
            i = line % 8
        else:
            if row < HALO:
                upper, lower, line, i = far_ref, near_ref, row, row + 8 - HALO
            else:
                upper, lower, line, i = near_ref, far_ref, row - HALO - height, row - HALO - height
            own = jnp.where(first_sub, upper[line, cut], lower[line, cut])
            tiles = [
                jnp.where(first_sub, upper[HALO + q, cut], lower[HALO + q, cut])
                for q in range(packets)
            ]
        return jnp.concatenate([own, unpack(tiles, i, lane)], axis=1)

    def left(x):
        return pltpu.roll(x, total - 1, 1)

    def right(x):
        return pltpu.roll(x, 1, 1)

    for row in range(rows):
        y_even[row] = source(row, start, count)

    if first:
        whole = panels * width
        lane = lax.broadcasted_iota(jnp.int32, (1, total), 1)
        lane = jnp.where(lane < width + width // 2, lane, lane - total + whole)
        column = lax.rem(lane + panel_ref[0] * width, whole)
        not_last = (column != whole - 1).astype(jnp.float32)
        not_first = (column != 0).astype(jnp.float32)
        factor = 2.0 / SPREAD
        weights = []
        scale = []
        for row in range(rows):
            side = source(row, planes - SIDE, SIDE)
            mass = side[4:5]
            inside = mass > 0.0
            scale.append(jnp.where(inside, 1.0 / jnp.sqrt(jnp.where(inside, mass, 1.0)), 0.0))
            weights.append([side[d : d + 1] for d in range(4)])
        edges = []
        for row in range(rows - 1):
            s0 = scale[row]
            s1 = scale[row + 1]
            w = weights[row]
            e0 = -factor * (w[0] * (s0 * left(s0))) * not_last
            e1 = -factor * (w[1] * (s0 * s1))
            e2 = -factor * (w[2] * (s0 * left(s1))) * not_last
            e3 = -factor * (w[3] * (s0 * right(s1))) * not_first
            edges.append((e0, e1, e2, e3))
        for row in range(1, rows - 1):
            w = weights[row]
            v = weights[row - 1]
            total_weight = (
                ((w[0] + w[1]) + (w[2] + w[3]))
                + (right(w[0] * not_last) + v[1])
                + (right(v[2] * not_last) + left(v[3] * not_first))
            )
            diagonal = factor * (scale[row] * scale[row] * total_weight - CENTRE)
            e0, e1, e2, e3 = edges[row]
            u0, u1, u2, u3 = edges[row - 1]
            planes_here = (diagonal, e1, u1, right(e0), right(e2), u3, e0, left(e3), u2)
            for index, plane in enumerate(planes_here):
                coef_ref[row, index : index + 1] = plane

    buffers = (y_even, y_odd)
    for order in range(1, DEGREE + 1):
        source_ref = buffers[(order - 1) % 2]
        target_ref = buffers[order % 2]
        for row in range(order, rows - order):
            c = [coef_ref[row, i : i + 1] for i in range(9)]
            ym = source_ref[row - 1]
            y0 = source_ref[row]
            yp = source_ref[row + 1]
            out = c[0] * y0 + (c[1] * yp + c[2] * ym)
            to_left = c[3] * y0 + (c[4] * yp + c[5] * ym)
            to_right = c[6] * y0 + (c[7] * yp + c[8] * ym)
            out = out + (left(to_left) + right(to_right))
            if order == 1:
                out = 0.5 * out
            else:
                out = out - target_ref[row]
            if order == DEGREE:
                own_ref[row - HALO] = out[:, 0:width]
            else:
                target_ref[row] = out


def filter_part(panel, sub, body, near, far, packets, panels, coef=None, ahead=None):
    height, planes, width = body.shape
    first = coef is None
    low = LOW_SHARE * (planes - SIDE) // 4
    count = low if first else planes - SIDE - low
    rows = height + 2 * HALO
    own = jax.ShapeDtypeStruct((height, count, width), jnp.float32)
    out = [own, jax.ShapeDtypeStruct((rows, 16, 2 * width), jnp.float32)] if first else own
    operands = [panel, sub, body, near, far, *packets, ahead if first else coef]
    buffer = pltpu.VMEM((rows, count, 2 * width), jnp.float32)
    return pl.pallas_call(
        lambda *refs: filter_kernel(*refs, packets=len(packets), first=first, panels=panels),
        in_specs=[SMEM, SMEM] + [VMEM] * (len(operands) - 2),
        out_specs=[VMEM, VMEM] if first else VMEM,
        out_shape=out,
        scratch_shapes=[buffer, buffer],
        compiler_params=pltpu.CompilerParams(vmem_limit_bytes=16 << 20),
        cost_estimate=pl.CostEstimate(flops=1, transcendentals=0, bytes_accessed=1),
        name="filter",
    )(*operands)


def product_kernel(block_ref, sub_ref, *refs, begin, last):
    part_refs = refs[0:2]
    locked_ref = refs[2]
    split = refs[-1]
    height, _, width = part_refs[0].shape
    count = part_refs[0].shape[1] + part_refs[1].shape[1]
    for row in range(height):
        full = jnp.concatenate([part[row] for part in part_refs], axis=0)
        high = full.astype(jnp.bfloat16)
        rest = full - high.astype(jnp.float32)
        middle = rest.astype(jnp.bfloat16)
        low = (rest - middle.astype(jnp.float32)).astype(jnp.bfloat16)
        split[:, row * width : (row + 1) * width] = jnp.concatenate([high, middle, low], axis=0)

    dims = (((1,), (1,)), ((), ()))
    pieces = split[...]
    gram = lax.dot_general(pieces, pieces, dims, preferred_element_type=jnp.float32)
    gram = gram[0:count] + gram[count : 2 * count] + gram[2 * count : 3 * count]
    gram = gram[:, 0:count] + gram[:, count : 2 * count] + gram[:, 2 * count : 3 * count]
    span = height * width
    at = pl.multiple_of(block_ref[0] * span, span)
    products = lax.dot_general(
        pieces, locked_ref[:, pl.ds(at, span)], dims, preferred_element_type=jnp.float32
    )
    products = products[0:count] + products[count : 2 * count] + products[2 * count : 3 * count]
    basis = products.shape[1]
    half = basis // 2
    dense = fold(gram, half)
    if not begin:
        sum_ref = refs[3]
        products = products + sum_ref[0:count]
        dense = dense + sum_ref[count : count + 8, 0:half]
    if last:
        keep_ref, send_ref = refs[-3], refs[-2]
        first_sub = sub_ref[0] == 0
        lower = products[:, 0:half]
        upper = products[:, half:]
        keep_ref[0:count] = jnp.where(first_sub, lower, upper)
        send_ref[0:count] = jnp.where(first_sub, upper, lower)
        keep_ref[count : count + 8] = dense
        send_ref[count : count + 8] = dense
    else:
        out_ref = refs[-2]
        out_ref[0:count] = products
        out_ref[count : count + 8, 0:half] = dense


def fold(gram, width):
    count = gram.shape[0]
    parts = [gram[r : r + 8] for r in range(0, count, 8)]
    spare = width - count * len(parts)
    if spare > 0:
        parts.append(jnp.zeros((8, spare), jnp.float32))
    return jnp.concatenate(parts, axis=1)


def products(block, sub, parts, locked_flat, before, last):
    height, _, width = parts[0].shape
    count = parts[0].shape[1] + parts[1].shape[1]
    basis = locked_flat.shape[0]
    begin = before is None
    operands = [block, sub, *parts, in_vmem(locked_flat)] + ([] if begin else [before])
    whole = jax.ShapeDtypeStruct((count + 8, basis), jnp.float32)
    half = jax.ShapeDtypeStruct((count + 8, basis // 2), jnp.float32)
    return pl.pallas_call(
        lambda *refs: product_kernel(*refs, begin=begin, last=last),
        in_specs=[SMEM, SMEM] + [VMEM] * (len(operands) - 2),
        out_specs=[VMEM, VMEM] if last else VMEM,
        out_shape=[half, half] if last else whole,
        scratch_shapes=[pltpu.VMEM((3 * count, height * width), jnp.bfloat16)],
        compiler_params=pltpu.CompilerParams(vmem_limit_bytes=12 << 20),
        cost_estimate=pl.CostEstimate(flops=1, transcendentals=0, bytes_accessed=1),
        name="products",
    )(*operands)


def factor_kernel(gram_ref, factor_ref, inverse_ref, *, vertices):
    count = factor_ref.shape[0]
    tiles = count // 8
    dense = gram_ref[...]
    row = lax.broadcasted_iota(jnp.int32, (8, 128), 0)
    col = lax.broadcasted_iota(jnp.int32, (8, 128), 1)
    blank = jnp.zeros((8, 128 - count), jnp.float32)

    def fill(x):
        return jnp.broadcast_to(x, (8, 128))

    work = []
    for t in range(tiles):
        gram = jnp.concatenate([dense[:, t * count : (t + 1) * count], blank], axis=1)
        at = row + 8 * t
        gram = gram * (1.0 / vertices) + jnp.where(at == col, 1e-06, 0.0)
        work.append(gram + jnp.where(at + count == col, 1.0, 0.0))
    for b in range(tiles):
        columns = {
            (t, k): fill(work[t][:, 8 * b + k : 8 * b + k + 1])
            for t in range(b, tiles)
            for k in range(8)
        }
        pivots = jnp.ones((8, 128), jnp.float32)
        for j in range(8):
            pivot = fill(columns[b, j][j : j + 1])
            pivots = jnp.where(row == j, pivot, pivots)
            inverse = 1.0 / pivot
            pivot_row = fill(work[b][j : j + 1])
            entries = {k: fill(columns[b, k][j : j + 1]) for k in range(j + 1, 8)}
            for t in range(b, tiles):
                multiplier = columns[t, j] * inverse
                if t == b:
                    multiplier = jnp.where(row > j, multiplier, 0.0)
                for k in range(j + 1, 8):
                    columns[t, k] = columns[t, k] - multiplier * entries[k]
                work[t] = work[t] - multiplier * pivot_row
        work[b] = work[b] * (1.0 / jnp.sqrt(pivots))
    for t in range(tiles):
        upper = jnp.where(row + 8 * t <= col, work[t], 0.0)
        factor_ref[8 * t : 8 * t + 8, :] = upper[:, 0:count]
        inverse_ref[8 * t : 8 * t + 8, :] = work[t][:, count : 2 * count]


def factorize(dense, count, vertices):
    square = jax.ShapeDtypeStruct((count, count), jnp.float32)
    return pl.pallas_call(
        lambda *refs: factor_kernel(*refs, vertices=float(vertices)),
        in_specs=[VMEM],
        out_specs=[VMEM, VMEM],
        out_shape=[square, square],
        compiler_params=pltpu.CompilerParams(vmem_limit_bytes=8 << 20),
        name="factor",
    )(dense)


def finish_kernel(
    sub_ref, inverse_ref, low_ref, high_ref, mine_ref, other_ref, ortho_hbm, coupling_hbm,
    ortho_ref, coupling_ref, sems, *, vertices,
):
    count, height, width = ortho_ref.shape
    first_sub = sub_ref[0] == 0
    half = mine_ref.shape[1]
    mine = mine_ref[0:count]
    other = other_ref[...]
    inverse = inverse_ref[...]

    def times(left, right):
        return jnp.dot(
            left, right, precision=lax.Precision.HIGHEST, preferred_element_type=jnp.float32
        )

    flat = jnp.concatenate(
        [jnp.concatenate([low_ref[r], high_ref[r]], axis=0) for r in range(height)], axis=1
    )
    ortho = times(inverse, flat)
    stacked = jnp.stack([ortho[:, r * width : (r + 1) * width] for r in range(height)], axis=0)
    ortho_ref[...] = pltpu.einshape("rbc->brc", stacked)
    ortho_copy = pltpu.make_async_copy(ortho_ref, ortho_hbm, sems.at[0])
    ortho_copy.start()
    inverse = inverse * (1.0 / math.sqrt(vertices))
    coupling_ref[:, 0:half] = times(inverse, jnp.where(first_sub, mine, other))
    coupling_ref[:, half:] = times(inverse, jnp.where(first_sub, other, mine))
    coupling_copy = pltpu.make_async_copy(coupling_ref, coupling_hbm, sems.at[1])
    coupling_copy.start()
    ortho_copy.wait()
    coupling_copy.wait()


def finish(sub, inverse, parts, mine, other, vertices):
    height, _, width = parts[0].shape
    count = parts[0].shape[1] + parts[1].shape[1]
    ortho = (count, height, width)
    coupling = (count, 2 * mine.shape[1])
    return pl.pallas_call(
        lambda *refs: finish_kernel(*refs, vertices=float(vertices)),
        in_specs=[SMEM] + [VMEM] * 5,
        out_specs=[HBM, HBM],
        out_shape=[jax.ShapeDtypeStruct(s, jnp.float32) for s in (ortho, coupling)],
        scratch_shapes=[
            pltpu.VMEM(ortho, jnp.float32),
            pltpu.VMEM(coupling, jnp.float32),
            pltpu.SemaphoreType.DMA((2,)),
        ],
        compiler_params=pltpu.CompilerParams(vmem_limit_bytes=8 << 20),
        name="finish",
    )(sub, inverse, *parts, mine, other)


def swap(array, axis, distance):
    size = lax.axis_size(axis)
    return lax.ppermute(array, axis, [(i, i ^ distance) for i in range(size)])


def shifted(array, shift):
    size = lax.axis_size("panel")
    return lax.ppermute(array, "panel", [((i + shift) % size, i) for i in range(size)])


def strip_sum(part):
    strips = lax.axis_size("strip")
    distance = 1
    while distance * 4 < strips or distance * 2 == strips:
        part = part + swap(part, "strip", distance)
        distance *= 2
    if distance * 4 == strips:
        one = swap(part, "strip", distance)
        two = swap(part, "strip", 2 * distance)
        three = swap(part, "strip", 3 * distance)
        part = (part + one) + (two + three)
    return part


def on_device(start_block, edge_weights, mass, locked):
    panels = lax.axis_size("panel")
    lines = lax.axis_size(GRID_ROWS)
    count, height, width = start_block.shape
    vertices = height * width * lines * panels
    panel = lax.axis_index("panel").astype(jnp.int32).reshape(1)
    sub = lax.axis_index("sub").astype(jnp.int32).reshape(1)

    body, near, far, packet = pack(sub, start_block, edge_weights, mass)
    packets = [shifted(packet, 1)]
    if panels > 2:
        packets.append(shifted(packet, panels - 1))
    locked_flat = relayout(locked, panels)
    across = []
    for line in range(1, lines - 1, 2):
        across += [(line, line + 1), (line + 1, line)]
    tiles = height // 8 - 1

    def with_edges(rows, tile):
        edges = [lax.dynamic_slice_in_dim(p, tile * tiles, 1, 0) for p in packets]
        return jnp.concatenate([rows] + edges, axis=0)

    near = swap(with_edges(near, 1 - sub[0]), "sub", 1)
    far = lax.ppermute(with_edges(far, sub[0]), GRID_ROWS, across)
    low, coef = filter_part(
        panel, sub, body, near, far, packets, panels, ahead=in_vmem(locked_flat)
    )
    blocks = [[low]]
    blocks += [[shifted(low, t)] for t in range(1, panels)]
    high = filter_part(panel, sub, body, near, far, packets, panels, coef)
    blocks[0].append(high)
    for t in range(1, panels):
        blocks[t].append(shifted(high, t))
    total = None
    for t in range(panels):
        block = lax.rem(panel + t, panels)
        total = products(block, sub, blocks[t], locked_flat, total, t == panels - 1)
    keep, send = total
    part = strip_sum(keep + swap(send, "sub", 1))
    other = swap(part[:count], "sub", 1)
    factor, inverse = factorize(part[count:, : count * count // 8], count, vertices)
    ortho, coupling = finish(sub, inverse, blocks[0], part, other, vertices)
    return (ortho, jnp.transpose(coupling), factor)


def solution(mesh):
    return jax.shard_map(
        on_device,
        mesh=mesh,
        in_specs=(
            P("groups", ("strip", "sub"), "panel"),
            P("groups", ("strip", "sub"), "panel"),
            P(("groups", "strip", "sub"), "panel"),
            P(("groups", "panel"), ("strip", "sub"), None),
        ),
        out_specs=(
            P("groups", ("strip", "sub"), "panel"),
            P(("groups", "panel"), None),
            P("groups", None),
        ),
        check_vma=False,
    )
```

```python
import math

import jax
import jax.numpy as jnp
from jax import lax
from jax.experimental import pallas as pl
from jax.experimental.pallas import tpu as pltpu
from jax.sharding import PartitionSpec as P

DEGREE = 6
CUT_LOW = 2
CUT_HIGH = 32
CENTRE = 0.5 * (CUT_HIGH + CUT_LOW)
SPREAD = 0.5 * (CUT_HIGH - CUT_LOW)
HALO = DEGREE
GRID_ROWS = ("strip", "sub")
SIDE = 8

VMEM = pl.BlockSpec(memory_space=pltpu.VMEM)
SMEM = pl.BlockSpec(memory_space=pltpu.SMEM)
HBM = pl.BlockSpec(memory_space=pltpu.HBM)


def pack_kernel(
    sub_ref, block_hbm, weights_hbm, mass_hbm, body_ref, near_ref, far_ref,
    block_ref, weights_ref, mass_ref, sems,
):
    copies = [
        pltpu.make_async_copy(block_hbm, block_ref, sems.at[0]),
        pltpu.make_async_copy(weights_hbm.at[0:4], weights_ref, sems.at[1]),
        pltpu.make_async_copy(mass_hbm, mass_ref, sems.at[2]),
    ]
    for copy in copies:
        copy.start()
    for copy in copies:
        copy.wait()
    count, height, width = block_ref.shape
    body_ref[:, 0:count, :] = pltpu.einshape("brc->rbc", block_ref[...])
    mass = mass_ref[...][None]
    side = jnp.concatenate([weights_ref[...], mass, mass, mass, mass], axis=0)
    body_ref[:, count : count + SIDE, :] = pltpu.einshape("brc->rbc", side)
    sub = sub_ref[0]
    near_ref[...] = body_ref[pl.ds((1 - sub) * (height - HALO), HALO)]
    far_ref[...] = body_ref[pl.ds(sub * (height - HALO), HALO)]


def pack(sub, start_block, edge_weights, mass):
    count, height, width = start_block.shape
    halo = jax.ShapeDtypeStruct((HALO, count + SIDE, width), jnp.float32)
    return pl.pallas_call(
        pack_kernel,
        in_specs=[SMEM, HBM, HBM, HBM],
        out_specs=[VMEM, VMEM, VMEM],
        out_shape=[jax.ShapeDtypeStruct((height, count + SIDE, width), jnp.float32), halo, halo],
        scratch_shapes=[
            pltpu.VMEM((count, height, width), jnp.float32),
            pltpu.VMEM((4, height, width), jnp.float32),
            pltpu.VMEM((height, width), jnp.float32),
            pltpu.SemaphoreType.DMA((3,)),
        ],
        compiler_params=pltpu.CompilerParams(vmem_limit_bytes=8 << 20),
        name="pack",
    )(sub, *[in_hbm(x) for x in (start_block, edge_weights, mass)])


def in_hbm(array):
    return pltpu.with_memory_space_constraint(array, pltpu.HBM)


def in_vmem(array):
    return pltpu.with_memory_space_constraint(array, pltpu.VMEM)


def relayout_kernel(locked_hbm, flat_ref, chunks_ref, sems):
    chunks, size, height, width = chunks_ref.shape
    copies = [
        pltpu.make_async_copy(locked_hbm.at[pl.ds(i * size, size)], chunks_ref.at[i], sems.at[i])
        for i in range(chunks)
    ]
    for copy in copies:
        copy.start()
    for i in range(chunks):
        copies[i].wait()
        rows = pltpu.einshape("krc->rkc", chunks_ref[i])
        for r in range(height):
            flat_ref[pl.ds(i * size, size), r * width : (r + 1) * width] = rows[r]


def relayout(locked):
    basis, height, width = locked.shape
    chunks = max(1, basis // 64)
    return pl.pallas_call(
        relayout_kernel,
        in_specs=[HBM],
        out_specs=VMEM,
        out_shape=pltpu.VMEM((basis, height * width), locked.dtype),
        scratch_shapes=[
            pltpu.VMEM((chunks, basis // chunks, height, width), locked.dtype),
            pltpu.SemaphoreType.DMA((chunks,)),
        ],
        compiler_params=pltpu.CompilerParams(vmem_limit_bytes=12 << 20),
        name="relayout",
    )(in_hbm(locked))


def filter_kernel(panel_ref, sub_ref, *refs, panels, height, count, width):
    bodies = refs[0:panels]
    nears = refs[panels : 2 * panels]
    fars = refs[2 * panels : 3 * panels]
    locked_ref, keep_ref, send_ref, own_ref, y_even, y_odd, split = refs[3 * panels :]
    total = panels * width
    rows = height + 2 * HALO
    panel = panel_ref[0]
    first_sub = sub_ref[0] == 0

    def source(row):
        if HALO <= row < HALO + height:
            parts = [b[row - HALO] for b in bodies]
        elif row < HALO:
            parts = [jnp.where(first_sub, f[row], n[row]) for n, f in zip(nears, fars)]
        else:
            at = row - HALO - height
            parts = [jnp.where(first_sub, n[at], f[at]) for n, f in zip(nears, fars)]
        return jnp.concatenate(parts, axis=1)

    lane = lax.broadcasted_iota(jnp.int32, (1, total), 1)
    column = lax.rem(lane + panel * width, total)
    not_last = (column != total - 1).astype(jnp.float32)
    not_first = (column != 0).astype(jnp.float32)

    factor = 2.0 / SPREAD

    def left(x):
        return pltpu.roll(x, total - 1, 1)

    def right(x):
        return pltpu.roll(x, 1, 1)

    weights = []
    scale = []
    for row in range(rows):
        full = source(row)
        y_even[row] = full[0:count]
        side = full[count : count + SIDE]
        mass = side[4:5]
        inside = mass > 0.0
        scale.append(jnp.where(inside, 1.0 / jnp.sqrt(jnp.where(inside, mass, 1.0)), 0.0))
        weights.append([side[d : d + 1] for d in range(4)])
    edges = []
    for row in range(rows - 1):
        s0 = scale[row]
        s1 = scale[row + 1]
        w = weights[row]
        e0 = -factor * (w[0] * (s0 * left(s0))) * not_last
        e1 = -factor * (w[1] * (s0 * s1))
        e2 = -factor * (w[2] * (s0 * left(s1))) * not_last
        e3 = -factor * (w[3] * (s0 * right(s1))) * not_first
        edges.append((e0, e1, e2, e3))
    coefficients = [None]
    for row in range(1, rows - 1):
        w = weights[row]
        v = weights[row - 1]
        total_weight = (
            ((w[0] + w[1]) + (w[2] + w[3]))
            + (right(w[0] * not_last) + v[1])
            + (right(v[2] * not_last) + left(v[3] * not_first))
        )
        diagonal = factor * (scale[row] * scale[row] * total_weight - CENTRE)
        e0, e1, e2, e3 = edges[row]
        u0, u1, u2, u3 = edges[row - 1]
        coefficients.append((diagonal, e1, u1, right(e0), right(e2), u3, e0, left(e3), u2))

    buffers = (y_even, y_odd)
    for order in range(1, DEGREE + 1):
        source_ref = buffers[(order - 1) % 2]
        target_ref = buffers[order % 2]
        for row in range(order, rows - order):
            c = coefficients[row]
            ym = source_ref[row - 1]
            y0 = source_ref[row]
            yp = source_ref[row + 1]
            out = c[0] * y0 + (c[1] * yp + c[2] * ym)
            to_left = c[3] * y0 + (c[4] * yp + c[5] * ym)
            to_right = c[6] * y0 + (c[7] * yp + c[8] * ym)
            out = out + (left(to_left) + right(to_right))
            if order == 1:
                out = 0.5 * out
            else:
                out = out - target_ref[row]
            target_ref[row] = out
    result = buffers[DEGREE % 2]

    for row in range(height):
        full = result[row + HALO]
        own_ref[row] = full[:, 0:width]
        high = full.astype(jnp.bfloat16)
        rest = full - high.astype(jnp.float32)
        middle = rest.astype(jnp.bfloat16)
        low = (rest - middle.astype(jnp.float32)).astype(jnp.bfloat16)
        stacked = jnp.concatenate([high, middle, low], axis=0)
        for t in range(panels):
            at = row * total + lax.rem(panel + t, panels) * width
            split[:, pl.ds(pl.multiple_of(at, width), width)] = stacked[:, t * width : (t + 1) * width]

    dims = (((1,), (1,)), ((), ()))
    pieces = split[...]
    gram = lax.dot_general(pieces, pieces, dims, preferred_element_type=jnp.float32)
    gram = gram[0:count] + gram[count : 2 * count] + gram[2 * count : 3 * count]
    gram = gram[:, 0:count] + gram[:, count : 2 * count] + gram[:, 2 * count : 3 * count]
    products = lax.dot_general(pieces, locked_ref[...], dims, preferred_element_type=jnp.float32)
    products = products[0:count] + products[count : 2 * count] + products[2 * count : 3 * count]
    half = products.shape[1] // 2
    lower = products[:, 0:half]
    upper = products[:, half:]
    keep_ref[0:count] = jnp.where(first_sub, lower, upper)
    send_ref[0:count] = jnp.where(first_sub, upper, lower)
    dense = fold(gram, half)
    keep_ref[count : count + 8] = dense
    send_ref[count : count + 8] = dense


def fold(gram, width):
    count = gram.shape[0]
    parts = [gram[r : r + 8] for r in range(0, count, 8)]
    spare = width - count * len(parts)
    if spare > 0:
        parts.append(jnp.zeros((8, spare), jnp.float32))
    return jnp.concatenate(parts, axis=1)


def filter_call(panel, sub, bodies, nears, fars, locked_flat):
    panels = len(bodies)
    height, planes, width = bodies[0].shape
    count = planes - SIDE
    basis = locked_flat.shape[0]
    total = panels * width
    rows = height + 2 * HALO
    payload = jax.ShapeDtypeStruct((count + 8, basis // 2), jnp.float32)
    return pl.pallas_call(
        lambda *refs: filter_kernel(*refs, panels=panels, height=height, count=count, width=width),
        in_specs=[SMEM, SMEM] + [VMEM] * (3 * panels + 1),
        out_specs=[VMEM] * 3,
        out_shape=[payload, payload, jax.ShapeDtypeStruct((height, count, width), jnp.float32)],
        scratch_shapes=[
            pltpu.VMEM((rows, count, total), jnp.float32),
            pltpu.VMEM((rows, count, total), jnp.float32),
            pltpu.VMEM((3 * count, height * total), jnp.bfloat16),
        ],
        compiler_params=pltpu.CompilerParams(vmem_limit_bytes=20 << 20),
        name="filter",
    )(panel, sub, *bodies, *nears, *fars, locked_flat)


def factor_kernel(gram_ref, factor_ref, inverse_ref, *, vertices):
    count = factor_ref.shape[0]
    tiles = count // 8
    dense = gram_ref[...]
    row = lax.broadcasted_iota(jnp.int32, (8, 128), 0)
    col = lax.broadcasted_iota(jnp.int32, (8, 128), 1)
    blank = jnp.zeros((8, 128 - count), jnp.float32)

    def fill(x):
        return jnp.broadcast_to(x, (8, 128))

    work = []
    for t in range(tiles):
        gram = jnp.concatenate([dense[:, t * count : (t + 1) * count], blank], axis=1)
        at = row + 8 * t
        gram = gram * (1.0 / vertices) + jnp.where(at == col, 1e-06, 0.0)
        work.append(gram + jnp.where(at + count == col, 1.0, 0.0))
    for b in range(tiles):
        columns = {
            (t, k): fill(work[t][:, 8 * b + k : 8 * b + k + 1])
            for t in range(b, tiles)
            for k in range(8)
        }
        pivots = jnp.ones((8, 128), jnp.float32)
        for j in range(8):
            pivot = fill(columns[b, j][j : j + 1])
            pivots = jnp.where(row == j, pivot, pivots)
            inverse = 1.0 / pivot
            pivot_row = fill(work[b][j : j + 1])
            entries = {k: fill(columns[b, k][j : j + 1]) for k in range(j + 1, 8)}
            for t in range(b, tiles):
                multiplier = columns[t, j] * inverse
                if t == b:
                    multiplier = jnp.where(row > j, multiplier, 0.0)
                for k in range(j + 1, 8):
                    columns[t, k] = columns[t, k] - multiplier * entries[k]
                work[t] = work[t] - multiplier * pivot_row
        work[b] = work[b] * (1.0 / jnp.sqrt(pivots))
    for t in range(tiles):
        upper = jnp.where(row + 8 * t <= col, work[t], 0.0)
        factor_ref[8 * t : 8 * t + 8, :] = upper[:, 0:count]
        inverse_ref[8 * t : 8 * t + 8, :] = work[t][:, count : 2 * count]


def factorize(dense, count, vertices):
    square = jax.ShapeDtypeStruct((count, count), jnp.float32)
    return pl.pallas_call(
        lambda *refs: factor_kernel(*refs, vertices=float(vertices)),
        in_specs=[VMEM],
        out_specs=[VMEM, VMEM],
        out_shape=[square, square],
        compiler_params=pltpu.CompilerParams(vmem_limit_bytes=8 << 20),
        name="factor",
    )(dense)


def finish_kernel(
    sub_ref, inverse_ref, own_ref, mine_ref, other_ref, ortho_hbm, coupling_hbm,
    ortho_ref, coupling_ref, sems, *, vertices,
):
    height, count, width = own_ref.shape
    first_sub = sub_ref[0] == 0
    half = mine_ref.shape[1]
    mine = mine_ref[0:count]
    other = other_ref[...]
    inverse = inverse_ref[...]

    def times(left, right):
        return jnp.dot(
            left, right, precision=lax.Precision.HIGHEST, preferred_element_type=jnp.float32
        )

    flat = jnp.concatenate([own_ref[r] for r in range(height)], axis=1)
    ortho = times(inverse, flat)
    stacked = jnp.stack([ortho[:, r * width : (r + 1) * width] for r in range(height)], axis=0)
    ortho_ref[...] = pltpu.einshape("rbc->brc", stacked)
    ortho_copy = pltpu.make_async_copy(ortho_ref, ortho_hbm, sems.at[0])
    ortho_copy.start()
    inverse = inverse * (1.0 / math.sqrt(vertices))
    coupling_ref[:, 0:half] = times(inverse, jnp.where(first_sub, mine, other))
    coupling_ref[:, half:] = times(inverse, jnp.where(first_sub, other, mine))
    coupling_copy = pltpu.make_async_copy(coupling_ref, coupling_hbm, sems.at[1])
    coupling_copy.start()
    ortho_copy.wait()
    coupling_copy.wait()


def finish(sub, inverse, own, mine, other, vertices):
    height, count, width = own.shape
    ortho = (count, height, width)
    coupling = (count, 2 * mine.shape[1])
    return pl.pallas_call(
        lambda *refs: finish_kernel(*refs, vertices=float(vertices)),
        in_specs=[SMEM, VMEM, VMEM, VMEM, VMEM],
        out_specs=[HBM, HBM],
        out_shape=[jax.ShapeDtypeStruct(s, jnp.float32) for s in (ortho, coupling)],
        scratch_shapes=[
            pltpu.VMEM(ortho, jnp.float32),
            pltpu.VMEM(coupling, jnp.float32),
            pltpu.SemaphoreType.DMA((2,)),
        ],
        compiler_params=pltpu.CompilerParams(vmem_limit_bytes=8 << 20),
        name="finish",
    )(sub, inverse, own, mine, other)


def swap(array, axis, distance):
    size = lax.axis_size(axis)
    return lax.ppermute(array, axis, [(i, i ^ distance) for i in range(size)])


def strip_sum(part):
    strips = lax.axis_size("strip")
    distance = 1
    while distance * 4 < strips or distance * 2 == strips:
        part = part + swap(part, "strip", distance)
        distance *= 2
    if distance * 4 == strips:
        one = swap(part, "strip", distance)
        two = swap(part, "strip", 2 * distance)
        three = swap(part, "strip", 3 * distance)
        part = (part + one) + (two + three)
    return part


def on_device(start_block, edge_weights, mass, locked):
    panels = lax.axis_size("panel")
    lines = lax.axis_size(GRID_ROWS)
    count, height, width = start_block.shape
    vertices = height * width * lines * panels
    panel = lax.axis_index("panel").astype(jnp.int32).reshape(1)
    sub = lax.axis_index("sub").astype(jnp.int32).reshape(1)

    body, near, far = pack(sub, start_block, edge_weights, mass)
    bodies = [body]
    for shift in range(1, panels):
        bodies.append(
            lax.ppermute(body, "panel", [((i + shift) % panels, i) for i in range(panels)])
        )
    locked_flat = relayout(locked)

    def far_moves(shift):
        moves = []
        for line in range(1, lines - 1, 2):
            for a, b in ((line, line + 1), (line + 1, line)):
                for p in range(panels):
                    q = (p - shift) % panels
                    moves.append((((a // 2) * panels + p) * 2 + a % 2, ((b // 2) * panels + q) * 2 + b % 2))
        return moves

    fars = [
        lax.ppermute(far, ("strip", "panel", "sub"), far_moves(shift)) for shift in range(panels)
    ]
    nears = [swap(near, "sub", 1)]
    first = (1 - sub[0]) * (height - HALO)
    for other in bodies[1:]:
        nears.append(swap(lax.dynamic_slice_in_dim(other, first, HALO, 0), "sub", 1))
    keep, send, own = filter_call(panel, sub, bodies, nears, fars, in_vmem(locked_flat))
    part = strip_sum(keep + swap(send, "sub", 1))
    other = swap(part[:count], "sub", 1)
    factor, inverse = factorize(part[count:, : count * count // 8], count, vertices)
    ortho, coupling = finish(sub, inverse, own, part, other, vertices)
    return (ortho, jnp.transpose(coupling), factor)


def solution(mesh):
    return jax.shard_map(
        on_device,
        mesh=mesh,
        in_specs=(
            P("groups", ("strip", "sub"), "panel"),
            P("groups", ("strip", "sub"), "panel"),
            P(("groups", "strip", "sub"), "panel"),
            P(("groups", "panel"), ("strip", "sub"), None),
        ),
        out_specs=(
            P("groups", ("strip", "sub"), "panel"),
            P(("groups", "panel"), None),
            P("groups", None),
        ),
        check_vma=False,
    )
```

```python
import math

import jax
import jax.numpy as jnp
from jax import lax
from jax.experimental import pallas as pl
from jax.experimental.pallas import tpu as pltpu
from jax.sharding import PartitionSpec as P

DEGREE = 6
CUT_LOW = 2
CUT_HIGH = 32
CENTRE = 0.5 * (CUT_HIGH + CUT_LOW)
SPREAD = 0.5 * (CUT_HIGH - CUT_LOW)
HALO = DEGREE
GRID_ROWS = ("strip", "sub")
SIDE = 8

VMEM = pl.BlockSpec(memory_space=pltpu.VMEM)
SMEM = pl.BlockSpec(memory_space=pltpu.SMEM)
HBM = pl.BlockSpec(memory_space=pltpu.HBM)


def pack_kernel(
    panel_ref, sub_ref, block_hbm, weights_hbm, mass_hbm, body_ref, near_ref, far_ref,
    block_ref, weights_ref, mass_ref, sems,
):
    copies = [
        pltpu.make_async_copy(block_hbm, block_ref, sems.at[0]),
        pltpu.make_async_copy(weights_hbm.at[0:4], weights_ref, sems.at[1]),
        pltpu.make_async_copy(mass_hbm, mass_ref, sems.at[2]),
    ]
    for copy in copies:
        copy.start()
    for copy in copies:
        copy.wait()
    count, height, width = block_ref.shape
    body_ref[:, 0:count, :] = pltpu.einshape("brc->rbc", block_ref[...])
    mass = mass_ref[...][None]
    side = jnp.concatenate([weights_ref[...], mass, mass, mass, mass], axis=0)
    body_ref[:, count : count + SIDE, :] = pltpu.einshape("brc->rbc", side)
    sub = sub_ref[0]
    near_ref[...] = body_ref[pl.ds((1 - sub) * (height - HALO), HALO)]
    far_ref[...] = body_ref[pl.ds(sub * (height - HALO), HALO)]


def pack(panel, sub, start_block, edge_weights, mass):
    count, height, width = start_block.shape
    halo = jax.ShapeDtypeStruct((HALO, count + SIDE, width), jnp.float32)
    return pl.pallas_call(
        pack_kernel,
        in_specs=[SMEM, SMEM, HBM, HBM, HBM],
        out_specs=[VMEM, VMEM, VMEM],
        out_shape=[jax.ShapeDtypeStruct((height, count + SIDE, width), jnp.float32), halo, halo],
        scratch_shapes=[
            pltpu.VMEM((count, height, width), jnp.float32),
            pltpu.VMEM((4, height, width), jnp.float32),
            pltpu.VMEM((height, width), jnp.float32),
            pltpu.SemaphoreType.DMA((3,)),
        ],
        compiler_params=pltpu.CompilerParams(vmem_limit_bytes=8 << 20),
        name="pack",
    )(panel, sub, *[in_hbm(x) for x in (start_block, edge_weights, mass)])


def in_hbm(array):
    return pltpu.with_memory_space_constraint(array, pltpu.HBM)


def in_vmem(array):
    return pltpu.with_memory_space_constraint(array, pltpu.VMEM)


def relayout_kernel(locked_hbm, flat_ref, chunks_ref, sems):
    chunks, size, height, width = chunks_ref.shape
    copies = [
        pltpu.make_async_copy(locked_hbm.at[pl.ds(i * size, size)], chunks_ref.at[i], sems.at[i])
        for i in range(chunks)
    ]
    for copy in copies:
        copy.start()
    for i in range(chunks):
        copies[i].wait()
        rows = pltpu.einshape("krc->rkc", chunks_ref[i])
        for r in range(height):
            flat_ref[pl.ds(i * size, size), r * width : (r + 1) * width] = rows[r]


def relayout(locked):
    basis, height, width = locked.shape
    chunks = max(1, basis // 64)
    return pl.pallas_call(
        relayout_kernel,
        in_specs=[HBM],
        out_specs=VMEM,
        out_shape=pltpu.VMEM((basis, height * width), locked.dtype),
        scratch_shapes=[
            pltpu.VMEM((chunks, basis // chunks, height, width), locked.dtype),
            pltpu.SemaphoreType.DMA((chunks,)),
        ],
        compiler_params=pltpu.CompilerParams(vmem_limit_bytes=12 << 20),
        name="relayout",
    )(in_hbm(locked))


def near_kernel(sub_ref, body_ref, ahead_ref, near_ref):
    height = body_ref.shape[0]
    near_ref[...] = body_ref[pl.ds((1 - sub_ref[0]) * (height - HALO), HALO)]


def near_rows(sub, body, ahead):
    return pl.pallas_call(
        near_kernel,
        in_specs=[SMEM, VMEM, VMEM],
        out_specs=VMEM,
        out_shape=jax.ShapeDtypeStruct((HALO,) + body.shape[1:], body.dtype),
        compiler_params=pltpu.CompilerParams(vmem_limit_bytes=2 << 20),
        name="near_rows",
    )(sub, body, ahead)


def filter_kernel(panel_ref, sub_ref, *refs, panels, height, count, width):
    bodies = refs[0:panels]
    nears = refs[panels : 2 * panels]
    fars = refs[2 * panels : 3 * panels]
    locked_ref, keep_ref, send_ref, own_ref, y_even, y_odd, split = refs[3 * panels :]
    total = panels * width
    rows = height + 2 * HALO
    panel = panel_ref[0]
    first_sub = sub_ref[0] == 0

    def source(row):
        if HALO <= row < HALO + height:
            parts = [b[row - HALO] for b in bodies]
        elif row < HALO:
            parts = [jnp.where(first_sub, f[row], n[row]) for n, f in zip(nears, fars)]
        else:
            at = row - HALO - height
            parts = [jnp.where(first_sub, n[at], f[at]) for n, f in zip(nears, fars)]
        return jnp.concatenate(parts, axis=1)

    lane = lax.broadcasted_iota(jnp.int32, (1, total), 1)
    column = lax.rem(lane + panel * width, total)
    not_last = (column != total - 1).astype(jnp.float32)
    not_first = (column != 0).astype(jnp.float32)

    factor = 2.0 / SPREAD

    def left(x):
        return pltpu.roll(x, total - 1, 1)

    def right(x):
        return pltpu.roll(x, 1, 1)

    weights = []
    scale = []
    for row in range(rows):
        full = source(row)
        y_even[row] = full[0:count]
        side = full[count : count + SIDE]
        mass = side[4:5]
        inside = mass > 0.0
        scale.append(jnp.where(inside, 1.0 / jnp.sqrt(jnp.where(inside, mass, 1.0)), 0.0))
        weights.append([side[d : d + 1] for d in range(4)])
    edges = []
    for row in range(rows - 1):
        s0 = scale[row]
        s1 = scale[row + 1]
        w = weights[row]
        e0 = -factor * (w[0] * (s0 * left(s0))) * not_last
        e1 = -factor * (w[1] * (s0 * s1))
        e2 = -factor * (w[2] * (s0 * left(s1))) * not_last
        e3 = -factor * (w[3] * (s0 * right(s1))) * not_first
        edges.append((e0, e1, e2, e3))
    coefficients = [None]
    for row in range(1, rows - 1):
        w = weights[row]
        v = weights[row - 1]
        total_weight = (
            ((w[0] + w[1]) + (w[2] + w[3]))
            + (right(w[0] * not_last) + v[1])
            + (right(v[2] * not_last) + left(v[3] * not_first))
        )
        diagonal = factor * (scale[row] * scale[row] * total_weight - CENTRE)
        e0, e1, e2, e3 = edges[row]
        u0, u1, u2, u3 = edges[row - 1]
        coefficients.append((diagonal, e1, u1, right(e0), right(e2), u3, e0, left(e3), u2))

    buffers = (y_even, y_odd)
    for order in range(1, DEGREE + 1):
        source_ref = buffers[(order - 1) % 2]
        target_ref = buffers[order % 2]
        for row in range(order, rows - order):
            c = coefficients[row]
            ym = source_ref[row - 1]
            y0 = source_ref[row]
            yp = source_ref[row + 1]
            out = c[0] * y0 + (c[1] * yp + c[2] * ym)
            to_left = c[3] * y0 + (c[4] * yp + c[5] * ym)
            to_right = c[6] * y0 + (c[7] * yp + c[8] * ym)
            out = out + (left(to_left) + right(to_right))
            if order == 1:
                out = 0.5 * out
            else:
                out = out - target_ref[row]
            target_ref[row] = out
    result = buffers[DEGREE % 2]

    for row in range(height):
        full = result[row + HALO]
        own_ref[row] = full[:, 0:width]
        high = full.astype(jnp.bfloat16)
        rest = full - high.astype(jnp.float32)
        middle = rest.astype(jnp.bfloat16)
        low = (rest - middle.astype(jnp.float32)).astype(jnp.bfloat16)
        stacked = jnp.concatenate([high, middle, low], axis=0)
        for t in range(panels):
            at = row * total + lax.rem(panel + t, panels) * width
            split[:, pl.ds(pl.multiple_of(at, width), width)] = stacked[:, t * width : (t + 1) * width]

    dims = (((1,), (1,)), ((), ()))
    pieces = split[...]
    gram = lax.dot_general(pieces, pieces, dims, preferred_element_type=jnp.float32)
    gram = gram[0:count] + gram[count : 2 * count] + gram[2 * count : 3 * count]
    gram = gram[:, 0:count] + gram[:, count : 2 * count] + gram[:, 2 * count : 3 * count]
    products = lax.dot_general(pieces, locked_ref[...], dims, preferred_element_type=jnp.float32)
    products = products[0:count] + products[count : 2 * count] + products[2 * count : 3 * count]
    half = products.shape[1] // 2
    lower = products[:, 0:half]
    upper = products[:, half:]
    keep_ref[0:count] = jnp.where(first_sub, lower, upper)
    send_ref[0:count] = jnp.where(first_sub, upper, lower)
    dense = fold(gram, half)
    keep_ref[count : count + 8] = dense
    send_ref[count : count + 8] = dense


def fold(gram, width):
    count = gram.shape[0]
    parts = [gram[r : r + 8] for r in range(0, count, 8)]
    spare = width - count * len(parts)
    if spare > 0:
        parts.append(jnp.zeros((8, spare), jnp.float32))
    return jnp.concatenate(parts, axis=1)


def filter_call(panel, sub, bodies, nears, fars, locked_flat):
    panels = len(bodies)
    height, planes, width = bodies[0].shape
    count = planes - SIDE
    basis = locked_flat.shape[0]
    total = panels * width
    rows = height + 2 * HALO
    payload = jax.ShapeDtypeStruct((count + 8, basis // 2), jnp.float32)
    return pl.pallas_call(
        lambda *refs: filter_kernel(*refs, panels=panels, height=height, count=count, width=width),
        in_specs=[SMEM, SMEM] + [VMEM] * (3 * panels + 1),
        out_specs=[VMEM] * 3,
        out_shape=[payload, payload, jax.ShapeDtypeStruct((height, count, width), jnp.float32)],
        scratch_shapes=[
            pltpu.VMEM((rows, count, total), jnp.float32),
            pltpu.VMEM((rows, count, total), jnp.float32),
            pltpu.VMEM((3 * count, height * total), jnp.bfloat16),
        ],
        compiler_params=pltpu.CompilerParams(vmem_limit_bytes=20 << 20),
        name="filter",
    )(panel, sub, *bodies, *nears, *fars, locked_flat)


def factor_kernel(gram_ref, factor_ref, inverse_ref, *, vertices):
    count = factor_ref.shape[0]
    tiles = count // 8
    dense = gram_ref[...]
    row = lax.broadcasted_iota(jnp.int32, (8, 128), 0)
    col = lax.broadcasted_iota(jnp.int32, (8, 128), 1)
    blank = jnp.zeros((8, 128 - count), jnp.float32)

    def fill(x):
        return jnp.broadcast_to(x, (8, 128))

    work = []
    for t in range(tiles):
        gram = jnp.concatenate([dense[:, t * count : (t + 1) * count], blank], axis=1)
        at = row + 8 * t
        gram = gram * (1.0 / vertices) + jnp.where(at == col, 1e-06, 0.0)
        work.append(gram + jnp.where(at + count == col, 1.0, 0.0))
    for b in range(tiles):
        columns = {
            (t, k): fill(work[t][:, 8 * b + k : 8 * b + k + 1])
            for t in range(b, tiles)
            for k in range(8)
        }
        pivots = jnp.ones((8, 128), jnp.float32)
        for j in range(8):
            pivot = fill(columns[b, j][j : j + 1])
            pivots = jnp.where(row == j, pivot, pivots)
            inverse = 1.0 / pivot
            pivot_row = fill(work[b][j : j + 1])
            entries = {k: fill(columns[b, k][j : j + 1]) for k in range(j + 1, 8)}
            for t in range(b, tiles):
                multiplier = columns[t, j] * inverse
                if t == b:
                    multiplier = jnp.where(row > j, multiplier, 0.0)
                for k in range(j + 1, 8):
                    columns[t, k] = columns[t, k] - multiplier * entries[k]
                work[t] = work[t] - multiplier * pivot_row
        work[b] = work[b] * (1.0 / jnp.sqrt(pivots))
    for t in range(tiles):
        upper = jnp.where(row + 8 * t <= col, work[t], 0.0)
        factor_ref[8 * t : 8 * t + 8, :] = upper[:, 0:count]
        inverse_ref[8 * t : 8 * t + 8, :] = work[t][:, count : 2 * count]


def factorize(dense, count, vertices):
    square = jax.ShapeDtypeStruct((count, count), jnp.float32)
    return pl.pallas_call(
        lambda *refs: factor_kernel(*refs, vertices=float(vertices)),
        in_specs=[VMEM],
        out_specs=[VMEM, VMEM],
        out_shape=[square, square],
        compiler_params=pltpu.CompilerParams(vmem_limit_bytes=8 << 20),
        name="factor",
    )(dense)


def finish_kernel(
    sub_ref, inverse_ref, own_ref, mine_ref, other_ref, ortho_hbm, coupling_hbm,
    ortho_ref, coupling_ref, sems, *, vertices,
):
    height, count, width = own_ref.shape
    first_sub = sub_ref[0] == 0
    half = mine_ref.shape[1]
    mine = mine_ref[0:count]
    other = other_ref[...]
    inverse = inverse_ref[...]

    def times(left, right):
        return jnp.dot(
            left, right, precision=lax.Precision.HIGHEST, preferred_element_type=jnp.float32
        )

    flat = jnp.concatenate([own_ref[r] for r in range(height)], axis=1)
    ortho = times(inverse, flat)
    stacked = jnp.stack([ortho[:, r * width : (r + 1) * width] for r in range(height)], axis=0)
    ortho_ref[...] = pltpu.einshape("rbc->brc", stacked)
    ortho_copy = pltpu.make_async_copy(ortho_ref, ortho_hbm, sems.at[0])
    ortho_copy.start()
    inverse = inverse * (1.0 / math.sqrt(vertices))
    coupling_ref[:, 0:half] = times(inverse, jnp.where(first_sub, mine, other))
    coupling_ref[:, half:] = times(inverse, jnp.where(first_sub, other, mine))
    coupling_copy = pltpu.make_async_copy(coupling_ref, coupling_hbm, sems.at[1])
    coupling_copy.start()
    ortho_copy.wait()
    coupling_copy.wait()


def finish(sub, inverse, own, mine, other, vertices):
    height, count, width = own.shape
    ortho = (count, height, width)
    coupling = (count, 2 * mine.shape[1])
    return pl.pallas_call(
        lambda *refs: finish_kernel(*refs, vertices=float(vertices)),
        in_specs=[SMEM, VMEM, VMEM, VMEM, VMEM],
        out_specs=[HBM, HBM],
        out_shape=[jax.ShapeDtypeStruct(s, jnp.float32) for s in (ortho, coupling)],
        scratch_shapes=[
            pltpu.VMEM(ortho, jnp.float32),
            pltpu.VMEM(coupling, jnp.float32),
            pltpu.SemaphoreType.DMA((2,)),
        ],
        compiler_params=pltpu.CompilerParams(vmem_limit_bytes=8 << 20),
        name="finish",
    )(sub, inverse, own, mine, other)


def swap(array, axis, distance):
    size = lax.axis_size(axis)
    return lax.ppermute(array, axis, [(i, i ^ distance) for i in range(size)])


def strip_sum(part):
    strips = lax.axis_size("strip")
    distance = 1
    while distance * 4 < strips or distance * 2 == strips:
        part = part + swap(part, "strip", distance)
        distance *= 2
    if distance * 4 == strips:
        one = swap(part, "strip", distance)
        two = swap(part, "strip", 2 * distance)
        three = swap(part, "strip", 3 * distance)
        part = (part + one) + (two + three)
    return part


def on_device(start_block, edge_weights, mass, locked):
    panels = lax.axis_size("panel")
    lines = lax.axis_size(GRID_ROWS)
    count, height, width = start_block.shape
    vertices = height * width * lines * panels
    panel = lax.axis_index("panel").astype(jnp.int32).reshape(1)
    sub = lax.axis_index("sub").astype(jnp.int32).reshape(1)

    body, near, far = pack(panel, sub, start_block, edge_weights, mass)
    bodies = [body]
    for shift in range(1, panels):
        bodies.append(
            lax.ppermute(body, "panel", [((i + shift) % panels, i) for i in range(panels)])
        )
    locked_flat = relayout(locked)

    def far_moves(shift):
        moves = []
        for line in range(1, lines - 1, 2):
            for a, b in ((line, line + 1), (line + 1, line)):
                for p in range(panels):
                    q = (p - shift) % panels
                    moves.append((((a // 2) * panels + p) * 2 + a % 2, ((b // 2) * panels + q) * 2 + b % 2))
        return moves

    fars = [
        lax.ppermute(far, ("strip", "panel", "sub"), far_moves(shift)) for shift in range(panels)
    ]
    nears = [swap(near, "sub", 1)]
    locked_flat = in_vmem(locked_flat)
    for other in bodies[1:]:
        nears.append(swap(near_rows(sub, other, locked_flat), "sub", 1))
    keep, send, own = filter_call(panel, sub, bodies, nears, fars, locked_flat)
    part = strip_sum(keep + swap(send, "sub", 1))
    other = swap(part[:count], "sub", 1)
    factor, inverse = factorize(part[count:, : count * count // 8], count, vertices)
    ortho, coupling = finish(sub, inverse, own, part, other, vertices)
    return (ortho, jnp.transpose(coupling), factor)


def solution(mesh):
    return jax.shard_map(
        on_device,
        mesh=mesh,
        in_specs=(
            P("groups", ("strip", "sub"), "panel"),
            P("groups", ("strip", "sub"), "panel"),
            P(("groups", "strip", "sub"), "panel"),
            P(("groups", "panel"), ("strip", "sub"), None),
        ),
        out_specs=(
            P("groups", ("strip", "sub"), "panel"),
            P(("groups", "panel"), None),
            P("groups", None),
        ),
        check_vma=False,
    )
```

```python
import math

import jax
import jax.numpy as jnp
from jax import lax
from jax.experimental import pallas as pl
from jax.experimental.pallas import tpu as pltpu
from jax.sharding import PartitionSpec as P

DEGREE = 6
CUT_LOW = 2
CUT_HIGH = 32
CENTRE = 0.5 * (CUT_HIGH + CUT_LOW)
SPREAD = 0.5 * (CUT_HIGH - CUT_LOW)
HALO = DEGREE
GRID_ROWS = ("strip", "sub")
SIDE = 5

VMEM = pl.BlockSpec(memory_space=pltpu.VMEM)
SMEM = pl.BlockSpec(memory_space=pltpu.SMEM)
HBM = pl.BlockSpec(memory_space=pltpu.HBM)


def pack_kernel(
    panel_ref, sub_ref, block_hbm, weights_hbm, mass_hbm, body_ref,
    block_ref, weights_ref, mass_ref, sems,
):
    copies = [
        pltpu.make_async_copy(block_hbm, block_ref, sems.at[0]),
        pltpu.make_async_copy(weights_hbm.at[0:4], weights_ref, sems.at[1]),
        pltpu.make_async_copy(mass_hbm, mass_ref, sems.at[2]),
    ]
    for copy in copies:
        copy.start()
    for copy in copies:
        copy.wait()
    count, height, width = block_ref.shape
    body_ref[0 : height * count] = pltpu.einshape("brc->rbc", block_ref[...]).reshape(-1, width)
    for d in range(SIDE - 1):
        at = height * (count + d)
        body_ref[at : at + height] = weights_ref[d]
    body_ref[height * (count + SIDE - 1) :] = mass_ref[...]


def pack(panel, sub, start_block, edge_weights, mass):
    count, height, width = start_block.shape
    return pl.pallas_call(
        pack_kernel,
        in_specs=[SMEM, SMEM, HBM, HBM, HBM],
        out_specs=VMEM,
        out_shape=jax.ShapeDtypeStruct((height * (count + SIDE), width), jnp.float32),
        scratch_shapes=[
            pltpu.VMEM((count, height, width), jnp.float32),
            pltpu.VMEM((4, height, width), jnp.float32),
            pltpu.VMEM((height, width), jnp.float32),
            pltpu.SemaphoreType.DMA((3,)),
        ],
        compiler_params=pltpu.CompilerParams(vmem_limit_bytes=8 << 20),
        name="pack",
    )(panel, sub, *[in_hbm(x) for x in (start_block, edge_weights, mass)])


def in_hbm(array):
    return pltpu.with_memory_space_constraint(array, pltpu.HBM)


def in_vmem(array):
    return pltpu.with_memory_space_constraint(array, pltpu.VMEM)


def relayout_kernel(locked_hbm, flat_ref, chunks_ref, sems):
    chunks, size, height, width = chunks_ref.shape
    copies = [
        pltpu.make_async_copy(locked_hbm.at[pl.ds(i * size, size)], chunks_ref.at[i], sems.at[i])
        for i in range(chunks)
    ]
    for copy in copies:
        copy.start()
    for i in range(chunks):
        copies[i].wait()
        rows = pltpu.einshape("krc->rkc", chunks_ref[i])
        for r in range(height):
            flat_ref[pl.ds(i * size, size), r * width : (r + 1) * width] = rows[r]


def relayout(locked):
    basis, height, width = locked.shape
    chunks = max(1, basis // 64)
    return pl.pallas_call(
        relayout_kernel,
        in_specs=[HBM],
        out_specs=VMEM,
        out_shape=pltpu.VMEM((basis, height * width), locked.dtype),
        scratch_shapes=[
            pltpu.VMEM((chunks, basis // chunks, height, width), locked.dtype),
            pltpu.SemaphoreType.DMA((chunks,)),
        ],
        compiler_params=pltpu.CompilerParams(vmem_limit_bytes=12 << 20),
        name="relayout",
    )(in_hbm(locked))


def edge_kernel(sub_ref, body_ref, *refs, height, count, sides):
    sub = sub_ref[0]
    out_refs = refs[-sides:]
    for out_ref, at in zip(out_refs, (1 - sub, sub)):
        start = pl.multiple_of(at * ((height - HALO) * count), 8)
        out_ref[0 : HALO * count] = body_ref[pl.ds(start, HALO * count)]
        for d in range(SIDE):
            start = pl.multiple_of(height * (count + d) + at * (height - 8), 8)
            to = HALO * count + 8 * d
            out_ref[to : to + 8] = body_ref[pl.ds(start, 8)]


def edge_rows(sub, body, ahead, sides, height):
    count = body.shape[0] // height - SIDE
    rows = jax.ShapeDtypeStruct((HALO * count + 8 * SIDE, body.shape[1]), body.dtype)
    return pl.pallas_call(
        lambda *refs: edge_kernel(*refs, height=height, count=count, sides=sides),
        in_specs=[SMEM] + [VMEM] * (1 + len(ahead)),
        out_specs=[VMEM] * sides,
        out_shape=[rows] * sides,
        compiler_params=pltpu.CompilerParams(vmem_limit_bytes=2 << 20),
        name="edge_rows",
    )(sub, body, *ahead)


def filter_kernel(panel_ref, sub_ref, *refs, panels, height, count, width):
    bodies = refs[0:panels]
    nears = refs[panels : 2 * panels]
    fars = refs[2 * panels : 3 * panels]
    locked_ref, keep_ref, send_ref, own_ref, y_even, y_odd, split = refs[3 * panels :]
    total = panels * width
    rows = height + 2 * HALO
    panel = panel_ref[0]
    first_sub = sub_ref[0] == 0

    def fetch(row, own, above, below, size):
        if HALO <= row < HALO + height:
            parts = [b[own : own + size] for b in bodies]
        elif row < HALO:
            at = slice(above, above + size)
            parts = [jnp.where(first_sub, f[at], n[at]) for n, f in zip(nears, fars)]
        else:
            at = slice(below, below + size)
            parts = [jnp.where(first_sub, n[at], f[at]) for n, f in zip(nears, fars)]
        return jnp.concatenate(parts, axis=1)

    def vectors(row):
        return fetch(
            row, (row - HALO) * count, row * count, (row - HALO - height) * count, count
        )

    def side(row, d):
        base = HALO * count + 8 * d
        return fetch(
            row,
            height * (count + d) + row - HALO,
            base + row + 8 - HALO,
            base + row - HALO - height,
            1,
        )

    lane = lax.broadcasted_iota(jnp.int32, (1, total), 1)
    column = lax.rem(lane + panel * width, total)
    not_last = (column != total - 1).astype(jnp.float32)
    not_first = (column != 0).astype(jnp.float32)

    factor = 2.0 / SPREAD

    def left(x):
        return pltpu.roll(x, total - 1, 1)

    def right(x):
        return pltpu.roll(x, 1, 1)

    weights = []
    scale = []
    for row in range(rows):
        y_even[row] = vectors(row)
        mass = side(row, SIDE - 1)
        inside = mass > 0.0
        scale.append(jnp.where(inside, 1.0 / jnp.sqrt(jnp.where(inside, mass, 1.0)), 0.0))
        weights.append([side(row, d) for d in range(SIDE - 1)])
    edges = []
    for row in range(rows - 1):
        s0 = scale[row]
        s1 = scale[row + 1]
        w = weights[row]
        e0 = -factor * (w[0] * (s0 * left(s0))) * not_last
        e1 = -factor * (w[1] * (s0 * s1))
        e2 = -factor * (w[2] * (s0 * left(s1))) * not_last
        e3 = -factor * (w[3] * (s0 * right(s1))) * not_first
        edges.append((e0, e1, e2, e3))
    coefficients = [None]
    for row in range(1, rows - 1):
        w = weights[row]
        v = weights[row - 1]
        total_weight = (
            ((w[0] + w[1]) + (w[2] + w[3]))
            + (right(w[0] * not_last) + v[1])
            + (right(v[2] * not_last) + left(v[3] * not_first))
        )
        diagonal = factor * (scale[row] * scale[row] * total_weight - CENTRE)
        e0, e1, e2, e3 = edges[row]
        u0, u1, u2, u3 = edges[row - 1]
        coefficients.append((diagonal, e1, u1, right(e0), right(e2), u3, e0, left(e3), u2))

    buffers = (y_even, y_odd)
    for order in range(1, DEGREE + 1):
        source_ref = buffers[(order - 1) % 2]
        target_ref = buffers[order % 2]
        for row in range(order, rows - order):
            c = coefficients[row]
            ym = source_ref[row - 1]
            y0 = source_ref[row]
            yp = source_ref[row + 1]
            out = c[0] * y0 + (c[1] * yp + c[2] * ym)
            to_left = c[3] * y0 + (c[4] * yp + c[5] * ym)
            to_right = c[6] * y0 + (c[7] * yp + c[8] * ym)
            out = out + (left(to_left) + right(to_right))
            if order == 1:
                out = 0.5 * out
            else:
                out = out - target_ref[row]
            target_ref[row] = out
    result = buffers[DEGREE % 2]

    for row in range(height):
        full = result[row + HALO]
        own_ref[row] = full[:, 0:width]
        high = full.astype(jnp.bfloat16)
        rest = full - high.astype(jnp.float32)
        middle = rest.astype(jnp.bfloat16)
        low = (rest - middle.astype(jnp.float32)).astype(jnp.bfloat16)
        stacked = jnp.concatenate([high, middle, low], axis=0)
        for t in range(panels):
            at = row * total + lax.rem(panel + t, panels) * width
            split[:, pl.ds(pl.multiple_of(at, width), width)] = stacked[:, t * width : (t + 1) * width]

    dims = (((1,), (1,)), ((), ()))
    pieces = split[...]
    gram = lax.dot_general(pieces, pieces, dims, preferred_element_type=jnp.float32)
    gram = gram[0:count] + gram[count : 2 * count] + gram[2 * count : 3 * count]
    gram = gram[:, 0:count] + gram[:, count : 2 * count] + gram[:, 2 * count : 3 * count]
    products = lax.dot_general(pieces, locked_ref[...], dims, preferred_element_type=jnp.float32)
    products = products[0:count] + products[count : 2 * count] + products[2 * count : 3 * count]
    half = products.shape[1] // 2
    lower = products[:, 0:half]
    upper = products[:, half:]
    keep = jnp.where(first_sub, lower, upper)
    send = jnp.where(first_sub, upper, lower)
    for at in range(0, half, 128):
        to = count * (at // 128)
        keep_ref[to : to + count] = keep[:, at : at + 128]
        send_ref[to : to + count] = send[:, at : at + 128]
    to = count * (half // 128)
    dense = fold(gram, 128)
    keep_ref[to : to + 8] = dense
    send_ref[to : to + 8] = dense


def fold(gram, width):
    count = gram.shape[0]
    parts = [gram[r : r + 8] for r in range(0, count, 8)]
    spare = width - count * len(parts)
    if spare > 0:
        parts.append(jnp.zeros((8, spare), jnp.float32))
    return jnp.concatenate(parts, axis=1)


def filter_call(panel, sub, bodies, nears, fars, locked_flat, height):
    panels = len(bodies)
    width = bodies[0].shape[1]
    count = bodies[0].shape[0] // height - SIDE
    basis = locked_flat.shape[0]
    total = panels * width
    rows = height + 2 * HALO
    payload = jax.ShapeDtypeStruct((count * (basis // 256) + 8, 128), jnp.float32)
    return pl.pallas_call(
        lambda *refs: filter_kernel(*refs, panels=panels, height=height, count=count, width=width),
        in_specs=[SMEM, SMEM] + [VMEM] * (3 * panels + 1),
        out_specs=[VMEM] * 3,
        out_shape=[payload, payload, jax.ShapeDtypeStruct((height, count, width), jnp.float32)],
        scratch_shapes=[
            pltpu.VMEM((rows, count, total), jnp.float32),
            pltpu.VMEM((rows, count, total), jnp.float32),
            pltpu.VMEM((3 * count, height * total), jnp.bfloat16),
        ],
        compiler_params=pltpu.CompilerParams(vmem_limit_bytes=20 << 20),
        name="filter",
    )(panel, sub, *bodies, *nears, *fars, locked_flat)


def factor_kernel(gram_ref, factor_ref, inverse_ref, *, vertices):
    count = factor_ref.shape[0]
    tiles = count // 8
    dense = gram_ref[...]
    row = lax.broadcasted_iota(jnp.int32, (8, 128), 0)
    col = lax.broadcasted_iota(jnp.int32, (8, 128), 1)
    blank = jnp.zeros((8, 128 - count), jnp.float32)

    def fill(x):
        return jnp.broadcast_to(x, (8, 128))

    work = []
    for t in range(tiles):
        gram = jnp.concatenate([dense[:, t * count : (t + 1) * count], blank], axis=1)
        at = row + 8 * t
        gram = gram * (1.0 / vertices) + jnp.where(at == col, 1e-06, 0.0)
        work.append(gram + jnp.where(at + count == col, 1.0, 0.0))
    for b in range(tiles):
        columns = {
            (t, k): fill(work[t][:, 8 * b + k : 8 * b + k + 1])
            for t in range(b, tiles)
            for k in range(8)
        }
        pivots = jnp.ones((8, 128), jnp.float32)
        for j in range(8):
            pivot = fill(columns[b, j][j : j + 1])
            pivots = jnp.where(row == j, pivot, pivots)
            inverse = 1.0 / pivot
            pivot_row = fill(work[b][j : j + 1])
            entries = {k: fill(columns[b, k][j : j + 1]) for k in range(j + 1, 8)}
            for t in range(b, tiles):
                multiplier = columns[t, j] * inverse
                if t == b:
                    multiplier = jnp.where(row > j, multiplier, 0.0)
                for k in range(j + 1, 8):
                    columns[t, k] = columns[t, k] - multiplier * entries[k]
                work[t] = work[t] - multiplier * pivot_row
        work[b] = work[b] * (1.0 / jnp.sqrt(pivots))
    for t in range(tiles):
        upper = jnp.where(row + 8 * t <= col, work[t], 0.0)
        factor_ref[8 * t : 8 * t + 8, :] = upper[:, 0:count]
        inverse_ref[8 * t : 8 * t + 8, :] = work[t][:, count : 2 * count]


def factorize(dense, count, vertices):
    square = jax.ShapeDtypeStruct((count, count), jnp.float32)
    return pl.pallas_call(
        lambda *refs: factor_kernel(*refs, vertices=float(vertices)),
        in_specs=[VMEM],
        out_specs=[VMEM, VMEM],
        out_shape=[square, square],
        compiler_params=pltpu.CompilerParams(vmem_limit_bytes=8 << 20),
        name="factor",
    )(dense)


def finish_kernel(
    sub_ref, inverse_ref, own_ref, mine_ref, other_ref, ortho_hbm, coupling_hbm,
    ortho_ref, coupling_ref, sems, *, vertices,
):
    height, count, width = own_ref.shape
    first_sub = sub_ref[0] == 0
    blocks = other_ref.shape[0] // count
    inverse = inverse_ref[...]

    def times(left, right):
        return jnp.dot(
            left, right, precision=lax.Precision.HIGHEST, preferred_element_type=jnp.float32
        )

    flat = jnp.concatenate([own_ref[r] for r in range(height)], axis=1)
    ortho = times(inverse, flat)
    stacked = jnp.stack([ortho[:, r * width : (r + 1) * width] for r in range(height)], axis=0)
    ortho_ref[...] = pltpu.einshape("rbc->brc", stacked)
    ortho_copy = pltpu.make_async_copy(ortho_ref, ortho_hbm, sems.at[0])
    ortho_copy.start()
    inverse = inverse * (1.0 / math.sqrt(vertices))
    for i in range(blocks):
        mine = mine_ref[i * count : (i + 1) * count]
        other = other_ref[i * count : (i + 1) * count]
        for at, part in (
            (i, jnp.where(first_sub, mine, other)),
            (blocks + i, jnp.where(first_sub, other, mine)),
        ):
            coupling_ref[:, at * 128 : (at + 1) * 128] = times(inverse, part)
    coupling_copy = pltpu.make_async_copy(coupling_ref, coupling_hbm, sems.at[1])
    coupling_copy.start()
    ortho_copy.wait()
    coupling_copy.wait()


def finish(sub, inverse, own, mine, other, vertices):
    height, count, width = own.shape
    ortho = (count, height, width)
    coupling = (count, 256 * (other.shape[0] // count))
    return pl.pallas_call(
        lambda *refs: finish_kernel(*refs, vertices=float(vertices)),
        in_specs=[SMEM, VMEM, VMEM, VMEM, VMEM],
        out_specs=[HBM, HBM],
        out_shape=[jax.ShapeDtypeStruct(s, jnp.float32) for s in (ortho, coupling)],
        scratch_shapes=[
            pltpu.VMEM(ortho, jnp.float32),
            pltpu.VMEM(coupling, jnp.float32),
            pltpu.SemaphoreType.DMA((2,)),
        ],
        compiler_params=pltpu.CompilerParams(vmem_limit_bytes=8 << 20),
        name="finish",
    )(sub, inverse, own, mine, other)


def swap(array, axis, distance):
    size = lax.axis_size(axis)
    return lax.ppermute(array, axis, [(i, i ^ distance) for i in range(size)])


def strip_sum(part):
    strips = lax.axis_size("strip")
    distance = 1
    while distance * 4 < strips or distance * 2 == strips:
        part = part + swap(part, "strip", distance)
        distance *= 2
    if distance * 4 == strips:
        one = swap(part, "strip", distance)
        two = swap(part, "strip", 2 * distance)
        three = swap(part, "strip", 3 * distance)
        part = (part + one) + (two + three)
    return part


def on_device(start_block, edge_weights, mass, locked):
    panels = lax.axis_size("panel")
    lines = lax.axis_size(GRID_ROWS)
    count, height, width = start_block.shape
    vertices = height * width * lines * panels
    panel = lax.axis_index("panel").astype(jnp.int32).reshape(1)
    sub = lax.axis_index("sub").astype(jnp.int32).reshape(1)

    body = pack(panel, sub, start_block, edge_weights, mass)
    bodies = [body]
    for shift in range(1, panels):
        bodies.append(
            lax.ppermute(body, "panel", [((i + shift) % panels, i) for i in range(panels)])
        )
    locked_flat = in_vmem(relayout(locked))
    near, far = edge_rows(sub, body, [], 2, height)

    def far_moves(shift):
        moves = []
        for line in range(1, lines - 1, 2):
            for a, b in ((line, line + 1), (line + 1, line)):
                for p in range(panels):
                    q = (p - shift) % panels
                    moves.append((((a // 2) * panels + p) * 2 + a % 2, ((b // 2) * panels + q) * 2 + b % 2))
        return moves

    fars = [
        lax.ppermute(far, ("strip", "panel", "sub"), far_moves(shift)) for shift in range(panels)
    ]
    nears = [swap(near, "sub", 1)]
    for other in bodies[1:]:
        nears.append(swap(edge_rows(sub, other, [locked_flat], 1, height)[0], "sub", 1))
    keep, send, own = filter_call(panel, sub, bodies, nears, fars, locked_flat, height)
    part = strip_sum(keep + swap(send, "sub", 1))
    grams = part.shape[0] - 8
    other = swap(part[:grams], "sub", 1)
    factor, inverse = factorize(part[grams:, : count * count // 8], count, vertices)
    ortho, coupling = finish(sub, inverse, own, part, other, vertices)
    return (ortho, jnp.transpose(coupling), factor)


def solution(mesh):
    return jax.shard_map(
        on_device,
        mesh=mesh,
        in_specs=(
            P("groups", ("strip", "sub"), "panel"),
            P("groups", ("strip", "sub"), "panel"),
            P(("groups", "strip", "sub"), "panel"),
            P(("groups", "panel"), ("strip", "sub"), None),
        ),
        out_specs=(
            P("groups", ("strip", "sub"), "panel"),
            P(("groups", "panel"), None),
            P("groups", None),
        ),
        check_vma=False,
    )
```

```python
import math

import jax
import jax.numpy as jnp
from jax import lax
from jax.experimental import pallas as pl
from jax.experimental.pallas import tpu as pltpu
from jax.sharding import PartitionSpec as P

DEGREE = 6
CUT_LOW = 2
CUT_HIGH = 32
CENTRE = 0.5 * (CUT_HIGH + CUT_LOW)
SPREAD = 0.5 * (CUT_HIGH - CUT_LOW)
HALO = DEGREE
GRID_ROWS = ("strip", "sub")
SIDE = 5
CHUNK = 2

VMEM = pl.BlockSpec(memory_space=pltpu.VMEM)
SMEM = pl.BlockSpec(memory_space=pltpu.SMEM)
HBM = pl.BlockSpec(memory_space=pltpu.HBM)


def pack_kernel(
    panel_ref, sub_ref, block_hbm, weights_hbm, mass_hbm, body_ref,
    block_ref, weights_ref, mass_ref, sems,
):
    copies = [
        pltpu.make_async_copy(block_hbm, block_ref, sems.at[0]),
        pltpu.make_async_copy(weights_hbm.at[0:4], weights_ref, sems.at[1]),
        pltpu.make_async_copy(mass_hbm, mass_ref, sems.at[2]),
    ]
    for copy in copies:
        copy.start()
    for copy in copies:
        copy.wait()
    count, height, width = block_ref.shape
    body_ref[0 : height * count] = pltpu.einshape("brc->rbc", block_ref[...]).reshape(-1, width)
    for d in range(SIDE - 1):
        at = height * (count + d)
        body_ref[at : at + height] = weights_ref[d]
    body_ref[height * (count + SIDE - 1) :] = mass_ref[...]


def pack(panel, sub, start_block, edge_weights, mass):
    count, height, width = start_block.shape
    return pl.pallas_call(
        pack_kernel,
        in_specs=[SMEM, SMEM, HBM, HBM, HBM],
        out_specs=VMEM,
        out_shape=jax.ShapeDtypeStruct((height * (count + SIDE), width), jnp.float32),
        scratch_shapes=[
            pltpu.VMEM((count, height, width), jnp.float32),
            pltpu.VMEM((4, height, width), jnp.float32),
            pltpu.VMEM((height, width), jnp.float32),
            pltpu.SemaphoreType.DMA((3,)),
        ],
        compiler_params=pltpu.CompilerParams(vmem_limit_bytes=8 << 20),
        name="pack",
    )(panel, sub, *[in_hbm(x) for x in (start_block, edge_weights, mass)])


def in_hbm(array):
    return pltpu.with_memory_space_constraint(array, pltpu.HBM)


def in_vmem(array):
    return pltpu.with_memory_space_constraint(array, pltpu.VMEM)


def relayout_kernel(locked_hbm, flat_ref, chunks_ref, sems):
    chunks, size, height, width = chunks_ref.shape
    copies = [
        pltpu.make_async_copy(locked_hbm.at[pl.ds(i * size, size)], chunks_ref.at[i], sems.at[i])
        for i in range(chunks)
    ]
    for copy in copies:
        copy.start()
    for i in range(chunks):
        copies[i].wait()
        rows = pltpu.einshape("krc->rkc", chunks_ref[i])
        for r in range(height):
            flat_ref[pl.ds(i * size, size), r * width : (r + 1) * width] = rows[r]


def relayout(locked):
    basis, height, width = locked.shape
    chunks = max(1, basis // 64)
    return pl.pallas_call(
        relayout_kernel,
        in_specs=[HBM],
        out_specs=VMEM,
        out_shape=pltpu.VMEM((basis, height * width), locked.dtype),
        scratch_shapes=[
            pltpu.VMEM((chunks, basis // chunks, height, width), locked.dtype),
            pltpu.SemaphoreType.DMA((chunks,)),
        ],
        compiler_params=pltpu.CompilerParams(vmem_limit_bytes=12 << 20),
        name="relayout",
    )(in_hbm(locked))


def edge_kernel(sub_ref, body_ref, *refs, height, count, sides):
    sub = sub_ref[0]
    out_refs = refs[-sides:]
    for out_ref, at in zip(out_refs, (1 - sub, sub)):
        start = pl.multiple_of(at * ((height - HALO) * count), 8)
        out_ref[0 : HALO * count] = body_ref[pl.ds(start, HALO * count)]
        for d in range(SIDE):
            start = pl.multiple_of(height * (count + d) + at * (height - 8), 8)
            to = HALO * count + 8 * d
            out_ref[to : to + 8] = body_ref[pl.ds(start, 8)]


def edge_rows(sub, body, ahead, sides, height):
    count = body.shape[0] // height - SIDE
    rows = jax.ShapeDtypeStruct((HALO * count + 8 * SIDE, body.shape[1]), body.dtype)
    return pl.pallas_call(
        lambda *refs: edge_kernel(*refs, height=height, count=count, sides=sides),
        in_specs=[SMEM] + [VMEM] * (1 + len(ahead)),
        out_specs=[VMEM] * sides,
        out_shape=[rows] * sides,
        compiler_params=pltpu.CompilerParams(vmem_limit_bytes=2 << 20),
        name="edge_rows",
    )(sub, body, *ahead)


def filter_kernel(panel_ref, sub_ref, *refs, panels, height, count, width):
    bodies = refs[0:panels]
    nears = refs[panels : 2 * panels]
    fars = refs[2 * panels : 3 * panels]
    locked_ref, keep_ref, send_ref, own_ref, y_even, y_odd, split, sums, squares = refs[3 * panels :]
    total = panels * width
    rows = height + 2 * HALO
    panel = panel_ref[0]
    first_sub = sub_ref[0] == 0

    def fetch(row, own, above, below, size):
        if HALO <= row < HALO + height:
            parts = [b[own : own + size] for b in bodies]
        elif row < HALO:
            at = slice(above, above + size)
            parts = [jnp.where(first_sub, f[at], n[at]) for n, f in zip(nears, fars)]
        else:
            at = slice(below, below + size)
            parts = [jnp.where(first_sub, n[at], f[at]) for n, f in zip(nears, fars)]
        return jnp.concatenate(parts, axis=1)

    def vectors(row):
        return fetch(
            row, (row - HALO) * count, row * count, (row - HALO - height) * count, count
        )

    def side(row, d):
        base = HALO * count + 8 * d
        return fetch(
            row,
            height * (count + d) + row - HALO,
            base + row + 8 - HALO,
            base + row - HALO - height,
            1,
        )

    lane = lax.broadcasted_iota(jnp.int32, (1, total), 1)
    column = lax.rem(lane + panel * width, total)
    not_last = (column != total - 1).astype(jnp.float32)
    not_first = (column != 0).astype(jnp.float32)

    factor = 2.0 / SPREAD

    def left(x):
        return pltpu.roll(x, total - 1, 1)

    def right(x):
        return pltpu.roll(x, 1, 1)

    weights = []
    scale = []
    for row in range(rows):
        y_even[row] = vectors(row)
        mass = side(row, SIDE - 1)
        inside = mass > 0.0
        scale.append(jnp.where(inside, 1.0 / jnp.sqrt(jnp.where(inside, mass, 1.0)), 0.0))
        weights.append([side(row, d) for d in range(SIDE - 1)])
    edges = []
    for row in range(rows - 1):
        s0 = scale[row]
        s1 = scale[row + 1]
        w = weights[row]
        e0 = -factor * (w[0] * (s0 * left(s0))) * not_last
        e1 = -factor * (w[1] * (s0 * s1))
        e2 = -factor * (w[2] * (s0 * left(s1))) * not_last
        e3 = -factor * (w[3] * (s0 * right(s1))) * not_first
        edges.append((e0, e1, e2, e3))
    coefficients = [None]
    for row in range(1, rows - 1):
        w = weights[row]
        v = weights[row - 1]
        total_weight = (
            ((w[0] + w[1]) + (w[2] + w[3]))
            + (right(w[0] * not_last) + v[1])
            + (right(v[2] * not_last) + left(v[3] * not_first))
        )
        diagonal = factor * (scale[row] * scale[row] * total_weight - CENTRE)
        e0, e1, e2, e3 = edges[row]
        u0, u1, u2, u3 = edges[row - 1]
        coefficients.append((diagonal, e1, u1, right(e0), right(e2), u3, e0, left(e3), u2))

    dims = (((1,), (1,)), ((), ()))
    buffers = (y_even, y_odd)
    for wave in range(3, rows + DEGREE):
        for order in range(1, DEGREE + 1):
            row = wave - 2 * order
            if not order <= row < rows - order:
                continue
            source_ref = buffers[(order - 1) % 2]
            target_ref = buffers[order % 2]
            c = coefficients[row]
            ym = source_ref[row - 1]
            y0 = source_ref[row]
            yp = source_ref[row + 1]
            out = c[0] * y0 + (c[1] * yp + c[2] * ym)
            to_left = c[3] * y0 + (c[4] * yp + c[5] * ym)
            to_right = c[6] * y0 + (c[7] * yp + c[8] * ym)
            out = out + (left(to_left) + right(to_right))
            if order == 1:
                out = 0.5 * out
            else:
                out = out - target_ref[row]
            if order < DEGREE:
                target_ref[row] = out
        line = wave - 2 * DEGREE - HALO
        if not 0 <= line < height:
            continue
        own_ref[line] = out[:, 0:width]
        high = out.astype(jnp.bfloat16)
        rest = out - high.astype(jnp.float32)
        middle = rest.astype(jnp.bfloat16)
        low = (rest - middle.astype(jnp.float32)).astype(jnp.bfloat16)
        stacked = jnp.concatenate([high, middle, low], axis=0)
        for t in range(panels):
            at = line * total + lax.rem(panel + t, panels) * width
            split[:, pl.ds(pl.multiple_of(at, width), width)] = stacked[:, t * width : (t + 1) * width]
        if line % CHUNK == CHUNK - 1:
            cut = slice((line + 1 - CHUNK) * total, (line + 1) * total)
            pieces = split[:, cut]
            part = lax.dot_general(
                pieces, locked_ref[:, cut], dims, preferred_element_type=jnp.float32
            )
            square = lax.dot_general(pieces, pieces, dims, preferred_element_type=jnp.float32)
            if line >= CHUNK:
                part = part + sums[...]
                square = square + squares[...]
            sums[...] = part
            squares[...] = square

    gram = squares[...]
    gram = gram[0:count] + gram[count : 2 * count] + gram[2 * count : 3 * count]
    gram = gram[:, 0:count] + gram[:, count : 2 * count] + gram[:, 2 * count : 3 * count]
    products = sums[0:count] + sums[count : 2 * count] + sums[2 * count : 3 * count]
    half = products.shape[1] // 2
    lower = products[:, 0:half]
    upper = products[:, half:]
    keep = jnp.where(first_sub, lower, upper)
    send = jnp.where(first_sub, upper, lower)
    for at in range(0, half, 128):
        to = count * (at // 128)
        keep_ref[to : to + count] = keep[:, at : at + 128]
        send_ref[to : to + count] = send[:, at : at + 128]
    to = count * (half // 128)
    dense = fold(gram, 128)
    keep_ref[to : to + 8] = dense
    send_ref[to : to + 8] = dense


def fold(gram, width):
    count = gram.shape[0]
    parts = [gram[r : r + 8] for r in range(0, count, 8)]
    spare = width - count * len(parts)
    if spare > 0:
        parts.append(jnp.zeros((8, spare), jnp.float32))
    return jnp.concatenate(parts, axis=1)


def filter_call(panel, sub, bodies, nears, fars, locked_flat, height):
    panels = len(bodies)
    width = bodies[0].shape[1]
    count = bodies[0].shape[0] // height - SIDE
    basis = locked_flat.shape[0]
    total = panels * width
    rows = height + 2 * HALO
    payload = jax.ShapeDtypeStruct((count * (basis // 256) + 8, 128), jnp.float32)
    return pl.pallas_call(
        lambda *refs: filter_kernel(*refs, panels=panels, height=height, count=count, width=width),
        in_specs=[SMEM, SMEM] + [VMEM] * (3 * panels + 1),
        out_specs=[VMEM] * 3,
        out_shape=[payload, payload, jax.ShapeDtypeStruct((height, count, width), jnp.float32)],
        scratch_shapes=[
            pltpu.VMEM((rows, count, total), jnp.float32),
            pltpu.VMEM((rows, count, total), jnp.float32),
            pltpu.VMEM((3 * count, height * total), jnp.bfloat16),
            pltpu.VMEM((3 * count, basis), jnp.float32),
            pltpu.VMEM((3 * count, 3 * count), jnp.float32),
        ],
        compiler_params=pltpu.CompilerParams(vmem_limit_bytes=20 << 20),
        name="filter",
    )(panel, sub, *bodies, *nears, *fars, locked_flat)


def factor_kernel(gram_ref, factor_ref, inverse_ref, *, vertices):
    count = factor_ref.shape[0]
    tiles = count // 8
    dense = gram_ref[...]
    row = lax.broadcasted_iota(jnp.int32, (8, 128), 0)
    col = lax.broadcasted_iota(jnp.int32, (8, 128), 1)
    blank = jnp.zeros((8, 128 - count), jnp.float32)

    def fill(x):
        return jnp.broadcast_to(x, (8, 128))

    work = []
    for t in range(tiles):
        gram = jnp.concatenate([dense[:, t * count : (t + 1) * count], blank], axis=1)
        at = row + 8 * t
        gram = gram * (1.0 / vertices) + jnp.where(at == col, 1e-06, 0.0)
        work.append(gram + jnp.where(at + count == col, 1.0, 0.0))
    for b in range(tiles):
        columns = {
            (t, k): fill(work[t][:, 8 * b + k : 8 * b + k + 1])
            for t in range(b, tiles)
            for k in range(8)
        }
        pivots = jnp.ones((8, 128), jnp.float32)
        for j in range(8):
            pivot = fill(columns[b, j][j : j + 1])
            pivots = jnp.where(row == j, pivot, pivots)
            inverse = 1.0 / pivot
            pivot_row = fill(work[b][j : j + 1])
            entries = {k: fill(columns[b, k][j : j + 1]) for k in range(j + 1, 8)}
            for t in range(b, tiles):
                multiplier = columns[t, j] * inverse
                if t == b:
                    multiplier = jnp.where(row > j, multiplier, 0.0)
                for k in range(j + 1, 8):
                    columns[t, k] = columns[t, k] - multiplier * entries[k]
                work[t] = work[t] - multiplier * pivot_row
        work[b] = work[b] * (1.0 / jnp.sqrt(pivots))
    for t in range(tiles):
        upper = jnp.where(row + 8 * t <= col, work[t], 0.0)
        factor_ref[8 * t : 8 * t + 8, :] = upper[:, 0:count]
        inverse_ref[8 * t : 8 * t + 8, :] = work[t][:, count : 2 * count]


def factorize(dense, count, vertices):
    square = jax.ShapeDtypeStruct((count, count), jnp.float32)
    return pl.pallas_call(
        lambda *refs: factor_kernel(*refs, vertices=float(vertices)),
        in_specs=[VMEM],
        out_specs=[VMEM, VMEM],
        out_shape=[square, square],
        compiler_params=pltpu.CompilerParams(vmem_limit_bytes=8 << 20),
        name="factor",
    )(dense)


def finish_kernel(
    sub_ref, inverse_ref, own_ref, mine_ref, other_ref, ortho_hbm, coupling_hbm,
    ortho_ref, coupling_ref, sems, *, vertices,
):
    height, count, width = own_ref.shape
    first_sub = sub_ref[0] == 0
    blocks = other_ref.shape[0] // count
    inverse = inverse_ref[...]

    def times(left, right):
        return jnp.dot(
            left, right, precision=lax.Precision.HIGHEST, preferred_element_type=jnp.float32
        )

    flat = jnp.concatenate([own_ref[r] for r in range(height)], axis=1)
    ortho = times(inverse, flat)
    stacked = jnp.stack([ortho[:, r * width : (r + 1) * width] for r in range(height)], axis=0)
    ortho_ref[...] = pltpu.einshape("rbc->brc", stacked)
    ortho_copy = pltpu.make_async_copy(ortho_ref, ortho_hbm, sems.at[0])
    ortho_copy.start()
    inverse = inverse * (1.0 / math.sqrt(vertices))
    for i in range(blocks):
        mine = mine_ref[i * count : (i + 1) * count]
        other = other_ref[i * count : (i + 1) * count]
        for at, part in (
            (i, jnp.where(first_sub, mine, other)),
            (blocks + i, jnp.where(first_sub, other, mine)),
        ):
            coupling_ref[:, at * 128 : (at + 1) * 128] = times(inverse, part)
    coupling_copy = pltpu.make_async_copy(coupling_ref, coupling_hbm, sems.at[1])
    coupling_copy.start()
    ortho_copy.wait()
    coupling_copy.wait()


def finish(sub, inverse, own, mine, other, vertices):
    height, count, width = own.shape
    ortho = (count, height, width)
    coupling = (count, 256 * (other.shape[0] // count))
    return pl.pallas_call(
        lambda *refs: finish_kernel(*refs, vertices=float(vertices)),
        in_specs=[SMEM, VMEM, VMEM, VMEM, VMEM],
        out_specs=[HBM, HBM],
        out_shape=[jax.ShapeDtypeStruct(s, jnp.float32) for s in (ortho, coupling)],
        scratch_shapes=[
            pltpu.VMEM(ortho, jnp.float32),
            pltpu.VMEM(coupling, jnp.float32),
            pltpu.SemaphoreType.DMA((2,)),
        ],
        compiler_params=pltpu.CompilerParams(vmem_limit_bytes=8 << 20),
        name="finish",
    )(sub, inverse, own, mine, other)


def swap(array, axis, distance):
    size = lax.axis_size(axis)
    return lax.ppermute(array, axis, [(i, i ^ distance) for i in range(size)])


def strip_sum(part):
    strips = lax.axis_size("strip")
    distance = 1
    while distance * 4 < strips or distance * 2 == strips:
        part = part + swap(part, "strip", distance)
        distance *= 2
    if distance * 4 == strips:
        one = swap(part, "strip", distance)
        two = swap(part, "strip", 2 * distance)
        three = swap(part, "strip", 3 * distance)
        part = (part + one) + (two + three)
    return part


def on_device(start_block, edge_weights, mass, locked):
    panels = lax.axis_size("panel")
    lines = lax.axis_size(GRID_ROWS)
    count, height, width = start_block.shape
    vertices = height * width * lines * panels
    panel = lax.axis_index("panel").astype(jnp.int32).reshape(1)
    sub = lax.axis_index("sub").astype(jnp.int32).reshape(1)

    body = pack(panel, sub, start_block, edge_weights, mass)
    bodies = [body]
    for shift in range(1, panels):
        bodies.append(
            lax.ppermute(body, "panel", [((i + shift) % panels, i) for i in range(panels)])
        )
    locked_flat = in_vmem(relayout(locked))
    near, far = edge_rows(sub, body, [], 2, height)

    def far_moves(shift):
        moves = []
        for line in range(1, lines - 1, 2):
            for a, b in ((line, line + 1), (line + 1, line)):
                for p in range(panels):
                    q = (p - shift) % panels
                    moves.append((((a // 2) * panels + p) * 2 + a % 2, ((b // 2) * panels + q) * 2 + b % 2))
        return moves

    fars = [
        lax.ppermute(far, ("strip", "panel", "sub"), far_moves(shift)) for shift in range(panels)
    ]
    nears = [swap(near, "sub", 1)]
    for other in bodies[1:]:
        nears.append(swap(edge_rows(sub, other, [locked_flat], 1, height)[0], "sub", 1))
    keep, send, own = filter_call(panel, sub, bodies, nears, fars, locked_flat, height)
    part = strip_sum(keep + swap(send, "sub", 1))
    grams = part.shape[0] - 8
    other = swap(part[:grams], "sub", 1)
    factor, inverse = factorize(part[grams:, : count * count // 8], count, vertices)
    ortho, coupling = finish(sub, inverse, own, part, other, vertices)
    return (ortho, jnp.transpose(coupling), factor)


def solution(mesh):
    return jax.shard_map(
        on_device,
        mesh=mesh,
        in_specs=(
            P("groups", ("strip", "sub"), "panel"),
            P("groups", ("strip", "sub"), "panel"),
            P(("groups", "strip", "sub"), "panel"),
            P(("groups", "panel"), ("strip", "sub"), None),
        ),
        out_specs=(
            P("groups", ("strip", "sub"), "panel"),
            P(("groups", "panel"), None),
            P("groups", None),
        ),
        check_vma=False,
    )
```

```python
import math

import jax
import jax.numpy as jnp
from jax import lax
from jax.experimental import pallas as pl
from jax.experimental.pallas import tpu as pltpu
from jax.sharding import PartitionSpec as P

DEGREE = 6
CUT_LOW = 2
CUT_HIGH = 32
CENTRE = 0.5 * (CUT_HIGH + CUT_LOW)
SPREAD = 0.5 * (CUT_HIGH - CUT_LOW)
HALO = DEGREE
GRID_ROWS = ("strip", "sub")
SIDE = 5
CHUNK = 2

VMEM = pl.BlockSpec(memory_space=pltpu.VMEM)
SMEM = pl.BlockSpec(memory_space=pltpu.SMEM)
HBM = pl.BlockSpec(memory_space=pltpu.HBM)


def pack_kernel(
    panel_ref, sub_ref, block_hbm, weights_hbm, mass_hbm, body_ref,
    block_ref, weights_ref, mass_ref, sems,
):
    count, height, width = block_ref.shape
    lines = range(0, height, 8)
    block_copies = [
        pltpu.make_async_copy(
            block_hbm.at[:, at : at + 8], block_ref.at[:, at : at + 8], sems.at[2 + at // 8]
        )
        for at in lines
    ]
    side_copies = [
        pltpu.make_async_copy(weights_hbm.at[0:4], weights_ref, sems.at[0]),
        pltpu.make_async_copy(mass_hbm, mass_ref, sems.at[1]),
    ]
    for copy in block_copies + side_copies:
        copy.start()
    for at, copy in zip(lines, block_copies):
        copy.wait()
        rows = pltpu.einshape("brc->rbc", block_ref[:, at : at + 8])
        body_ref[at * count : (at + 8) * count] = rows.reshape(-1, width)
    for copy in side_copies:
        copy.wait()
    for d in range(SIDE - 1):
        at = height * (count + d)
        body_ref[at : at + height] = weights_ref[d]
    body_ref[height * (count + SIDE - 1) :] = mass_ref[...]


def pack(panel, sub, start_block, edge_weights, mass):
    count, height, width = start_block.shape
    return pl.pallas_call(
        pack_kernel,
        in_specs=[SMEM, SMEM, HBM, HBM, HBM],
        out_specs=VMEM,
        out_shape=jax.ShapeDtypeStruct((height * (count + SIDE), width), jnp.float32),
        scratch_shapes=[
            pltpu.VMEM((count, height, width), jnp.float32),
            pltpu.VMEM((4, height, width), jnp.float32),
            pltpu.VMEM((height, width), jnp.float32),
            pltpu.SemaphoreType.DMA((2 + height // 8,)),
        ],
        compiler_params=pltpu.CompilerParams(vmem_limit_bytes=8 << 20),
        name="pack",
    )(panel, sub, *[in_hbm(x) for x in (start_block, edge_weights, mass)])


def in_hbm(array):
    return pltpu.with_memory_space_constraint(array, pltpu.HBM)


def in_vmem(array):
    return pltpu.with_memory_space_constraint(array, pltpu.VMEM)


def relayout_kernel(locked_hbm, flat_ref, chunks_ref, sems):
    chunks, size, height, width = chunks_ref.shape
    copies = [
        pltpu.make_async_copy(locked_hbm.at[pl.ds(i * size, size)], chunks_ref.at[i], sems.at[i])
        for i in range(chunks)
    ]
    for copy in copies:
        copy.start()
    for i in range(chunks):
        copies[i].wait()
        rows = pltpu.einshape("krc->rkc", chunks_ref[i])
        for r in range(height):
            flat_ref[pl.ds(i * size, size), r * width : (r + 1) * width] = rows[r]


def relayout(locked):
    basis, height, width = locked.shape
    chunks = max(1, basis // 64)
    return pl.pallas_call(
        relayout_kernel,
        in_specs=[HBM],
        out_specs=VMEM,
        out_shape=pltpu.VMEM((basis, height * width), locked.dtype),
        scratch_shapes=[
            pltpu.VMEM((chunks, basis // chunks, height, width), locked.dtype),
            pltpu.SemaphoreType.DMA((chunks,)),
        ],
        compiler_params=pltpu.CompilerParams(vmem_limit_bytes=12 << 20),
        name="relayout",
    )(in_hbm(locked))


def edge_kernel(sub_ref, body_ref, *refs, height, count, sides):
    sub = sub_ref[0]
    out_refs = refs[-sides:]
    for out_ref, at in zip(out_refs, (1 - sub, sub)):
        start = pl.multiple_of(at * ((height - HALO) * count), 8)
        out_ref[0 : HALO * count] = body_ref[pl.ds(start, HALO * count)]
        for d in range(SIDE):
            start = pl.multiple_of(height * (count + d) + at * (height - 8), 8)
            to = HALO * count + 8 * d
            out_ref[to : to + 8] = body_ref[pl.ds(start, 8)]


def edge_rows(sub, body, ahead, sides, height):
    count = body.shape[0] // height - SIDE
    rows = jax.ShapeDtypeStruct((HALO * count + 8 * SIDE, body.shape[1]), body.dtype)
    return pl.pallas_call(
        lambda *refs: edge_kernel(*refs, height=height, count=count, sides=sides),
        in_specs=[SMEM] + [VMEM] * (1 + len(ahead)),
        out_specs=[VMEM] * sides,
        out_shape=[rows] * sides,
        compiler_params=pltpu.CompilerParams(vmem_limit_bytes=2 << 20),
        name="edge_rows",
    )(sub, body, *ahead)


def filter_kernel(panel_ref, sub_ref, *refs, panels, height, count, width):
    bodies = refs[0:panels]
    nears = refs[panels : 2 * panels]
    fars = refs[2 * panels : 3 * panels]
    locked_ref, keep_ref, send_ref, own_ref, y_even, y_odd, split, sums, squares = refs[3 * panels :]
    total = panels * width
    rows = height + 2 * HALO
    panel = panel_ref[0]
    first_sub = sub_ref[0] == 0

    def fetch(row, own, above, below, size):
        if HALO <= row < HALO + height:
            parts = [b[own : own + size] for b in bodies]
        elif row < HALO:
            at = slice(above, above + size)
            parts = [jnp.where(first_sub, f[at], n[at]) for n, f in zip(nears, fars)]
        else:
            at = slice(below, below + size)
            parts = [jnp.where(first_sub, n[at], f[at]) for n, f in zip(nears, fars)]
        return jnp.concatenate(parts, axis=1)

    def vectors(row):
        return fetch(
            row, (row - HALO) * count, row * count, (row - HALO - height) * count, count
        )

    def side(row, d):
        base = HALO * count + 8 * d
        return fetch(
            row,
            height * (count + d) + row - HALO,
            base + row + 8 - HALO,
            base + row - HALO - height,
            1,
        )

    lane = lax.broadcasted_iota(jnp.int32, (1, total), 1)
    column = lax.rem(lane + panel * width, total)
    not_last = (column != total - 1).astype(jnp.float32)
    not_first = (column != 0).astype(jnp.float32)

    factor = 2.0 / SPREAD

    def left(x):
        return pltpu.roll(x, total - 1, 1)

    def right(x):
        return pltpu.roll(x, 1, 1)

    weights = []
    scale = []
    for row in range(rows):
        y_even[row] = vectors(row)
        mass = side(row, SIDE - 1)
        inside = mass > 0.0
        scale.append(jnp.where(inside, 1.0 / jnp.sqrt(jnp.where(inside, mass, 1.0)), 0.0))
        weights.append([side(row, d) for d in range(SIDE - 1)])
    edges = []
    for row in range(rows - 1):
        s0 = scale[row]
        s1 = scale[row + 1]
        w = weights[row]
        e0 = -factor * (w[0] * (s0 * left(s0))) * not_last
        e1 = -factor * (w[1] * (s0 * s1))
        e2 = -factor * (w[2] * (s0 * left(s1))) * not_last
        e3 = -factor * (w[3] * (s0 * right(s1))) * not_first
        edges.append((e0, e1, e2, e3))
    coefficients = [None]
    for row in range(1, rows - 1):
        w = weights[row]
        v = weights[row - 1]
        total_weight = (
            ((w[0] + w[1]) + (w[2] + w[3]))
            + (right(w[0] * not_last) + v[1])
            + (right(v[2] * not_last) + left(v[3] * not_first))
        )
        diagonal = factor * (scale[row] * scale[row] * total_weight - CENTRE)
        e0, e1, e2, e3 = edges[row]
        u0, u1, u2, u3 = edges[row - 1]
        coefficients.append((diagonal, e1, u1, right(e0), right(e2), u3, e0, left(e3), u2))

    dims = (((1,), (1,)), ((), ()))
    buffers = (y_even, y_odd)
    for wave in range(3, rows + DEGREE):
        for order in range(1, DEGREE + 1):
            row = wave - 2 * order
            if not order <= row < rows - order:
                continue
            source_ref = buffers[(order - 1) % 2]
            target_ref = buffers[order % 2]
            c = coefficients[row]
            ym = source_ref[row - 1]
            y0 = source_ref[row]
            yp = source_ref[row + 1]
            out = c[0] * y0 + (c[1] * yp + c[2] * ym)
            to_left = c[3] * y0 + (c[4] * yp + c[5] * ym)
            to_right = c[6] * y0 + (c[7] * yp + c[8] * ym)
            out = out + (left(to_left) + right(to_right))
            if order == 1:
                out = 0.5 * out
            else:
                out = out - target_ref[row]
            if order < DEGREE:
                target_ref[row] = out
        line = wave - 2 * DEGREE - HALO
        if not 0 <= line < height:
            continue
        own_ref[line] = out[:, 0:width]
        high = out.astype(jnp.bfloat16)
        rest = out - high.astype(jnp.float32)
        middle = rest.astype(jnp.bfloat16)
        low = (rest - middle.astype(jnp.float32)).astype(jnp.bfloat16)
        stacked = jnp.concatenate([high, middle, low], axis=0)
        for t in range(panels):
            at = line * total + lax.rem(panel + t, panels) * width
            split[:, pl.ds(pl.multiple_of(at, width), width)] = stacked[:, t * width : (t + 1) * width]
        if line % CHUNK == CHUNK - 1:
            cut = slice((line + 1 - CHUNK) * total, (line + 1) * total)
            pieces = split[:, cut]
            part = lax.dot_general(
                pieces, locked_ref[:, cut], dims, preferred_element_type=jnp.float32
            )
            square = lax.dot_general(pieces, pieces, dims, preferred_element_type=jnp.float32)
            if line >= CHUNK:
                part = part + sums[...]
                square = square + squares[...]
            sums[...] = part
            squares[...] = square

    gram = squares[...]
    gram = gram[0:count] + gram[count : 2 * count] + gram[2 * count : 3 * count]
    gram = gram[:, 0:count] + gram[:, count : 2 * count] + gram[:, 2 * count : 3 * count]
    products = sums[0:count] + sums[count : 2 * count] + sums[2 * count : 3 * count]
    half = products.shape[1] // 2
    lower = products[:, 0:half]
    upper = products[:, half:]
    keep = jnp.where(first_sub, lower, upper)
    send = jnp.where(first_sub, upper, lower)
    for at in range(0, half, 128):
        to = count * (at // 128)
        keep_ref[to : to + count] = keep[:, at : at + 128]
        send_ref[to : to + count] = send[:, at : at + 128]
    to = count * (half // 128)
    dense = fold(gram, 128)
    keep_ref[to : to + 8] = dense
    send_ref[to : to + 8] = dense


def fold(gram, width):
    count = gram.shape[0]
    parts = [gram[r : r + 8] for r in range(0, count, 8)]
    spare = width - count * len(parts)
    if spare > 0:
        parts.append(jnp.zeros((8, spare), jnp.float32))
    return jnp.concatenate(parts, axis=1)


def filter_call(panel, sub, bodies, nears, fars, locked_flat, height):
    panels = len(bodies)
    width = bodies[0].shape[1]
    count = bodies[0].shape[0] // height - SIDE
    basis = locked_flat.shape[0]
    total = panels * width
    rows = height + 2 * HALO
    payload = jax.ShapeDtypeStruct((count * (basis // 256) + 8, 128), jnp.float32)
    return pl.pallas_call(
        lambda *refs: filter_kernel(*refs, panels=panels, height=height, count=count, width=width),
        in_specs=[SMEM, SMEM] + [VMEM] * (3 * panels + 1),
        out_specs=[VMEM] * 3,
        out_shape=[payload, payload, jax.ShapeDtypeStruct((height, count, width), jnp.float32)],
        scratch_shapes=[
            pltpu.VMEM((rows, count, total), jnp.float32),
            pltpu.VMEM((rows, count, total), jnp.float32),
            pltpu.VMEM((3 * count, height * total), jnp.bfloat16),
            pltpu.VMEM((3 * count, basis), jnp.float32),
            pltpu.VMEM((3 * count, 3 * count), jnp.float32),
        ],
        compiler_params=pltpu.CompilerParams(vmem_limit_bytes=20 << 20),
        name="filter",
    )(panel, sub, *bodies, *nears, *fars, locked_flat)


def factor_kernel(gram_ref, factor_ref, inverse_ref, *, vertices):
    count = factor_ref.shape[0]
    tiles = count // 8
    dense = gram_ref[...]
    row = lax.broadcasted_iota(jnp.int32, (8, 128), 0)
    col = lax.broadcasted_iota(jnp.int32, (8, 128), 1)
    blank = jnp.zeros((8, 128 - count), jnp.float32)

    def fill(x):
        return jnp.broadcast_to(x, (8, 128))

    work = []
    for t in range(tiles):
        gram = jnp.concatenate([dense[:, t * count : (t + 1) * count], blank], axis=1)
        at = row + 8 * t
        gram = gram * (1.0 / vertices) + jnp.where(at == col, 1e-06, 0.0)
        work.append(gram + jnp.where(at + count == col, 1.0, 0.0))
    for b in range(tiles):
        columns = {
            (t, k): fill(work[t][:, 8 * b + k : 8 * b + k + 1])
            for t in range(b, tiles)
            for k in range(8)
        }
        pivots = jnp.ones((8, 128), jnp.float32)
        for j in range(0, 8, 2):
            first, second = columns[b, j], columns[b, j + 1]
            pivot = fill(first[j : j + 1])
            off = fill(first[j + 1 : j + 2])
            det = pivot * fill(second[j + 1 : j + 2]) - off * off
            inverse = 1.0 / pivot
            inverse_det = 1.0 / det
            pivots = jnp.where(row == j, pivot, jnp.where(row == j + 1, det * inverse, pivots))
            ratio = off * inverse
            top = fill(work[b][j : j + 1])
            low = fill(work[b][j + 1 : j + 2]) - ratio * top
            tops = {k: fill(columns[b, k][j : j + 1]) for k in range(j + 2, 8)}
            lows = {
                k: fill(columns[b, k][j + 1 : j + 2]) - ratio * tops[k] for k in range(j + 2, 8)
            }
            for t in range(b, tiles):
                one = columns[t, j] * inverse
                two = (columns[t, j + 1] * pivot - columns[t, j] * off) * inverse_det
                if t == b:
                    one = jnp.where(row > j, one, 0.0)
                    two = jnp.where(row > j + 1, two, 0.0)
                for k in range(j + 2, 8):
                    columns[t, k] = columns[t, k] - (one * tops[k] + two * lows[k])
                work[t] = work[t] - (one * top + two * low)
        work[b] = work[b] * (1.0 / jnp.sqrt(pivots))
    for t in range(tiles):
        upper = jnp.where(row + 8 * t <= col, work[t], 0.0)
        factor_ref[8 * t : 8 * t + 8, :] = upper[:, 0:count]
        inverse_ref[8 * t : 8 * t + 8, :] = work[t][:, count : 2 * count]


def factorize(dense, count, vertices):
    square = jax.ShapeDtypeStruct((count, count), jnp.float32)
    return pl.pallas_call(
        lambda *refs: factor_kernel(*refs, vertices=float(vertices)),
        in_specs=[VMEM],
        out_specs=[VMEM, VMEM],
        out_shape=[square, square],
        compiler_params=pltpu.CompilerParams(vmem_limit_bytes=8 << 20),
        name="factor",
    )(dense)


def finish_kernel(
    sub_ref, inverse_ref, own_ref, mine_ref, other_ref, ortho_hbm, coupling_hbm,
    ortho_ref, coupling_ref, sems, *, vertices,
):
    height, count, width = own_ref.shape
    first_sub = sub_ref[0] == 0
    blocks = other_ref.shape[0] // count
    inverse = inverse_ref[...]

    def times(left, right):
        return jnp.dot(
            left, right, precision=lax.Precision.HIGHEST, preferred_element_type=jnp.float32
        )

    flat = jnp.concatenate([own_ref[r] for r in range(height)], axis=1)
    ortho = times(inverse, flat)
    stacked = jnp.stack([ortho[:, r * width : (r + 1) * width] for r in range(height)], axis=0)
    ortho_ref[...] = pltpu.einshape("rbc->brc", stacked)
    ortho_copy = pltpu.make_async_copy(ortho_ref, ortho_hbm, sems.at[0])
    ortho_copy.start()
    inverse = inverse * (1.0 / math.sqrt(vertices))
    for i in range(blocks):
        mine = mine_ref[i * count : (i + 1) * count]
        other = other_ref[i * count : (i + 1) * count]
        for at, part in (
            (i, jnp.where(first_sub, mine, other)),
            (blocks + i, jnp.where(first_sub, other, mine)),
        ):
            coupling_ref[:, at * 128 : (at + 1) * 128] = times(inverse, part)
    coupling_copy = pltpu.make_async_copy(coupling_ref, coupling_hbm, sems.at[1])
    coupling_copy.start()
    ortho_copy.wait()
    coupling_copy.wait()


def finish(sub, inverse, own, mine, other, vertices):
    height, count, width = own.shape
    ortho = (count, height, width)
    coupling = (count, 256 * (other.shape[0] // count))
    return pl.pallas_call(
        lambda *refs: finish_kernel(*refs, vertices=float(vertices)),
        in_specs=[SMEM, VMEM, VMEM, VMEM, VMEM],
        out_specs=[HBM, HBM],
        out_shape=[jax.ShapeDtypeStruct(s, jnp.float32) for s in (ortho, coupling)],
        scratch_shapes=[
            pltpu.VMEM(ortho, jnp.float32),
            pltpu.VMEM(coupling, jnp.float32),
            pltpu.SemaphoreType.DMA((2,)),
        ],
        compiler_params=pltpu.CompilerParams(vmem_limit_bytes=8 << 20),
        name="finish",
    )(sub, inverse, own, mine, other)


def swap(array, axis, distance):
    size = lax.axis_size(axis)
    return lax.ppermute(array, axis, [(i, i ^ distance) for i in range(size)])


def strip_sum(part):
    strips = lax.axis_size("strip")
    distance = 1
    while distance * 4 < strips or distance * 2 == strips:
        part = part + swap(part, "strip", distance)
        distance *= 2
    if distance * 4 == strips:
        one = swap(part, "strip", distance)
        two = swap(part, "strip", 2 * distance)
        three = swap(part, "strip", 3 * distance)
        part = (part + one) + (two + three)
    return part


def on_device(start_block, edge_weights, mass, locked):
    panels = lax.axis_size("panel")
    lines = lax.axis_size(GRID_ROWS)
    count, height, width = start_block.shape
    vertices = height * width * lines * panels
    panel = lax.axis_index("panel").astype(jnp.int32).reshape(1)
    sub = lax.axis_index("sub").astype(jnp.int32).reshape(1)

    body = pack(panel, sub, start_block, edge_weights, mass)
    bodies = [body]
    for shift in range(1, panels):
        bodies.append(
            lax.ppermute(body, "panel", [((i + shift) % panels, i) for i in range(panels)])
        )
    locked_flat = in_vmem(relayout(locked))
    near, far = edge_rows(sub, body, [], 2, height)

    def far_moves(shift):
        moves = []
        for line in range(1, lines - 1, 2):
            for a, b in ((line, line + 1), (line + 1, line)):
                for p in range(panels):
                    q = (p - shift) % panels
                    moves.append((((a // 2) * panels + p) * 2 + a % 2, ((b // 2) * panels + q) * 2 + b % 2))
        return moves

    fars = [
        lax.ppermute(far, ("strip", "panel", "sub"), far_moves(shift)) for shift in range(panels)
    ]
    nears = [swap(near, "sub", 1)]
    for other in bodies[1:]:
        nears.append(swap(edge_rows(sub, other, [locked_flat], 1, height)[0], "sub", 1))
    keep, send, own = filter_call(panel, sub, bodies, nears, fars, locked_flat, height)
    part = strip_sum(keep + swap(send, "sub", 1))
    grams = part.shape[0] - 8
    other = swap(part[:grams], "sub", 1)
    factor, inverse = factorize(part[grams:, : count * count // 8], count, vertices)
    ortho, coupling = finish(sub, inverse, own, part, other, vertices)
    return (ortho, jnp.transpose(coupling), factor)


def solution(mesh):
    return jax.shard_map(
        on_device,
        mesh=mesh,
        in_specs=(
            P("groups", ("strip", "sub"), "panel"),
            P("groups", ("strip", "sub"), "panel"),
            P(("groups", "strip", "sub"), "panel"),
            P(("groups", "panel"), ("strip", "sub"), None),
        ),
        out_specs=(
            P("groups", ("strip", "sub"), "panel"),
            P(("groups", "panel"), None),
            P("groups", None),
        ),
        check_vma=False,
    )
```

```python
import math

import jax
import jax.numpy as jnp
from jax import lax
from jax.experimental import pallas as pl
from jax.experimental.pallas import tpu as pltpu
from jax.sharding import PartitionSpec as P

DEGREE = 6
CUT_LOW = 2
CUT_HIGH = 32
CENTRE = 0.5 * (CUT_HIGH + CUT_LOW)
SPREAD = 0.5 * (CUT_HIGH - CUT_LOW)
HALO = DEGREE
GRID_ROWS = ("strip", "sub")
SIDE = 5
CHUNK = 1

VMEM = pl.BlockSpec(memory_space=pltpu.VMEM)
SMEM = pl.BlockSpec(memory_space=pltpu.SMEM)
HBM = pl.BlockSpec(memory_space=pltpu.HBM)


def pack_kernel(
    panel_ref, sub_ref, block_hbm, weights_hbm, mass_hbm, body_ref,
    block_ref, weights_ref, mass_ref, sems,
):
    count, height, width = block_ref.shape
    lines = range(0, height, 8)
    block_copies = [
        pltpu.make_async_copy(
            block_hbm.at[:, at : at + 8], block_ref.at[:, at : at + 8], sems.at[2 + at // 8]
        )
        for at in lines
    ]
    side_copies = [
        pltpu.make_async_copy(weights_hbm.at[0:4], weights_ref, sems.at[0]),
        pltpu.make_async_copy(mass_hbm, mass_ref, sems.at[1]),
    ]
    for copy in block_copies + side_copies:
        copy.start()
    for at, copy in zip(lines, block_copies):
        copy.wait()
        rows = pltpu.einshape("brc->rbc", block_ref[:, at : at + 8])
        body_ref[at * count : (at + 8) * count] = rows.reshape(-1, width)
    for copy in side_copies:
        copy.wait()
    for d in range(SIDE - 1):
        at = height * (count + d)
        body_ref[at : at + height] = weights_ref[d]
    body_ref[height * (count + SIDE - 1) :] = mass_ref[...]


def pack(panel, sub, start_block, edge_weights, mass):
    count, height, width = start_block.shape
    return pl.pallas_call(
        pack_kernel,
        in_specs=[SMEM, SMEM, HBM, HBM, HBM],
        out_specs=VMEM,
        out_shape=jax.ShapeDtypeStruct((height * (count + SIDE), width), jnp.float32),
        scratch_shapes=[
            pltpu.VMEM((count, height, width), jnp.float32),
            pltpu.VMEM((4, height, width), jnp.float32),
            pltpu.VMEM((height, width), jnp.float32),
            pltpu.SemaphoreType.DMA((2 + height // 8,)),
        ],
        compiler_params=pltpu.CompilerParams(vmem_limit_bytes=8 << 20),
        name="pack",
    )(panel, sub, *[in_hbm(x) for x in (start_block, edge_weights, mass)])


def in_hbm(array):
    return pltpu.with_memory_space_constraint(array, pltpu.HBM)


def in_vmem(array):
    return pltpu.with_memory_space_constraint(array, pltpu.VMEM)


def relayout_kernel(locked_hbm, flat_ref, chunks_ref, sems):
    chunks, size, height, width = chunks_ref.shape
    copies = [
        pltpu.make_async_copy(locked_hbm.at[pl.ds(i * size, size)], chunks_ref.at[i], sems.at[i])
        for i in range(chunks)
    ]
    for copy in copies:
        copy.start()
    for i in range(chunks):
        copies[i].wait()
        rows = pltpu.einshape("krc->rkc", chunks_ref[i])
        for r in range(height):
            flat_ref[pl.ds(i * size, size), r * width : (r + 1) * width] = rows[r]


def relayout(locked):
    basis, height, width = locked.shape
    chunks = max(1, basis // 64)
    return pl.pallas_call(
        relayout_kernel,
        in_specs=[HBM],
        out_specs=VMEM,
        out_shape=pltpu.VMEM((basis, height * width), locked.dtype),
        scratch_shapes=[
            pltpu.VMEM((chunks, basis // chunks, height, width), locked.dtype),
            pltpu.SemaphoreType.DMA((chunks,)),
        ],
        compiler_params=pltpu.CompilerParams(vmem_limit_bytes=12 << 20),
        name="relayout",
    )(in_hbm(locked))


def edge_kernel(sub_ref, body_ref, *refs, height, count, sides):
    sub = sub_ref[0]
    out_refs = refs[-sides:]
    for out_ref, at in zip(out_refs, (1 - sub, sub)):
        start = pl.multiple_of(at * ((height - HALO) * count), 8)
        out_ref[0 : HALO * count] = body_ref[pl.ds(start, HALO * count)]
        for d in range(SIDE):
            start = pl.multiple_of(height * (count + d) + at * (height - 8), 8)
            to = HALO * count + 8 * d
            out_ref[to : to + 8] = body_ref[pl.ds(start, 8)]


def edge_rows(sub, body, ahead, sides, height):
    count = body.shape[0] // height - SIDE
    rows = jax.ShapeDtypeStruct((HALO * count + 8 * SIDE, body.shape[1]), body.dtype)
    return pl.pallas_call(
        lambda *refs: edge_kernel(*refs, height=height, count=count, sides=sides),
        in_specs=[SMEM] + [VMEM] * (1 + len(ahead)),
        out_specs=[VMEM] * sides,
        out_shape=[rows] * sides,
        compiler_params=pltpu.CompilerParams(vmem_limit_bytes=2 << 20),
        name="edge_rows",
    )(sub, body, *ahead)


def filter_kernel(panel_ref, sub_ref, *refs, panels, height, count, width):
    bodies = refs[0:panels]
    nears = refs[panels : 2 * panels]
    fars = refs[2 * panels : 3 * panels]
    locked_ref, keep_ref, send_ref, own_ref, y_even, y_odd, split, sums, squares = refs[3 * panels :]
    total = panels * width
    rows = height + 2 * HALO
    panel = panel_ref[0]
    first_sub = sub_ref[0] == 0

    def fetch(row, own, above, below, size):
        if HALO <= row < HALO + height:
            parts = [b[own : own + size] for b in bodies]
        elif row < HALO:
            at = slice(above, above + size)
            parts = [jnp.where(first_sub, f[at], n[at]) for n, f in zip(nears, fars)]
        else:
            at = slice(below, below + size)
            parts = [jnp.where(first_sub, n[at], f[at]) for n, f in zip(nears, fars)]
        return jnp.concatenate(parts, axis=1)

    def vectors(row):
        return fetch(
            row, (row - HALO) * count, row * count, (row - HALO - height) * count, count
        )

    def side(row, d):
        base = HALO * count + 8 * d
        return fetch(
            row,
            height * (count + d) + row - HALO,
            base + row + 8 - HALO,
            base + row - HALO - height,
            1,
        )

    lane = lax.broadcasted_iota(jnp.int32, (1, total), 1)
    column = lax.rem(lane + panel * width, total)
    not_last = (column != total - 1).astype(jnp.float32)
    not_first = (column != 0).astype(jnp.float32)

    factor = 2.0 / SPREAD

    def left(x):
        return pltpu.roll(x, total - 1, 1)

    def right(x):
        return pltpu.roll(x, 1, 1)

    weights = []
    scale = []
    for row in range(rows):
        y_even[row] = vectors(row)
        mass = side(row, SIDE - 1)
        inside = mass > 0.0
        scale.append(jnp.where(inside, 1.0 / jnp.sqrt(jnp.where(inside, mass, 1.0)), 0.0))
        weights.append([side(row, d) for d in range(SIDE - 1)])
    edges = []
    for row in range(rows - 1):
        s0 = scale[row]
        s1 = scale[row + 1]
        w = weights[row]
        e0 = -factor * (w[0] * (s0 * left(s0))) * not_last
        e1 = -factor * (w[1] * (s0 * s1))
        e2 = -factor * (w[2] * (s0 * left(s1))) * not_last
        e3 = -factor * (w[3] * (s0 * right(s1))) * not_first
        edges.append((e0, e1, e2, e3))
    coefficients = [None]
    for row in range(1, rows - 1):
        w = weights[row]
        v = weights[row - 1]
        total_weight = (
            ((w[0] + w[1]) + (w[2] + w[3]))
            + (right(w[0] * not_last) + v[1])
            + (right(v[2] * not_last) + left(v[3] * not_first))
        )
        diagonal = factor * (scale[row] * scale[row] * total_weight - CENTRE)
        e0, e1, e2, e3 = edges[row]
        u0, u1, u2, u3 = edges[row - 1]
        coefficients.append((diagonal, e1, u1, right(e0), right(e2), u3, e0, left(e3), u2))

    dims = (((1,), (1,)), ((), ()))
    buffers = (y_even, y_odd)
    for wave in range(3, rows + DEGREE):
        for order in range(1, DEGREE + 1):
            row = wave - 2 * order
            if not order <= row < rows - order:
                continue
            source_ref = buffers[(order - 1) % 2]
            target_ref = buffers[order % 2]
            c = coefficients[row]
            ym = source_ref[row - 1]
            y0 = source_ref[row]
            yp = source_ref[row + 1]
            out = c[0] * y0 + (c[1] * yp + c[2] * ym)
            to_left = c[3] * y0 + (c[4] * yp + c[5] * ym)
            to_right = c[6] * y0 + (c[7] * yp + c[8] * ym)
            out = out + (left(to_left) + right(to_right))
            if order == 1:
                out = 0.5 * out
            else:
                out = out - target_ref[row]
            if order < DEGREE:
                target_ref[row] = out
        line = wave - 2 * DEGREE - HALO
        if not 0 <= line < height:
            continue
        own_ref[line] = out[:, 0:width]
        high = out.astype(jnp.bfloat16)
        rest = out - high.astype(jnp.float32)
        middle = rest.astype(jnp.bfloat16)
        low = (rest - middle.astype(jnp.float32)).astype(jnp.bfloat16)
        stacked = jnp.concatenate([high, middle, low], axis=0)
        for t in range(panels):
            at = line * total + lax.rem(panel + t, panels) * width
            split[:, pl.ds(pl.multiple_of(at, width), width)] = stacked[:, t * width : (t + 1) * width]
        if line % CHUNK == CHUNK - 1:
            cut = slice((line + 1 - CHUNK) * total, (line + 1) * total)
            pieces = split[:, cut]
            part = lax.dot_general(
                pieces, locked_ref[:, cut], dims, preferred_element_type=jnp.float32
            )
            square = lax.dot_general(pieces, pieces, dims, preferred_element_type=jnp.float32)
            if line >= CHUNK:
                part = part + sums[...]
                square = square + squares[...]
            sums[...] = part
            squares[...] = square

    gram = squares[...]
    gram = gram[0:count] + gram[count : 2 * count] + gram[2 * count : 3 * count]
    gram = gram[:, 0:count] + gram[:, count : 2 * count] + gram[:, 2 * count : 3 * count]
    products = sums[0:count] + sums[count : 2 * count] + sums[2 * count : 3 * count]
    half = products.shape[1] // 2
    lower = products[:, 0:half]
    upper = products[:, half:]
    keep = jnp.where(first_sub, lower, upper)
    send = jnp.where(first_sub, upper, lower)
    for at in range(0, half, 128):
        to = count * (at // 128)
        keep_ref[to : to + count] = keep[:, at : at + 128]
        send_ref[to : to + count] = send[:, at : at + 128]
    to = count * (half // 128)
    dense = fold(gram, 128)
    keep_ref[to : to + 8] = dense
    send_ref[to : to + 8] = dense


def fold(gram, width):
    count = gram.shape[0]
    parts = [gram[r : r + 8] for r in range(0, count, 8)]
    spare = width - count * len(parts)
    if spare > 0:
        parts.append(jnp.zeros((8, spare), jnp.float32))
    return jnp.concatenate(parts, axis=1)


def filter_call(panel, sub, bodies, nears, fars, locked_flat, height):
    panels = len(bodies)
    width = bodies[0].shape[1]
    count = bodies[0].shape[0] // height - SIDE
    basis = locked_flat.shape[0]
    total = panels * width
    rows = height + 2 * HALO
    payload = jax.ShapeDtypeStruct((count * (basis // 256) + 8, 128), jnp.float32)
    return pl.pallas_call(
        lambda *refs: filter_kernel(*refs, panels=panels, height=height, count=count, width=width),
        in_specs=[SMEM, SMEM] + [VMEM] * (3 * panels + 1),
        out_specs=[VMEM] * 3,
        out_shape=[payload, payload, jax.ShapeDtypeStruct((height, count, width), jnp.float32)],
        scratch_shapes=[
            pltpu.VMEM((rows, count, total), jnp.float32),
            pltpu.VMEM((rows, count, total), jnp.float32),
            pltpu.VMEM((3 * count, height * total), jnp.bfloat16),
            pltpu.VMEM((3 * count, basis), jnp.float32),
            pltpu.VMEM((3 * count, 3 * count), jnp.float32),
        ],
        compiler_params=pltpu.CompilerParams(vmem_limit_bytes=20 << 20),
        name="filter",
    )(panel, sub, *bodies, *nears, *fars, locked_flat)


def factor_kernel(gram_ref, factor_ref, inverse_ref, *, vertices):
    count = factor_ref.shape[0]
    tiles = count // 8
    dense = gram_ref[...]
    row = lax.broadcasted_iota(jnp.int32, (8, 128), 0)
    col = lax.broadcasted_iota(jnp.int32, (8, 128), 1)
    blank = jnp.zeros((8, 128 - count), jnp.float32)

    def fill(x):
        return jnp.broadcast_to(x, (8, 128))

    work = []
    for t in range(tiles):
        gram = jnp.concatenate([dense[:, t * count : (t + 1) * count], blank], axis=1)
        at = row + 8 * t
        gram = gram * (1.0 / vertices) + jnp.where(at == col, 1e-06, 0.0)
        work.append(gram + jnp.where(at + count == col, 1.0, 0.0))
    for b in range(tiles):
        columns = {
            (t, k): fill(work[t][:, 8 * b + k : 8 * b + k + 1])
            for t in range(b, tiles)
            for k in range(8)
        }
        pivots = jnp.ones((8, 128), jnp.float32)
        for j in range(0, 8, 2):
            first, second = columns[b, j], columns[b, j + 1]
            pivot = fill(first[j : j + 1])
            off = fill(first[j + 1 : j + 2])
            det = pivot * fill(second[j + 1 : j + 2]) - off * off
            inverse = 1.0 / pivot
            inverse_det = 1.0 / det
            pivots = jnp.where(row == j, pivot, jnp.where(row == j + 1, det * inverse, pivots))
            ratio = off * inverse
            top = fill(work[b][j : j + 1])
            low = fill(work[b][j + 1 : j + 2]) - ratio * top
            tops = {k: fill(columns[b, k][j : j + 1]) for k in range(j + 2, 8)}
            lows = {
                k: fill(columns[b, k][j + 1 : j + 2]) - ratio * tops[k] for k in range(j + 2, 8)
            }
            for t in range(b, tiles):
                one = columns[t, j] * inverse
                two = (columns[t, j + 1] * pivot - columns[t, j] * off) * inverse_det
                if t == b:
                    one = jnp.where(row > j, one, 0.0)
                    two = jnp.where(row > j + 1, two, 0.0)
                for k in range(j + 2, 8):
                    columns[t, k] = columns[t, k] - (one * tops[k] + two * lows[k])
                work[t] = work[t] - (one * top + two * low)
        work[b] = work[b] * (1.0 / jnp.sqrt(pivots))
    for t in range(tiles):
        upper = jnp.where(row + 8 * t <= col, work[t], 0.0)
        factor_ref[8 * t : 8 * t + 8, :] = upper[:, 0:count]
        inverse_ref[8 * t : 8 * t + 8, :] = work[t][:, count : 2 * count]


def factorize(dense, count, vertices):
    square = jax.ShapeDtypeStruct((count, count), jnp.float32)
    return pl.pallas_call(
        lambda *refs: factor_kernel(*refs, vertices=float(vertices)),
        in_specs=[VMEM],
        out_specs=[VMEM, VMEM],
        out_shape=[square, square],
        compiler_params=pltpu.CompilerParams(vmem_limit_bytes=8 << 20),
        name="factor",
    )(dense)


def finish_kernel(
    sub_ref, inverse_ref, own_ref, mine_ref, other_ref, ortho_hbm, coupling_hbm,
    ortho_ref, coupling_ref, sems, *, vertices,
):
    height, count, width = own_ref.shape
    first_sub = sub_ref[0] == 0
    blocks = other_ref.shape[0] // count
    inverse = inverse_ref[...]

    def times(left, right):
        return jnp.dot(
            left, right, precision=lax.Precision.HIGHEST, preferred_element_type=jnp.float32
        )

    flat = jnp.concatenate([own_ref[r] for r in range(height)], axis=1)
    ortho = times(inverse, flat)
    stacked = jnp.stack([ortho[:, r * width : (r + 1) * width] for r in range(height)], axis=0)
    ortho_ref[...] = pltpu.einshape("rbc->brc", stacked)
    ortho_copy = pltpu.make_async_copy(ortho_ref, ortho_hbm, sems.at[0])
    ortho_copy.start()
    inverse = inverse * (1.0 / math.sqrt(vertices))
    for i in range(blocks):
        mine = mine_ref[i * count : (i + 1) * count]
        other = other_ref[i * count : (i + 1) * count]
        for at, part in (
            (i, jnp.where(first_sub, mine, other)),
            (blocks + i, jnp.where(first_sub, other, mine)),
        ):
            coupling_ref[:, at * 128 : (at + 1) * 128] = times(inverse, part)
    coupling_copy = pltpu.make_async_copy(coupling_ref, coupling_hbm, sems.at[1])
    coupling_copy.start()
    ortho_copy.wait()
    coupling_copy.wait()


def finish(sub, inverse, own, mine, other, vertices):
    height, count, width = own.shape
    ortho = (count, height, width)
    coupling = (count, 256 * (other.shape[0] // count))
    return pl.pallas_call(
        lambda *refs: finish_kernel(*refs, vertices=float(vertices)),
        in_specs=[SMEM, VMEM, VMEM, VMEM, VMEM],
        out_specs=[HBM, HBM],
        out_shape=[jax.ShapeDtypeStruct(s, jnp.float32) for s in (ortho, coupling)],
        scratch_shapes=[
            pltpu.VMEM(ortho, jnp.float32),
            pltpu.VMEM(coupling, jnp.float32),
            pltpu.SemaphoreType.DMA((2,)),
        ],
        compiler_params=pltpu.CompilerParams(vmem_limit_bytes=8 << 20),
        name="finish",
    )(sub, inverse, own, mine, other)


def swap(array, axis, distance):
    size = lax.axis_size(axis)
    return lax.ppermute(array, axis, [(i, i ^ distance) for i in range(size)])


def strip_sum(part):
    strips = lax.axis_size("strip")
    distance = 1
    while distance * 4 < strips or distance * 2 == strips:
        part = part + swap(part, "strip", distance)
        distance *= 2
    if distance * 4 == strips:
        one = swap(part, "strip", distance)
        two = swap(part, "strip", 2 * distance)
        three = swap(part, "strip", 3 * distance)
        part = (part + one) + (two + three)
    return part


def on_device(start_block, edge_weights, mass, locked):
    panels = lax.axis_size("panel")
    lines = lax.axis_size(GRID_ROWS)
    count, height, width = start_block.shape
    vertices = height * width * lines * panels
    panel = lax.axis_index("panel").astype(jnp.int32).reshape(1)
    sub = lax.axis_index("sub").astype(jnp.int32).reshape(1)

    body = pack(panel, sub, start_block, edge_weights, mass)
    bodies = [body]
    for shift in range(1, panels):
        bodies.append(
            lax.ppermute(body, "panel", [((i + shift) % panels, i) for i in range(panels)])
        )
    locked_flat = in_vmem(relayout(locked))
    near, far = edge_rows(sub, body, [], 2, height)

    def far_moves(shift):
        moves = []
        for line in range(1, lines - 1, 2):
            for a, b in ((line, line + 1), (line + 1, line)):
                for p in range(panels):
                    q = (p - shift) % panels
                    moves.append((((a // 2) * panels + p) * 2 + a % 2, ((b // 2) * panels + q) * 2 + b % 2))
        return moves

    fars = [
        lax.ppermute(far, ("strip", "panel", "sub"), far_moves(shift)) for shift in range(panels)
    ]
    nears = [swap(near, "sub", 1)]
    for other in bodies[1:]:
        nears.append(swap(edge_rows(sub, other, [locked_flat], 1, height)[0], "sub", 1))
    keep, send, own = filter_call(panel, sub, bodies, nears, fars, locked_flat, height)
    part = strip_sum(keep + swap(send, "sub", 1))
    grams = part.shape[0] - 8
    other = swap(part[:grams], "sub", 1)
    factor, inverse = factorize(part[grams:, : count * count // 8], count, vertices)
    ortho, coupling = finish(sub, inverse, own, part, other, vertices)
    return (ortho, jnp.transpose(coupling), factor)


def solution(mesh):
    return jax.shard_map(
        on_device,
        mesh=mesh,
        in_specs=(
            P("groups", ("strip", "sub"), "panel"),
            P("groups", ("strip", "sub"), "panel"),
            P(("groups", "strip", "sub"), "panel"),
            P(("groups", "panel"), ("strip", "sub"), None),
        ),
        out_specs=(
            P("groups", ("strip", "sub"), "panel"),
            P(("groups", "panel"), None),
            P("groups", None),
        ),
        check_vma=False,
    )
```
